512 devices in a mesh: ctx: 64 (over y, z), tp: 8 (over x, core).
Axes of the slice: x: 4, y: 4, z: 16, core: 2. Of those that a mesh axis runs over, the one named last changes fastest.
Arguments:
- inputs: bfloat16 [8192, 2048], P('ctx', 'tp'), may hold values from -6.5 to 6.5
- query_weight: bfloat16 [2048, 1024], P(None, 'tp'), may hold values from -0.125 to 0.125
- key_weight: bfloat16 [2048, 1024], P(None, 'tp'), may hold values from -0.125 to 0.125
- value_weight: bfloat16 [2048, 2048], P(None, 'tp'), may hold values from -0.125 to 0.125
- beta_weight: bfloat16 [2048, 16], P(None, 'tp'), may hold values from -1.5 to 1.5
- alpha_weight: bfloat16 [2048, 16], P(None, 'tp'), may hold values from -0.125 to 0.125
- query_filter: bfloat16 [4, 1024], P(None, 'tp'), may hold values from -3 to 3
- key_filter: bfloat16 [4, 1024], P(None, 'tp'), may hold values from -3 to 3
- value_filter: bfloat16 [4, 2048], P(None, 'tp'), may hold values from -3 to 3
- decay_log: float32 [16], P('tp'), may hold values from 0 to 2.77
- step_bias: float32 [16], P('tp'), may hold values from -16 to -2.3
- grad_core: bfloat16 [8192, 2048], P('ctx', 'tp'), may hold values from -6 to 6
Outputs:
- grad_inputs: bfloat16 [8192, 2048], P('ctx', 'tp')
The draws below stay inside these ranges and needn't reach their ends.
All inputs are finite; a program needn't handle non-finite values.
Results may differ from the reference program's by a relative error of at most 0.019.
Values may be sent and summed in bfloat16 or wider, within the bound.
No kernel may reach another device: no remote copies, remote signals or barrier semaphores. Data moves between devices by JAX's collectives and lax.ppermute only.
A program may use at most 128 MiB of HBM per device.

```python
import math
import jax
import jax.numpy as jnp
from jax import lax

D = 2048
HK = 8
HV = 16
DH = 128
CONV = 4
GROUP = 64
SEQ = 8192


def head_roles(key):
    order = jax.random.permutation(jax.random.fold_in(key, 7001), HV)
    keeping = HV // 2
    return order < keeping


def mean_signs(key):
    flips = jax.random.randint(jax.random.fold_in(key, 7002), (D,), 0, 2)
    return flips.astype(jnp.float32) - 0.5


def draw_inputs(key, part):
    signs = mean_signs(key)
    noise_key = jax.random.fold_in(key, 7003)
    noise = jax.random.truncated_normal(noise_key, -6.0, 6.0, (SEQ, D), jnp.float32)
    return (noise + signs[None, :]).astype(jnp.bfloat16)


def draw_beta_weight(key, part):
    keeping = head_roles(key)
    signs = mean_signs(key)
    base_key = jax.random.fold_in(key, 7005)
    base = jax.random.truncated_normal(base_key, -6.0, 6.0, (D, HV), jnp.float32)
    target = math.log(0.6 * DH / SEQ)
    slow_cols = base * (0.5 / math.sqrt(D)) + target * 4.0 / D * signs[:, None]
    fast_cols = base * (1.0 / math.sqrt(D))
    return jnp.where(keeping[None, :], slow_cols, fast_cols).astype(jnp.bfloat16)


def draw_decay_log(key, part):
    keeping = head_roles(key)
    spread = jax.random.uniform(jax.random.fold_in(key, 7006), (HV,), jnp.float32, 0.0, 1.0)
    return jnp.where(keeping, 0.3 * spread, 2.77 * spread).astype(jnp.float32)


def draw_step_bias(key, part):
    keeping = head_roles(key)
    spread = jax.random.uniform(jax.random.fold_in(key, 7007), (HV,), jnp.float32, 0.0, 1.0)
    slow_bias = math.log(0.1 / SEQ) - 1.0 + spread
    fast_bias = -7.0 + 4.7 * spread
    return jnp.where(keeping, slow_bias, fast_bias).astype(jnp.float32)


def levels(stream_key, shape, cuts, low, largest):
    def one(dim, blocks):
        steps = jax.random.uniform(jax.random.fold_in(jax.random.fold_in(stream_key, 6), dim), (blocks,), jnp.float32, low / len(cuts), largest / len(cuts))
        return jnp.repeat(jnp.exp(steps), shape[dim] // blocks).reshape((-1,) + (1,) * (len(shape) - dim - 1))

    level = one(*cuts[0])
    for cut in cuts[1:]:
        level = level * one(*cut)
    return level


def centred(rng, extent, deviation, reach, split=(), kind=jnp.bfloat16):
    values = deviation * jax.random.normal(rng, extent, jnp.float32)
    if split:
        values = values * levels(rng, extent, split, -0.22, 0.18)
    return jnp.clip(values, -reach, reach).astype(kind)


def setup_inputs(seed: int = 0) -> dict:
    splits = jax.random.split(jax.random.key(seed), 13)
    inputs = draw_inputs(jax.random.fold_in(splits[12], 71), 0)
    query_weight = centred(splits[1], (D, HK * DH), D ** -0.5, 0.125, ((1, 8),))
    key_weight = centred(splits[2], (D, HK * DH), D ** -0.5, 0.125, ((1, 8),))
    value_weight = centred(splits[3], (D, HV * DH), D ** -0.5, 0.125, ((1, 8),))
    beta_weight = draw_beta_weight(jax.random.fold_in(splits[12], 71), 0)
    alpha_weight = centred(splits[5], (D, HV), D ** -0.5, 0.125, ((1, 8),))
    query_filter = centred(splits[6], (CONV, HK * DH), CONV ** -0.5, 3.0, ((1, 8),))
    key_filter = centred(splits[7], (CONV, HK * DH), CONV ** -0.5, 3.0, ((1, 8),))
    value_filter = centred(splits[8], (CONV, HV * DH), CONV ** -0.5, 3.0, ((1, 8),))
    decay_log = draw_decay_log(jax.random.fold_in(splits[12], 71), 0)
    step_bias = draw_step_bias(jax.random.fold_in(splits[12], 71), 0)
    grad_core = centred(splits[11], (SEQ, HV * DH), 1.0, 6.0, ((0, 64), (1, 8)))
    return dict(inputs=inputs, query_weight=query_weight, key_weight=key_weight, value_weight=value_weight, beta_weight=beta_weight, alpha_weight=alpha_weight, query_filter=query_filter, key_filter=key_filter, value_filter=value_filter, decay_log=decay_log, step_bias=step_bias, grad_core=grad_core)


EPS = 1e-06

def contract(form, left_arr, right_arr):
    return jnp.einsum(form, left_arr, right_arr, precision=lax.Precision.HIGHEST, preferred_element_type=jnp.float32)

def unit_lower_inverse(strict):
    size_now = strict.shape[-1]
    identity = jnp.eye(size_now, dtype=jnp.float32)
    result = identity - strict
    power_of = contract('...ij,...jk->...ik', strict, strict)
    covered = 2
    while covered < size_now:
        result = contract('...ij,...jk->...ik', result, identity + power_of)
        power_of = contract('...ij,...jk->...ik', power_of, power_of)
        covered = covered * 2
    return result

def conv_silu(padded, weight):
    tap_count = weight.shape[0]
    length = padded.shape[0] - tap_count + 1
    running = jnp.zeros((length, padded.shape[1]), jnp.float32)
    for tap_index in range(tap_count):
        running = running + weight[tap_index].astype(jnp.float32) * padded[tap_index:tap_index + length]
    return jax.nn.silu(running)

def normalized(rows_in, heads_count):
    shaped = rows_in.reshape(rows_in.shape[0], heads_count, -1)
    return shaped * lax.rsqrt(lax.optimization_barrier(jnp.sum(shaped * shaped, axis=-1, keepdims=True)) + EPS)

def to_blocks(rows_in, block_count):
    return rows_in.reshape(block_count, GROUP, rows_in.shape[1], -1).transpose(0, 2, 1, 3)

def prepare(query_pad, key_pad, value_pad, beta_raw, alpha_raw, query_filter, key_filter, value_filter, decay_log, step_bias):
    query_act = conv_silu(query_pad, query_filter)
    key_act = conv_silu(key_pad, key_filter)
    value_act = conv_silu(value_pad, value_filter)
    length = query_act.shape[0]
    key_heads = query_act.shape[1] // DH
    value_heads = value_act.shape[1] // DH
    ratio_kv = value_heads // key_heads
    block_count = length // GROUP
    query_unit = jnp.repeat(normalized(query_act, key_heads) * DH ** (-0.5), ratio_kv, axis=1)
    key_unit = jnp.repeat(normalized(key_act, key_heads), ratio_kv, axis=1)
    query_blk = to_blocks(query_unit, block_count)
    key_blk = to_blocks(key_unit, block_count)
    value_blk = to_blocks(value_act.reshape(length, value_heads, DH), block_count)
    beta_blk = jax.nn.sigmoid(beta_raw).reshape(block_count, GROUP, value_heads).transpose(0, 2, 1)
    log_decay = -jnp.exp(decay_log) * jax.nn.softplus(alpha_raw + step_bias)
    cum_decay = jnp.cumsum(log_decay.reshape(block_count, GROUP, value_heads).transpose(0, 2, 1), axis=-1)
    row_pos = lax.broadcasted_iota(jnp.int32, (GROUP, GROUP), 0)
    col_pos = lax.broadcasted_iota(jnp.int32, (GROUP, GROUP), 1)
    lower_mask = row_pos >= col_pos
    strictly = row_pos > col_pos
    gap_log = cum_decay[..., :, None] - cum_decay[..., None, :]
    decay_ij = jnp.where(lower_mask, jnp.exp(jnp.where(lower_mask, gap_log, 0.0)), 0.0)
    key_gram = contract('nhia,nhja->nhij', key_blk, key_blk)
    strict = jnp.where(strictly, beta_blk[..., :, None] * key_gram * decay_ij, 0.0)
    inverse = unit_lower_inverse(strict)
    gamma_at = jnp.exp(cum_decay)
    value_mix = contract('nhij,nhjb->nhib', inverse, beta_blk[..., None] * value_blk)
    key_weighted = contract('nhij,nhja->nhia', inverse, (beta_blk * gamma_at)[..., None] * key_blk)
    query_scaled = gamma_at[..., None] * query_blk
    key_tail = jnp.exp(cum_decay[..., -1:] - cum_decay)[..., None] * key_blk
    mixing = contract('nhia,nhja->nhij', query_blk, key_blk) * decay_ij
    end_decay = jnp.exp(cum_decay[..., -1])
    return (query_scaled, key_weighted, value_mix, key_tail, mixing, end_decay)

def transitions(pieces):
    query_scaled, key_weighted, value_mix, key_tail, mixing, end_decay = pieces
    unit_matrix = jnp.eye(key_tail.shape[-1], dtype=jnp.float32)
    trans_step = end_decay[..., None, None] * unit_matrix - contract('nhca,nhcd->nhad', key_tail, key_weighted)
    inject_step = contract('nhca,nhcb->nhab', key_tail, value_mix)
    return (trans_step, inject_step)

def head_outputs(pieces, starts):
    query_scaled, key_weighted, value_mix, key_tail, mixing, end_decay = pieces
    fresh = value_mix - contract('nhca,nhab->nhcb', key_weighted, starts)
    return contract('nhca,nhab->nhcb', query_scaled, starts) + contract('nhij,nhjb->nhib', mixing, fresh)

def core_forward(proj_query, proj_key, proj_value, proj_beta, proj_alpha, query_filter, key_filter, value_filter, decay_log, step_bias):
    conv_lag = CONV - 1

    def front_pad(rows_in):
        return jnp.concatenate([jnp.zeros((conv_lag, rows_in.shape[1]), jnp.float32), rows_in], 0)
    pieces = prepare(front_pad(proj_query), front_pad(proj_key), front_pad(proj_value), proj_beta, proj_alpha, query_filter, key_filter, value_filter, decay_log, step_bias)
    trans_step, inject_step = transitions(pieces)

    def advance(carried, step_pair):
        return (contract('had,hdb->hab', step_pair[0], carried) + step_pair[1], carried)
    initial = jnp.zeros(inject_step.shape[1:], jnp.float32)
    _, starts = lax.scan(advance, initial, (trans_step, inject_step))
    heads_out = head_outputs(pieces, starts)
    return heads_out.transpose(0, 2, 1, 3).reshape(proj_query.shape[0], -1)

def reference(inputs, query_weight, key_weight, value_weight, beta_weight, alpha_weight, query_filter, key_filter, value_filter, decay_log, step_bias, grad_core):
    weights = (query_weight, key_weight, value_weight, beta_weight, alpha_weight)
    rounded = lax.optimization_barrier(tuple((jnp.dot(inputs, weight, preferred_element_type=jnp.float32).astype(jnp.bfloat16) for weight in weights)))
    primals = tuple((member.astype(jnp.float32) for member in rounded))

    def forward(proj_query, proj_key, proj_value, proj_beta, proj_alpha):
        return core_forward(proj_query, proj_key, proj_value, proj_beta, proj_alpha, query_filter, key_filter, value_filter, decay_log, step_bias)
    _, backward = jax.vjp(forward, *primals)
    gradients = backward(grad_core.astype(jnp.float32))
    running = jnp.zeros(inputs.shape, jnp.float32)
    for grad_rows, weight in zip(gradients, weights):
        running = running + lax.dot_general(grad_rows.astype(jnp.bfloat16), weight, (((1,), (1,)), ((), ())), preferred_element_type=jnp.float32)
    return running.astype(jnp.bfloat16)
```

```python
import functools

import jax
import jax.numpy as jnp
from jax import lax
from jax.experimental import pallas as pl
from jax.experimental.pallas import tpu as pltpu
from jax.sharding import PartitionSpec as P

DH = 128
CONV = 4
EPS = 1e-06
SCALE = DH ** (-0.5)
RADIX = 4
PACK = 2 * DH + 16
F32 = jnp.float32
BF16 = jnp.bfloat16


def bf(value):
    return value.astype(BF16)


def dot(left, right, dims=(1, 0)):
    return lax.dot_general(
        bf(left), bf(right), (((dims[0],), (dims[1],)), ((), ())), preferred_element_type=F32
    )


def halves(value):
    high = bf(value)
    return high, bf(value - high.astype(F32))


def dot3(left, right, dims=(1, 0)):
    left_high, left_low = halves(left)
    right_high, right_low = halves(right)
    return dot(left_high, right_high, dims) + (
        dot(left_high, right_low, dims) + dot(left_low, right_high, dims)
    )


def dot_exact(left, right):
    return lax.dot_general(
        left, right, (((1,), (0,)), ((), ())),
        precision=lax.Precision.HIGHEST, preferred_element_type=F32,
    )


def positions(shape=(DH, DH)):
    return lax.broadcasted_iota(jnp.int32, shape, 0), lax.broadcasted_iota(jnp.int32, shape, 1)


def sigmoid(value):
    return 1.0 / (1.0 + jnp.exp(-value))


def softplus(value):
    return jnp.maximum(value, 0.0) + jnp.log1p(jnp.exp(-jnp.abs(value)))


def lanes_of(pieces):
    _, lane = positions()
    result = jnp.zeros((DH, DH), F32)
    for place, piece in enumerate(pieces):
        result = jnp.where(lane == place, piece, result)
    return result


def unit_lower_inverse(strict):
    row, col = positions()
    identity = jnp.where(row == col, 1.0, 0.0).astype(F32)
    inner = jnp.where(row // 8 == col // 8, strict, 0.0)
    square = dot3(inner, inner)
    result = dot3(identity - inner, identity + square)
    result = dot3(result, identity + dot3(square, square))
    size = 8
    while size < DH:
        off = (row // (2 * size) == col // (2 * size)) & (row // size != col // size)
        result = result - dot3(dot3(result, jnp.where(off, strict, 0.0)), result)
        size *= 2
    return result


def project_kernel(x_ref, wq_ref, wk_ref, wv_ref, wb_ref, wa_ref, proj_ref, ba_ref, tail_ref):
    parts = x_ref.shape[0]
    width = x_ref.shape[2]
    weights = (wq_ref, wk_ref, wv_ref, wb_ref, wa_ref)
    sums = [None] * 5
    for part in range(parts):
        rows = x_ref[part]
        for place, weight in enumerate(weights):
            piece = jnp.dot(
                rows, weight[part * width : (part + 1) * width, :], preferred_element_type=F32
            )
            sums[place] = piece if part == 0 else sums[place] + piece
    proj_ref[:, :DH] = bf(sums[0])
    proj_ref[:, DH : 2 * DH] = bf(sums[1])
    proj_ref[:, 2 * DH :] = bf(sums[2])
    tail_ref[:, :DH] = bf(sums[0][DH - 16 :])
    tail_ref[:, DH : 2 * DH] = bf(sums[1][DH - 16 :])
    tail_ref[:, 2 * DH :] = bf(sums[2][DH - 16 :])
    ba_ref[...] = bf(
        lanes_of([sums[3][:, 0:1], sums[3][:, 1:2], sums[4][:, 0:1], sums[4][:, 1:2]])
    )


def gate_rows(decay_ref, bias_ref):
    rate = lanes_of([0.0, 0.0, -jnp.exp(decay_ref[:, 0:1]), -jnp.exp(decay_ref[:, 1:2])])
    bias = lanes_of([0.0, 0.0, bias_ref[:, 0:1], bias_ref[:, 1:2]])
    return rate, bias


def split_decay(value):
    high = bf(value).astype(F32)
    middle = bf(value - high).astype(F32)
    low = value - high - middle
    row = lax.broadcasted_iota(jnp.int32, (16, DH), 0)
    return bf(jnp.where(row == 0, high, jnp.where(row == 1, middle, jnp.where(row == 2, low, 0.0))))


def slab_kernel(
    proj_ref, tail_ref, ba_ref, fq_ref, fk_ref, fv_ref, decay_ref, bias_ref, grad_ref,
    send_ref, pre_ref, unit_ref, cols_ref, inverse_ref, mixed_ref, weighted_ref,
    back_ref, gap_ref, gram_ref, cross_ref, pad_ref,
):
    row, col = positions()
    pad_ref[0:8] = tail_ref[8:16].astype(F32)
    pad_ref[8 : 8 + DH] = proj_ref[...].astype(F32)
    taps = jnp.concatenate(
        [fq_ref[...].astype(F32), fk_ref[...].astype(F32), fv_ref[...].astype(F32)], axis=1
    )
    pre = jnp.zeros((DH, 4 * DH), F32)
    for tap in range(CONV):
        start = 8 - (CONV - 1) + tap
        pre = pre + taps[tap : tap + 1] * pad_ref[start : start + DH]
    pre_ref[...] = pre
    act = pre * sigmoid(pre)
    query_act, key_act = act[:, :DH], act[:, DH : 2 * DH]
    query = query_act * (lax.rsqrt(jnp.sum(query_act * query_act, 1, keepdims=True) + EPS) * SCALE)
    key = key_act * lax.rsqrt(jnp.sum(key_act * key_act, 1, keepdims=True) + EPS)
    unit_ref[0] = query
    unit_ref[1] = key
    raw = ba_ref[...].astype(F32)
    rate, bias = gate_rows(decay_ref, bias_ref)
    log_decay = rate * softplus(raw + bias)
    lower = jnp.where(row >= col, 1.0, 0.0).astype(F32)
    summed = dot_exact(lower, log_decay)
    cols = jnp.where(col < 2, sigmoid(raw), summed)
    cols_ref[...] = cols
    rows = cols.T
    gram = dot3(key, key, (1, 1))
    cross = dot3(query, key, (1, 1))
    gram_ref[...] = gram
    cross_ref[...] = cross
    for head in range(2):
        beta = cols[:, head : head + 1]
        cum = cols[:, 2 + head : 3 + head]
        cum_row = rows[2 + head : 3 + head, :]
        value = act[:, (2 + head) * DH : (3 + head) * DH]
        grad = grad_ref[:, head * DH : (head + 1) * DH]
        gap = jnp.where(row >= col, jnp.exp(jnp.where(row >= col, cum - cum_row, 0.0)), 0.0)
        gap_ref[head] = gap
        gamma = jnp.exp(cum)
        last = cum[DH - 1 : DH, :]
        key_tail = jnp.exp(last - cum) * key
        strict = jnp.where(row > col, beta * gram * gap, 0.0)
        inverse = unit_lower_inverse(strict)
        mixed = dot3(inverse, beta * value)
        weighted = dot3(inverse, (beta * gamma) * key)
        back = dot(cross * gap, grad, (0, 0))
        inverse_ref[head] = bf(inverse)
        mixed_ref[head] = mixed
        weighted_ref[head] = bf(weighted)
        back_ref[head] = back
        moved = dot(key_tail, weighted, (0, 0))
        decay_rows = split_decay(jnp.exp(last))
        send_ref[2 * head, 0:DH] = bf(moved)
        send_ref[2 * head, DH : 2 * DH] = bf(dot(key_tail, mixed, (0, 0)))
        send_ref[2 * head, 2 * DH :] = decay_rows
        send_ref[2 * head + 1, 0:DH] = bf(moved.T)
        send_ref[2 * head + 1, DH : 2 * DH] = bf(
            dot(gamma * query, grad, (0, 0)) - dot(weighted, back, (0, 0))
        )
        send_ref[2 * head + 1, 2 * DH :] = decay_rows


def unpack(ref, place):
    decay = ref[place, 2 * DH :].astype(F32)
    return (
        decay[0:1, 0:1] + decay[1:2, 0:1] + decay[2:3, 0:1],
        ref[place, 0:DH],
        ref[place, DH : 2 * DH].astype(F32),
    )


def apply_map(later, state):
    decay, matrix, offset = later
    return decay * state - dot(matrix, state) + offset


def compose(later, earlier):
    decay, matrix, offset = later
    return (
        decay * earlier[0],
        decay * earlier[1] + earlier[0] * matrix.astype(F32) - dot(matrix, earlier[1]),
        apply_map(later, earlier[2]),
    )


def pack(ref, total):
    decay, matrix, offset = total
    packed = (bf(matrix), bf(offset), split_decay(decay))
    for place in range(RADIX):
        ref[place, 0:DH] = packed[0]
        ref[place, DH : 2 * DH] = packed[1]
        ref[place, 2 * DH :] = packed[2]


def widen(item):
    return item[0], item[1].astype(F32), item[2]


def in_order(step, backward):
    return jnp.where(backward, RADIX - 1 - step, step)


def group_kernel(got_ref, total_ref):
    backward = lax.axis_index("ctx") % 2 == 1
    total = widen(unpack(got_ref, in_order(0, backward)))
    for step in range(1, RADIX):
        total = compose(unpack(got_ref, in_order(step, backward)), total)
    pack(total_ref, total)


def row_kernel(got_ref, total_ref, before_ref):
    mine = lax.axis_index("ctx")
    backward = mine % 2 == 1
    place = in_order((mine // RADIX) % RADIX, backward)
    before_ref[0:DH] = jnp.zeros((DH, DH), F32)
    before_ref[DH : 2 * DH] = jnp.zeros((DH, DH), F32)
    before_ref[2 * DH :] = jnp.ones((8, DH), F32)
    total = widen(unpack(got_ref, in_order(0, backward)))
    for step in range(1, RADIX):

        @pl.when(place == step)
        def _(total=total):
            before_ref[0:DH] = total[1]
            before_ref[DH : 2 * DH] = total[2]
            before_ref[2 * DH :] = jnp.broadcast_to(total[0], (8, DH))

        total = compose(unpack(got_ref, in_order(step, backward)), total)
    pack(total_ref, total)


def states_kernel(rows_ref, before_ref, group_ref, out_ref):
    mine = lax.axis_index("ctx")
    backward = mine % 2 == 1
    place = in_order(mine // (RADIX * RADIX), backward)
    state = jnp.zeros((DH, DH), F32)
    for step in range(RADIX - 1):
        later = apply_map(unpack(rows_ref, in_order(step, backward)), state)
        state = jnp.where(step < place, later, state)
    before = (before_ref[2 * DH : 2 * DH + 1, 0:1], before_ref[0:DH], before_ref[DH : 2 * DH])
    state = apply_map(before, state)
    for step in range(RADIX):
        spot = in_order(step, backward)
        out_ref[spot] = bf(state)
        if step < RADIX - 1:
            state = apply_map(unpack(group_ref, spot), state)


def gradient_kernel(
    states_ref, pre_ref, unit_ref, cols_ref, ba_ref, inverse_ref, mixed_ref, weighted_ref,
    back_ref, gap_ref, gram_ref, cross_ref, grad_ref, fq_ref, fk_ref, fv_ref, decay_ref, bias_ref,
    full_ref, gates_ref, halo_ref, pad_ref,
):
    row, col = positions()
    cols = cols_ref[...]
    gram = gram_ref[...]
    cross = cross_ref[...]
    query = unit_ref[0]
    key = unit_ref[1]
    pre = pre_ref[...]
    gate = sigmoid(pre)
    act = pre * gate
    slope = gate * (1.0 + pre * (1.0 - gate))
    grad_query = jnp.zeros((DH, DH), F32)
    grad_key = jnp.zeros((DH, DH), F32)
    pieces = []
    columns = jnp.zeros((DH, DH), F32)
    sides = []
    for head in range(2):
        state = states_ref[2 * head]
        after = states_ref[2 * head + 1]
        beta = cols[:, head : head + 1]
        cum = cols[:, 2 + head : 3 + head]
        gamma = jnp.exp(cum)
        last = cum[DH - 1 : DH, :]
        rest = jnp.exp(last - cum)
        value = act[:, (2 + head) * DH : (3 + head) * DH]
        grad = grad_ref[:, head * DH : (head + 1) * DH]
        gap = gap_ref[head]
        fresh = mixed_ref[head] - dot(weighted_ref[head], state)
        grad_fresh = back_ref[head] + dot(rest * key, after)
        solved = dot(inverse_ref[head], grad_fresh, (0, 0))
        grad_strict = jnp.where(row > col, -dot(solved, fresh, (1, 1)), 0.0) * gap
        grad_cross = dot(grad, fresh, (1, 1)) * gap
        grad_weighted = -dot(solved, state, (1, 1))
        grad_scaled = dot(grad, state, (1, 1))
        grad_tail = dot(fresh, after, (1, 1))
        grad_query = grad_query + gamma * grad_scaled + dot(grad_cross, key)
        grad_gram = beta * grad_strict
        grad_key = grad_key + (
            dot(grad_cross, query, (0, 0))
            + dot(grad_gram, key)
            + dot(grad_gram, key, (0, 0))
            + (beta * gamma) * grad_weighted
            + rest * grad_tail
        )
        pieces.append(beta * solved)
        by_beta = jnp.sum(grad_strict * gram, 1, keepdims=True)
        by_key = gamma * jnp.sum(grad_weighted * key, 1, keepdims=True)
        grad_beta = jnp.sum(solved * value, 1, keepdims=True) + by_key + by_beta
        by_gap = grad_gram * gram + grad_cross * cross
        by_tail = rest * jnp.sum(grad_tail * key, 1, keepdims=True)
        at_end = jnp.sum(by_tail, 0, keepdims=True) + jnp.exp(last) * jnp.sum(
            jnp.sum(state.astype(F32) * after.astype(F32), 1, keepdims=True), 0, keepdims=True
        )
        grad_cum = (
            jnp.sum(by_gap, 1, keepdims=True)
            + gamma * jnp.sum(grad_scaled * query, 1, keepdims=True)
            + beta * by_key
            - by_tail
            + jnp.where(row[:, 0:1] == DH - 1, at_end, 0.0)
        )
        columns = jnp.where(row == 2 + head, jnp.sum(by_gap, 0, keepdims=True), columns)
        sides.append((grad_beta, grad_cum))
    raw = ba_ref[...].astype(F32)
    rate, bias = gate_rows(decay_ref, bias_ref)
    sides = lanes_of([sides[0][0], sides[1][0], sides[0][1], sides[1][1]]) - columns.T
    upper = jnp.where(row <= col, 1.0, 0.0).astype(F32)
    grad_log = dot_exact(upper, sides)
    beta = cols
    gates_ref[...] = bf(
        jnp.where(
            col < 2,
            sides * beta * (1.0 - beta),
            jnp.where(col < 4, grad_log * rate * sigmoid(raw + bias), 0.0),
        )
    )
    key_act = act[:, DH : 2 * DH]
    query_act = act[:, :DH]
    query_size = lax.rsqrt(jnp.sum(query_act * query_act, 1, keepdims=True) + EPS)
    key_size = lax.rsqrt(jnp.sum(key_act * key_act, 1, keepdims=True) + EPS)
    query_dir = query_act * query_size
    grad_query = grad_query * SCALE
    grad_query = query_size * (
        grad_query - query_dir * jnp.sum(grad_query * query_dir, 1, keepdims=True)
    )
    grad_key = key_size * (grad_key - key * jnp.sum(grad_key * key, 1, keepdims=True))
    pad_ref[0:8] = jnp.zeros((8, 4 * DH), F32)
    pad_ref[8 + DH :] = jnp.zeros((8, 4 * DH), F32)
    for place, piece in enumerate([grad_query, grad_key] + pieces):
        span = slice(place * DH, (place + 1) * DH)
        pad_ref[8 : 8 + DH, span] = piece * slope[:, span]
    taps = jnp.concatenate(
        [fq_ref[...].astype(F32), fk_ref[...].astype(F32), fv_ref[...].astype(F32)], axis=1
    )
    total = jnp.zeros((8 + DH, 4 * DH), F32)
    for tap in range(CONV):
        start = CONV - 1 - tap
        total = total + taps[tap : tap + 1] * pad_ref[start : start + 8 + DH]
    halo_ref[...] = total[0:8]
    full_ref[...] = total[8:]


def spread_kernel(full_ref, halo_ref, gates_ref, wq_ref, wk_ref, wv_ref, wb_ref, wa_ref, out_ref):
    full = full_ref[...]
    end = full[DH - 8 :] + halo_ref[...]
    grads = bf(jnp.concatenate([full[: DH - 8], end], axis=0))
    gates = gates_ref[...]
    width = out_ref.shape[2]
    for part in range(out_ref.shape[0]):
        span = slice(part * width, (part + 1) * width)
        total = dot(grads[:, :DH], wq_ref[span, :], (1, 1))
        total = total + dot(grads[:, DH : 2 * DH], wk_ref[span, :], (1, 1))
        total = total + dot(grads[:, 2 * DH :], wv_ref[span, :], (1, 1))
        total = total + dot(gates[:, 0:2], wb_ref[span, :], (1, 1))
        total = total + dot(gates[:, 2:4], wa_ref[span, :], (1, 1))
        out_ref[part] = bf(total)


def call(kernel, outs, scratch=()):
    return pl.pallas_call(
        kernel,
        out_shape=[jax.ShapeDtypeStruct(shape, kind) for shape, kind in outs],
        scratch_shapes=[pltpu.VMEM(shape, F32) for shape in scratch],
        compiler_params=pltpu.CompilerParams(vmem_limit_bytes=48 * 1024 * 1024),
    )


def project(gathered, weights):
    return call(
        project_kernel, [((DH, 4 * DH), BF16), ((DH, DH), BF16), ((16, 4 * DH), BF16)]
    )(gathered, *weights)


def slab(proj, tail, gates, filters, decay, bias, grad):
    square = (DH, DH)
    return call(
        slab_kernel,
        [
            ((4, PACK, DH), BF16), ((DH, 4 * DH), F32), ((2,) + square, F32), (square, F32),
            ((2,) + square, BF16), ((2,) + square, F32), ((2,) + square, BF16),
            ((2,) + square, F32), ((2,) + square, F32), (square, F32), (square, F32),
        ],
        [(8 + DH, 4 * DH)],
    )(proj, tail, gates, *filters, decay, bias, grad)


def gradient(states, kept, gates, filters, decay, bias, grad):
    pre, unit, cols, inverse, mixed, weighted, back, gap, gram, cross = kept
    return call(
        gradient_kernel,
        [((DH, 4 * DH), F32), ((DH, DH), BF16), ((8, 4 * DH), F32)],
        [(16 + DH, 4 * DH)],
    )(
        states, pre, unit, cols, gates, inverse, mixed, weighted, back, gap, gram, cross,
        grad, *filters, decay, bias,
    )


def spread(full, halo, gates, weights, parts):
    width = weights[0].shape[0] // parts
    return call(spread_kernel, [((parts, DH, width), BF16)])(full, halo, gates, *weights)[0]


def local(
    inputs, query_weight, key_weight, value_weight, beta_weight, alpha_weight,
    query_filter, key_filter, value_filter, decay_log, step_bias, grad_core,
):
    weights = (query_weight, key_weight, value_weight, beta_weight, alpha_weight)
    filters = (query_filter, key_filter, value_filter)
    decay = decay_log.reshape(1, 2)
    bias = step_bias.reshape(1, 2)
    count = lax.axis_size("ctx")
    parts = lax.axis_size("tp")
    slabs = range(count)
    group = [[s for s in slabs if s // RADIX == g] for g in range(count // RADIX)]
    row = [
        [s for s in slabs if s // 16 == y and s % RADIX == low]
        for y in range(count // 16) for low in range(RADIX)
    ]
    rank = [[s for s in slabs if s % 16 == z] for z in range(16)]

    def exchange(value, groups):
        return lax.all_to_all(value, "ctx", 0, 0, axis_index_groups=groups)

    gathered = lax.all_gather(inputs, "tp", axis=0)
    proj, gates, tail = project(gathered, weights)
    tail = lax.ppermute(tail, "ctx", [(s, s + 1) for s in range(count - 1)])
    send, *kept = slab(proj, tail, gates, filters, decay, bias, grad_core)
    got = exchange(send, group)
    total = call(group_kernel, [((RADIX, PACK, DH), BF16)])(got)[0]
    total, before = call(
        row_kernel, [((RADIX, PACK, DH), BF16), ((2 * DH + 8, DH), F32)]
    )(exchange(total, row))
    states = call(states_kernel, [((RADIX, DH, DH), BF16)])(exchange(total, rank), before, got)[0]
    states = exchange(states, group)
    full, grad_gates, halo = gradient(states, kept, gates, filters, decay, bias, grad_core)
    halo = lax.ppermute(halo, "ctx", [(s + 1, s) for s in range(count - 1)])
    shares = spread(full, halo, grad_gates, weights, parts)
    shares = lax.all_to_all(shares, "tp", 0, 0)
    return jnp.sum(shares.astype(F32), axis=0).astype(BF16)


def solution(mesh):
    sharded = P("ctx", "tp")
    kept = P(None, "tp")
    return jax.shard_map(
        local,
        mesh=mesh,
        in_specs=(sharded,) + (kept,) * 8 + (P("tp"), P("tp"), sharded),
        out_specs=sharded,
        check_vma=False,
    )
```

```python
import functools

import jax
import jax.numpy as jnp
from jax import lax
from jax.experimental import pallas as pl
from jax.experimental.pallas import tpu as pltpu
from jax.sharding import PartitionSpec as P

DH = 128
CONV = 4
EPS = 1e-06
SCALE = DH ** (-0.5)
PACK = 2 * DH + 16
F32 = jnp.float32
BF16 = jnp.bfloat16


def bf(value):
    return value.astype(BF16)


def dot(left, right, dims=(1, 0)):
    return lax.dot_general(
        bf(left), bf(right), (((dims[0],), (dims[1],)), ((), ())), preferred_element_type=F32
    )


def halves(value):
    high = bf(value)
    return high, bf(value - high.astype(F32))


def dot3(left, right, dims=(1, 0)):
    left_high, left_low = halves(left)
    right_high, right_low = halves(right)
    return dot(left_high, right_high, dims) + (
        dot(left_high, right_low, dims) + dot(left_low, right_high, dims)
    )


def dot_exact(left, right):
    return lax.dot_general(
        left, right, (((1,), (0,)), ((), ())),
        precision=lax.Precision.HIGHEST, preferred_element_type=F32,
    )


def positions(shape=(DH, DH)):
    return lax.broadcasted_iota(jnp.int32, shape, 0), lax.broadcasted_iota(jnp.int32, shape, 1)


def sigmoid(value):
    return 1.0 / (1.0 + jnp.exp(-value))


def softplus(value):
    return jnp.maximum(value, 0.0) + jnp.log1p(jnp.exp(-jnp.abs(value)))


def lanes_of(pieces):
    _, lane = positions()
    result = jnp.zeros((DH, DH), F32)
    for place, piece in enumerate(pieces):
        result = jnp.where(lane == place, piece, result)
    return result


def unit_lower_inverse(strict):
    row, col = positions()
    identity = jnp.where(row == col, 1.0, 0.0).astype(F32)
    inner = jnp.where(row // 8 == col // 8, strict, 0.0)
    square = dot3(inner, inner)
    result = dot3(identity - inner, identity + square)
    result = dot3(result, identity + dot3(square, square))
    size = 8
    while size < DH:
        off = (row // (2 * size) == col // (2 * size)) & (row // size != col // size)
        result = result - dot3(dot3(result, jnp.where(off, strict, 0.0)), result)
        size *= 2
    return result


def project_kernel(x_ref, wq_ref, wk_ref, wv_ref, wb_ref, wa_ref, proj_ref, ba_ref, tail_ref):
    parts = x_ref.shape[0]
    width = x_ref.shape[2]
    sums = [0.0] * 5
    for part in range(parts):
        rows = x_ref[part]
        span = slice(part * width, (part + 1) * width)
        for place, weight in enumerate((wq_ref, wk_ref, wv_ref)):
            sums[place] = sums[place] + dot(rows, weight[span, :])
        for place, weight in enumerate((wb_ref, wa_ref), 3):
            sums[place] = sums[place] + dot(rows, weight[:, span], (1, 1))
    proj_ref[:, :DH] = bf(sums[0])
    proj_ref[:, DH : 2 * DH] = bf(sums[1])
    proj_ref[:, 2 * DH :] = bf(sums[2])
    tail_ref[:, :DH] = bf(sums[0][DH - 16 :])
    tail_ref[:, DH : 2 * DH] = bf(sums[1][DH - 16 :])
    tail_ref[:, 2 * DH :] = bf(sums[2][DH - 16 :])
    ba_ref[...] = bf(
        lanes_of([sums[3][:, 0:1], sums[3][:, 1:2], sums[4][:, 0:1], sums[4][:, 1:2]])
    )


def gate_rows(decay_ref, bias_ref):
    rate = lanes_of([0.0, 0.0, -jnp.exp(decay_ref[:, 0:1]), -jnp.exp(decay_ref[:, 1:2])])
    bias = lanes_of([0.0, 0.0, bias_ref[:, 0:1], bias_ref[:, 1:2]])
    return rate, bias


def split_decay(value):
    high = bf(value).astype(F32)
    middle = bf(value - high).astype(F32)
    low = value - high - middle
    row = lax.broadcasted_iota(jnp.int32, (16, DH), 0)
    return bf(jnp.where(row == 0, high, jnp.where(row == 1, middle, jnp.where(row == 2, low, 0.0))))


def slab_kernel(
    proj_ref, tail_ref, ba_ref, fq_ref, fk_ref, fv_ref, decay_ref, bias_ref, grad_ref,
    own_ref, send_ref, pre_ref, unit_ref, cols_ref, inverse_ref, mixed_ref, weighted_ref,
    back_ref, gap_ref, gram_ref, cross_ref, pad_ref, maps_ref,
):
    row, col = positions()
    pad_ref[0:8] = tail_ref[8:16].astype(F32)
    pad_ref[8 : 8 + DH] = proj_ref[...].astype(F32)
    taps = jnp.concatenate(
        [fq_ref[...].astype(F32), fk_ref[...].astype(F32), fv_ref[...].astype(F32)], axis=1
    )
    pre = jnp.zeros((DH, 4 * DH), F32)
    for tap in range(CONV):
        start = 8 - (CONV - 1) + tap
        pre = pre + taps[tap : tap + 1] * pad_ref[start : start + DH]
    pre_ref[...] = pre
    act = pre * sigmoid(pre)
    query_act, key_act = act[:, :DH], act[:, DH : 2 * DH]
    query = query_act * (lax.rsqrt(jnp.sum(query_act * query_act, 1, keepdims=True) + EPS) * SCALE)
    key = key_act * lax.rsqrt(jnp.sum(key_act * key_act, 1, keepdims=True) + EPS)
    unit_ref[0] = query
    unit_ref[1] = key
    raw = ba_ref[...].astype(F32)
    rate, bias = gate_rows(decay_ref, bias_ref)
    log_decay = rate * softplus(raw + bias)
    lower = jnp.where(row >= col, 1.0, 0.0).astype(F32)
    summed = dot_exact(lower, log_decay)
    cols = jnp.where(col < 2, sigmoid(raw), summed)
    cols_ref[...] = cols
    rows = cols.T
    gram = dot3(key, key, (1, 1))
    cross = dot3(query, key, (1, 1))
    gram_ref[...] = gram
    cross_ref[...] = cross
    for head in range(2):
        beta = cols[:, head : head + 1]
        cum = cols[:, 2 + head : 3 + head]
        cum_row = rows[2 + head : 3 + head, :]
        value = act[:, (2 + head) * DH : (3 + head) * DH]
        grad = grad_ref[:, head * DH : (head + 1) * DH]
        gap = jnp.where(row >= col, jnp.exp(jnp.where(row >= col, cum - cum_row, 0.0)), 0.0)
        gap_ref[head] = gap
        gamma = jnp.exp(cum)
        last = cum[DH - 1 : DH, :]
        key_tail = jnp.exp(last - cum) * key
        strict = jnp.where(row > col, beta * gram * gap, 0.0)
        inverse = unit_lower_inverse(strict)
        mixed = dot3(inverse, beta * value)
        weighted = dot3(inverse, (beta * gamma) * key)
        back = dot(cross * gap, grad, (0, 0))
        inverse_ref[head] = bf(inverse)
        mixed_ref[head] = mixed
        weighted_ref[head] = bf(weighted)
        back_ref[head] = back
        maps_ref[head, 0:DH] = bf(dot(key_tail, weighted, (0, 0)))
        maps_ref[head, DH : 2 * DH] = bf(dot(key_tail, mixed, (0, 0)))
        maps_ref[head, 2 * DH : 3 * DH] = bf(
            dot(gamma * query, grad, (0, 0)) - dot(weighted, back, (0, 0))
        )
        maps_ref[head, 3 * DH :] = split_decay(jnp.exp(last))
    mine = bit(0)
    own_ref[...] = maps_ref[mine]
    send_ref[...] = maps_ref[1 - mine]


def unpack(ref):
    decay = ref[2 * DH :].astype(F32)
    return (
        decay[0:1, 0:1] + decay[1:2, 0:1] + decay[2:3, 0:1],
        ref[0:DH].astype(F32),
        ref[DH : 2 * DH].astype(F32),
    )


def pack(ref, total):
    decay, matrix, offset = total
    ref[0:DH] = bf(matrix)
    ref[DH : 2 * DH] = bf(offset)
    ref[2 * DH :] = split_decay(decay)


def apply_map(later, state):
    decay, matrix, offset = later
    return decay * state - dot(matrix, state) + offset


def compose(later, earlier):
    decay, matrix, offset = later
    return (
        decay * earlier[0],
        decay * earlier[1] + earlier[0] * matrix - dot(matrix, earlier[1]),
        apply_map(later, earlier[2]),
    )


def bit(place):
    return (lax.axis_index("ctx") >> place) & 1


def pair_maps(own_ref, got_ref):
    second = bit(0) == 1
    maps = []
    for flip in (second, jnp.logical_not(second)):
        parts = jnp.where(flip, got_ref[...].astype(F32), own_ref[...].astype(F32))
        decay = parts[3 * DH : 3 * DH + 1, 0:1] + parts[3 * DH + 1 : 3 * DH + 2, 0:1]
        decay = decay + parts[3 * DH + 2 : 3 * DH + 3, 0:1]
        maps.append((decay, parts[0:DH], parts[DH : 2 * DH], parts[2 * DH : 3 * DH]))
    return maps


def pair_kernel(own_ref, got_ref, send_ref, keep_ref):
    first, second = pair_maps(own_ref, got_ref)
    decay, matrix, offset = compose(second[:3], first[:3])
    adjoint = first[0] * second[3] - dot(first[1], second[3], (0, 0)) + first[3]
    turned = matrix.T
    backward = bit(1) == 1
    pack(send_ref, (decay, jnp.where(backward, matrix, turned), jnp.where(backward, offset, adjoint)))
    pack(keep_ref, (decay, jnp.where(backward, turned, matrix), jnp.where(backward, adjoint, offset)))


def group_kernel(keep_ref, got_ref, total_ref):
    pack(total_ref, compose(unpack(got_ref), unpack(keep_ref)))


def first_window_kernel(total_ref, got_ref, wider_ref):
    pack(wider_ref, compose(unpack(total_ref), unpack(got_ref)))


def window_kernel(total_ref, before_ref, got_ref, wider_ref, past_ref):
    got = unpack(got_ref)
    pack(wider_ref, compose(unpack(total_ref), got))
    pack(past_ref, compose(unpack(before_ref), got))


def last_window_kernel(total_ref, before_ref, got_ref, wider_ref, past_ref):
    got = unpack(got_ref)
    wider_ref[...] = bf(apply_map(unpack(total_ref), got[2]))
    pack(past_ref, compose(unpack(before_ref), got))


def start_kernel(past_ref, got_ref, keep_ref, mine_ref, send_ref):
    state = apply_map(unpack(past_ref), got_ref[...].astype(F32))
    mine_ref[...] = bf(state)
    send_ref[...] = bf(apply_map(unpack(keep_ref), state))


def states_kernel(mine_ref, got_ref, own_ref, partner_ref, here_ref, send_ref):
    first, second = pair_maps(own_ref, partner_ref)
    backward = bit(1) == 1
    mine = mine_ref[...].astype(F32)
    got = got_ref[...].astype(F32)
    state = jnp.where(backward, got, mine)
    after = jnp.where(backward, mine, got)
    later_state = apply_map(first[:3], state)
    earlier_after = second[0] * after - dot(second[1], after, (0, 0)) + second[3]
    odd = bit(0) == 1
    here_ref[0] = bf(jnp.where(odd, later_state, state))
    here_ref[1] = bf(jnp.where(odd, after, earlier_after))
    send_ref[0] = bf(jnp.where(odd, state, later_state))
    send_ref[1] = bf(jnp.where(odd, earlier_after, after))


def gradient_kernel(
    here_ref, there_ref, pre_ref, unit_ref, cols_ref, ba_ref, inverse_ref, mixed_ref, weighted_ref,
    back_ref, gap_ref, gram_ref, cross_ref, grad_ref, fq_ref, fk_ref, fv_ref, decay_ref, bias_ref,
    full_ref, gates_ref, halo_ref, pad_ref,
):
    row, col = positions()
    cols = cols_ref[...]
    gram = gram_ref[...]
    cross = cross_ref[...]
    query = unit_ref[0]
    key = unit_ref[1]
    pre = pre_ref[...]
    gate = sigmoid(pre)
    act = pre * gate
    slope = gate * (1.0 + pre * (1.0 - gate))
    grad_query = jnp.zeros((DH, DH), F32)
    grad_key = jnp.zeros((DH, DH), F32)
    pieces = []
    columns = jnp.zeros((DH, DH), F32)
    sides = []
    for head in range(2):
        held = bit(0) == head
        state = jnp.where(held, here_ref[0], there_ref[0])
        after = jnp.where(held, here_ref[1], there_ref[1])
        beta = cols[:, head : head + 1]
        cum = cols[:, 2 + head : 3 + head]
        gamma = jnp.exp(cum)
        last = cum[DH - 1 : DH, :]
        rest = jnp.exp(last - cum)
        value = act[:, (2 + head) * DH : (3 + head) * DH]
        grad = grad_ref[:, head * DH : (head + 1) * DH]
        gap = gap_ref[head]
        fresh = mixed_ref[head] - dot(weighted_ref[head], state)
        grad_fresh = back_ref[head] + dot(rest * key, after)
        solved = dot(inverse_ref[head], grad_fresh, (0, 0))
        grad_strict = jnp.where(row > col, -dot(solved, fresh, (1, 1)), 0.0) * gap
        grad_cross = dot(grad, fresh, (1, 1)) * gap
        grad_weighted = -dot(solved, state, (1, 1))
        grad_scaled = dot(grad, state, (1, 1))
        grad_tail = dot(fresh, after, (1, 1))
        grad_query = grad_query + gamma * grad_scaled + dot(grad_cross, key)
        grad_gram = beta * grad_strict
        grad_key = grad_key + (
            dot(grad_cross, query, (0, 0))
            + dot(grad_gram, key)
            + dot(grad_gram, key, (0, 0))
            + (beta * gamma) * grad_weighted
            + rest * grad_tail
        )
        pieces.append(beta * solved)
        by_beta = jnp.sum(grad_strict * gram, 1, keepdims=True)
        by_key = gamma * jnp.sum(grad_weighted * key, 1, keepdims=True)
        grad_beta = jnp.sum(solved * value, 1, keepdims=True) + by_key + by_beta
        by_gap = grad_gram * gram + grad_cross * cross
        by_tail = rest * jnp.sum(grad_tail * key, 1, keepdims=True)
        at_end = jnp.sum(by_tail, 0, keepdims=True) + jnp.exp(last) * jnp.sum(
            jnp.sum(state.astype(F32) * after.astype(F32), 1, keepdims=True), 0, keepdims=True
        )
        grad_cum = (
            jnp.sum(by_gap, 1, keepdims=True)
            + gamma * jnp.sum(grad_scaled * query, 1, keepdims=True)
            + beta * by_key
            - by_tail
            + jnp.where(row[:, 0:1] == DH - 1, at_end, 0.0)
        )
        columns = jnp.where(row == 2 + head, jnp.sum(by_gap, 0, keepdims=True), columns)
        sides.append((grad_beta, grad_cum))
    raw = ba_ref[...].astype(F32)
    rate, bias = gate_rows(decay_ref, bias_ref)
    sides = lanes_of([sides[0][0], sides[1][0], sides[0][1], sides[1][1]]) - columns.T
    upper = jnp.where(row <= col, 1.0, 0.0).astype(F32)
    grad_log = dot_exact(upper, sides)
    beta = cols
    gates_ref[...] = bf(
        jnp.where(
            col < 2,
            sides * beta * (1.0 - beta),
            jnp.where(col < 4, grad_log * rate * sigmoid(raw + bias), 0.0),
        )
    )
    key_act = act[:, DH : 2 * DH]
    query_act = act[:, :DH]
    query_size = lax.rsqrt(jnp.sum(query_act * query_act, 1, keepdims=True) + EPS)
    key_size = lax.rsqrt(jnp.sum(key_act * key_act, 1, keepdims=True) + EPS)
    query_dir = query_act * query_size
    grad_query = grad_query * SCALE
    grad_query = query_size * (
        grad_query - query_dir * jnp.sum(grad_query * query_dir, 1, keepdims=True)
    )
    grad_key = key_size * (grad_key - key * jnp.sum(grad_key * key, 1, keepdims=True))
    pad_ref[0:8] = jnp.zeros((8, 4 * DH), F32)
    pad_ref[8 + DH :] = jnp.zeros((8, 4 * DH), F32)
    for place, piece in enumerate([grad_query, grad_key] + pieces):
        span = slice(place * DH, (place + 1) * DH)
        pad_ref[8 : 8 + DH, span] = piece * slope[:, span]
    taps = jnp.concatenate(
        [fq_ref[...].astype(F32), fk_ref[...].astype(F32), fv_ref[...].astype(F32)], axis=1
    )
    total = jnp.zeros((8 + DH, 4 * DH), F32)
    for tap in range(CONV):
        start = CONV - 1 - tap
        total = total + taps[tap : tap + 1] * pad_ref[start : start + 8 + DH]
    halo_ref[...] = total[0:8]
    full_ref[...] = total[8:]


def spread_kernel(full_ref, halo_ref, gates_ref, wq_ref, wk_ref, wv_ref, wb_ref, wa_ref, out_ref):
    full = full_ref[...]
    end = full[DH - 8 :] + halo_ref[...]
    grads = bf(jnp.concatenate([full[: DH - 8], end], axis=0))
    gates = gates_ref[...]
    width = out_ref.shape[2]
    for part in range(out_ref.shape[0]):
        span = slice(part * width, (part + 1) * width)
        total = dot(grads[:, :DH], wq_ref[span, :], (1, 1))
        total = total + dot(grads[:, DH : 2 * DH], wk_ref[span, :], (1, 1))
        total = total + dot(grads[:, 2 * DH :], wv_ref[span, :], (1, 1))
        total = total + dot(gates[:, 0:2], wb_ref[:, span])
        total = total + dot(gates[:, 2:4], wa_ref[:, span])
        out_ref[part] = bf(total)


def call(kernel, outs, scratch=()):
    return pl.pallas_call(
        kernel,
        out_shape=[jax.ShapeDtypeStruct(shape, kind) for shape, kind in outs],
        scratch_shapes=[pltpu.VMEM(shape, kind) for shape, kind in scratch],
        compiler_params=pltpu.CompilerParams(vmem_limit_bytes=48 * 1024 * 1024),
    )


def project(gathered, weights):
    return call(
        project_kernel, [((DH, 4 * DH), BF16), ((DH, DH), BF16), ((16, 4 * DH), BF16)]
    )(gathered, *weights)


def slab(proj, tail, gates, filters, decay, bias, grad):
    square = (DH, DH)
    return call(
        slab_kernel,
        [
            ((PACK + DH, DH), BF16), ((PACK + DH, DH), BF16),
            ((DH, 4 * DH), F32), ((2,) + square, F32), (square, F32),
            ((2,) + square, BF16), ((2,) + square, F32), ((2,) + square, BF16),
            ((2,) + square, F32), ((2,) + square, F32), (square, F32), (square, F32),
        ],
        [((8 + DH, 4 * DH), F32), ((2, PACK + DH, DH), BF16)],
    )(proj, tail, gates, *filters, decay, bias, grad)


def gradient(here, there, kept, gates, filters, decay, bias, grad):
    pre, unit, cols, inverse, mixed, weighted, back, gap, gram, cross = kept
    return call(
        gradient_kernel,
        [((DH, 4 * DH), F32), ((DH, DH), BF16), ((8, 4 * DH), F32)],
        [((16 + DH, 4 * DH), F32)],
    )(
        here, there, pre, unit, cols, gates, inverse, mixed, weighted, back, gap, gram, cross,
        grad, *filters, decay, bias,
    )


def spread(full, halo, gates, weights, parts):
    width = weights[0].shape[0] // parts
    return call(spread_kernel, [((parts, DH, width), BF16)])(full, halo, gates, *weights)[0]


def local(
    inputs, query_weight, key_weight, value_weight, beta_weight, alpha_weight,
    query_filter, key_filter, value_filter, decay_log, step_bias, grad_core,
):
    weights = (query_weight, key_weight, value_weight, beta_weight.T, alpha_weight.T)
    filters = (query_filter, key_filter, value_filter)
    decay = decay_log.reshape(1, 2)
    bias = step_bias.reshape(1, 2)
    count = lax.axis_size("ctx")
    parts = lax.axis_size("tp")
    packed = ((PACK, DH), BF16)
    square = ((DH, DH), BF16)

    def swap(value, distance):
        return lax.ppermute(value, "ctx", [(s, s ^ distance) for s in range(count)])

    def onward(value, distance):
        steps = [(s, s - distance if s & 2 else s + distance) for s in range(count)]
        return lax.ppermute(value, "ctx", [(s, t) for s, t in steps if 0 <= t < count])

    gathered = lax.all_gather(inputs, "tp", axis=0)
    proj, gates, tail = project(gathered, weights)
    tail = lax.ppermute(tail, "ctx", [(s, s + 1) for s in range(count - 1)])
    own, send, *kept = slab(proj, tail, gates, filters, decay, bias, grad_core)
    partner = swap(send, 1)
    send, keep = call(pair_kernel, [packed, packed])(own, partner)
    total = call(group_kernel, [packed])(keep, swap(send, 2))[0]
    before = onward(total, 4)
    total = call(first_window_kernel, [packed])(total, before)[0]
    total, before = call(window_kernel, [packed, packed])(total, before, onward(total, 8))
    total, before = call(last_window_kernel, [square, packed])(total, before, onward(total, 16))
    mine, send = call(start_kernel, [square, square])(before, onward(total, 32), keep)
    here, send = call(states_kernel, [((2, DH, DH), BF16)] * 2)(mine, swap(send, 2), own, partner)
    there = swap(send, 1)
    full, grad_gates, halo = gradient(here, there, kept, gates, filters, decay, bias, grad_core)
    halo = lax.ppermute(halo, "ctx", [(s + 1, s) for s in range(count - 1)])
    shares = spread(full, halo, grad_gates, weights, parts)
    shares = lax.all_to_all(shares, "tp", 0, 0)
    return jnp.sum(shares.astype(F32), axis=0).astype(BF16)


def solution(mesh):
    sharded = P("ctx", "tp")
    kept = P(None, "tp")
    return jax.shard_map(
        local,
        mesh=mesh,
        in_specs=(sharded,) + (kept,) * 8 + (P("tp"), P("tp"), sharded),
        out_specs=sharded,
        check_vma=False,
    )
```

```python
import functools

import jax
import jax.numpy as jnp
from jax import lax
from jax.experimental import pallas as pl
from jax.experimental.pallas import tpu as pltpu
from jax.sharding import PartitionSpec as P

DH = 128
CONV = 4
EPS = 1e-06
SCALE = DH ** (-0.5)
RADIX = 4
PACK = 2 * DH + 16
F32 = jnp.float32
BF16 = jnp.bfloat16


def bf(value):
    return value.astype(BF16)


def dot(left, right, dims=(1, 0)):
    return lax.dot_general(
        bf(left), bf(right), (((dims[0],), (dims[1],)), ((), ())), preferred_element_type=F32
    )


def halves(value):
    high = bf(value)
    return high, bf(value - high.astype(F32))


def dot3(left, right, dims=(1, 0)):
    left_high, left_low = halves(left)
    right_high, right_low = halves(right)
    return dot(left_high, right_high, dims) + (
        dot(left_high, right_low, dims) + dot(left_low, right_high, dims)
    )


def dot_exact(left, right):
    return lax.dot_general(
        left, right, (((1,), (0,)), ((), ())),
        precision=lax.Precision.HIGHEST, preferred_element_type=F32,
    )


def positions(shape=(DH, DH)):
    return lax.broadcasted_iota(jnp.int32, shape, 0), lax.broadcasted_iota(jnp.int32, shape, 1)


def sigmoid(value):
    return 1.0 / (1.0 + jnp.exp(-value))


def softplus(value):
    return jnp.maximum(value, 0.0) + jnp.log1p(jnp.exp(-jnp.abs(value)))


def lanes_of(pieces):
    _, lane = positions()
    result = jnp.zeros((DH, DH), F32)
    for place, piece in enumerate(pieces):
        result = jnp.where(lane == place, piece, result)
    return result


def unit_lower_inverse(strict):
    row, col = positions()
    identity = jnp.where(row == col, 1.0, 0.0).astype(F32)
    inner = jnp.where(row // 8 == col // 8, strict, 0.0)
    square = dot3(inner, inner)
    result = dot3(identity - inner, identity + square)
    result = dot3(result, identity + dot3(square, square))
    size = 8
    while size < DH:
        off = (row // (2 * size) == col // (2 * size)) & (row // size != col // size)
        result = result - dot3(dot3(result, jnp.where(off, strict, 0.0)), result)
        size *= 2
    return result


def project_kernel(
    x_ref, wq_ref, wk_ref, wv_ref, wb_ref, wa_ref, proj_ref, ba_ref, tail_ref, held_ref, sems
):
    parts, _, width = x_ref.shape
    places = (slice(0, DH), slice(DH, 2 * DH), slice(2 * DH, 4 * DH))
    copies = []
    for part in range(parts):
        span = slice(part * width, (part + 1) * width)
        for place, weight in enumerate((wq_ref, wk_ref, wv_ref)):
            copies.append(
                pltpu.make_async_copy(
                    weight.at[span, :], held_ref.at[span, places[place]], sems.at[part, place]
                )
            )
            copies[-1].start()
    total = jnp.zeros((DH, 4 * DH), F32)
    beta = jnp.zeros((DH, 2), F32)
    alpha = jnp.zeros((DH, 2), F32)
    for part in range(parts):
        rows = x_ref[part]
        span = slice(part * width, (part + 1) * width)
        beta = beta + dot(rows, wb_ref[:, span], (1, 1))
        alpha = alpha + dot(rows, wa_ref[:, span], (1, 1))
        for copy in copies[3 * part : 3 * part + 3]:
            copy.wait()
        total = total + dot(rows, held_ref[span, :])
    proj_ref[...] = bf(total)
    tail_ref[...] = bf(total[DH - 16 :])
    ba_ref[...] = bf(lanes_of([beta[:, 0:1], beta[:, 1:2], alpha[:, 0:1], alpha[:, 1:2]]))


def gate_rows(decay_ref, bias_ref):
    rate = lanes_of([0.0, 0.0, -jnp.exp(decay_ref[:, 0:1]), -jnp.exp(decay_ref[:, 1:2])])
    bias = lanes_of([0.0, 0.0, bias_ref[:, 0:1], bias_ref[:, 1:2]])
    return rate, bias


def split_decay(value):
    high = bf(value).astype(F32)
    middle = bf(value - high).astype(F32)
    low = value - high - middle
    row = lax.broadcasted_iota(jnp.int32, (16, DH), 0)
    return bf(jnp.where(row == 0, high, jnp.where(row == 1, middle, jnp.where(row == 2, low, 0.0))))


def slab_kernel(
    proj_ref, tail_ref, ba_ref, fq_ref, fk_ref, fv_ref, decay_ref, bias_ref, grad_ref,
    send_ref, pre_ref, unit_ref, cols_ref, inverse_ref, mixed_ref, weighted_ref,
    back_ref, gap_ref, gram_ref, cross_ref, pad_ref,
):
    row, col = positions()
    pad_ref[0:8] = tail_ref[8:16].astype(F32)
    pad_ref[8 : 8 + DH] = proj_ref[...].astype(F32)
    taps = jnp.concatenate(
        [fq_ref[...].astype(F32), fk_ref[...].astype(F32), fv_ref[...].astype(F32)], axis=1
    )
    pre = jnp.zeros((DH, 4 * DH), F32)
    for tap in range(CONV):
        start = 8 - (CONV - 1) + tap
        pre = pre + taps[tap : tap + 1] * pad_ref[start : start + DH]
    pre_ref[...] = pre
    act = pre * sigmoid(pre)
    query_act, key_act = act[:, :DH], act[:, DH : 2 * DH]
    query = query_act * (lax.rsqrt(jnp.sum(query_act * query_act, 1, keepdims=True) + EPS) * SCALE)
    key = key_act * lax.rsqrt(jnp.sum(key_act * key_act, 1, keepdims=True) + EPS)
    unit_ref[0] = query
    unit_ref[1] = key
    raw = ba_ref[...].astype(F32)
    rate, bias = gate_rows(decay_ref, bias_ref)
    log_decay = rate * softplus(raw + bias)
    lower = jnp.where(row >= col, 1.0, 0.0).astype(F32)
    summed = dot_exact(lower, log_decay)
    cols = jnp.where(col < 2, sigmoid(raw), summed)
    cols_ref[...] = cols
    rows = cols.T
    gram = dot3(key, key, (1, 1))
    cross = dot3(query, key, (1, 1))
    gram_ref[...] = gram
    cross_ref[...] = cross
    for head in range(2):
        beta = cols[:, head : head + 1]
        cum = cols[:, 2 + head : 3 + head]
        cum_row = rows[2 + head : 3 + head, :]
        value = act[:, (2 + head) * DH : (3 + head) * DH]
        grad = grad_ref[:, head * DH : (head + 1) * DH]
        gap = jnp.where(row >= col, jnp.exp(jnp.where(row >= col, cum - cum_row, 0.0)), 0.0)
        gap_ref[head] = gap
        gamma = jnp.exp(cum)
        last = cum[DH - 1 : DH, :]
        key_tail = jnp.exp(last - cum) * key
        strict = jnp.where(row > col, beta * gram * gap, 0.0)
        inverse = unit_lower_inverse(strict)
        mixed = dot3(inverse, beta * value)
        weighted = dot3(inverse, (beta * gamma) * key)
        back = dot(cross * gap, grad, (0, 0))
        inverse_ref[head] = bf(inverse)
        mixed_ref[head] = mixed
        weighted_ref[head] = bf(weighted)
        back_ref[head] = back
        moved = dot(key_tail, weighted, (0, 0))
        decay_rows = split_decay(jnp.exp(last))
        send_ref[2 * head, 0:DH] = bf(moved)
        send_ref[2 * head, DH : 2 * DH] = bf(dot(key_tail, mixed, (0, 0)))
        send_ref[2 * head, 2 * DH :] = decay_rows
        send_ref[2 * head + 1, 0:DH] = bf(moved.T)
        send_ref[2 * head + 1, DH : 2 * DH] = bf(
            dot(gamma * query, grad, (0, 0)) - dot(weighted, back, (0, 0))
        )
        send_ref[2 * head + 1, 2 * DH :] = decay_rows


def unpack(ref):
    decay = ref[2 * DH :].astype(F32)
    return (
        decay[0:1, 0:1] + decay[1:2, 0:1] + decay[2:3, 0:1],
        ref[0:DH].astype(F32),
        ref[DH : 2 * DH].astype(F32),
    )


def apply_map(later, state):
    decay, matrix, offset = later
    return decay * state - dot(matrix, state) + offset


def compose(later, earlier):
    decay, matrix, offset = later
    return (
        decay * earlier[0],
        decay * earlier[1] + earlier[0] * matrix - dot(matrix, earlier[1]),
        apply_map(later, earlier[2]),
    )


def pack(total):
    decay, matrix, offset = total
    return jnp.concatenate([bf(matrix), bf(offset), split_decay(decay)], axis=0)


def is_backward():
    return lax.axis_index("ctx") % 2 == 1


def in_order(step, backward):
    return jnp.where(backward, RADIX - 1 - step, step)


def group_kernel(got_ref, total_ref):
    backward = is_backward()
    total = unpack(got_ref.at[in_order(0, backward)])
    for step in range(1, RADIX):
        total = compose(unpack(got_ref.at[in_order(step, backward)]), total)
    total_ref[...] = pack(total)


def window_kernel(total_ref, last_ref, middle_ref, first_ref, wider_ref, before_ref):
    before = compose(unpack(last_ref), compose(unpack(middle_ref), unpack(first_ref)))
    before_ref[0:DH] = before[1]
    before_ref[DH : 2 * DH] = before[2]
    before_ref[2 * DH :] = jnp.broadcast_to(before[0], (8, DH))
    wider = pack(compose(unpack(total_ref), before))
    for place in range(RADIX):
        wider_ref[place] = wider


def states_kernel(rows_ref, before_ref, group_ref, out_ref):
    backward = is_backward()
    place = in_order(lax.axis_index("ctx") // (RADIX * RADIX), backward)
    state = jnp.zeros((DH, DH), F32)
    for step in range(RADIX - 1):
        later = apply_map(unpack(rows_ref.at[in_order(step, backward)]), state)
        state = jnp.where(step < place, later, state)
    before = (before_ref[2 * DH : 2 * DH + 1, 0:1], before_ref[0:DH], before_ref[DH : 2 * DH])
    state = apply_map(before, state)
    for step in range(RADIX):
        spot = in_order(step, backward)
        out_ref[spot] = bf(state)
        if step < RADIX - 1:
            state = apply_map(unpack(group_ref.at[spot]), state)


def gradient_kernel(
    states_ref, pre_ref, unit_ref, cols_ref, ba_ref, inverse_ref, mixed_ref, weighted_ref,
    back_ref, gap_ref, gram_ref, cross_ref, grad_ref, fq_ref, fk_ref, fv_ref, decay_ref, bias_ref,
    full_ref, gates_ref, halo_ref, pad_ref,
):
    row, col = positions()
    cols = cols_ref[...]
    gram = gram_ref[...]
    cross = cross_ref[...]
    query = unit_ref[0]
    key = unit_ref[1]
    pre = pre_ref[...]
    gate = sigmoid(pre)
    act = pre * gate
    slope = gate * (1.0 + pre * (1.0 - gate))
    grad_query = jnp.zeros((DH, DH), F32)
    grad_key = jnp.zeros((DH, DH), F32)
    pieces = []
    columns = jnp.zeros((DH, DH), F32)
    sides = []
    for head in range(2):
        state = states_ref[2 * head]
        after = states_ref[2 * head + 1]
        beta = cols[:, head : head + 1]
        cum = cols[:, 2 + head : 3 + head]
        gamma = jnp.exp(cum)
        last = cum[DH - 1 : DH, :]
        rest = jnp.exp(last - cum)
        value = act[:, (2 + head) * DH : (3 + head) * DH]
        grad = grad_ref[:, head * DH : (head + 1) * DH]
        gap = gap_ref[head]
        fresh = mixed_ref[head] - dot(weighted_ref[head], state)
        grad_fresh = back_ref[head] + dot(rest * key, after)
        solved = dot(inverse_ref[head], grad_fresh, (0, 0))
        grad_strict = jnp.where(row > col, -dot(solved, fresh, (1, 1)), 0.0) * gap
        grad_cross = dot(grad, fresh, (1, 1)) * gap
        grad_weighted = -dot(solved, state, (1, 1))
        grad_scaled = dot(grad, state, (1, 1))
        grad_tail = dot(fresh, after, (1, 1))
        grad_query = grad_query + gamma * grad_scaled + dot(grad_cross, key)
        grad_gram = beta * grad_strict
        grad_key = grad_key + (
            dot(grad_cross, query, (0, 0))
            + dot(grad_gram, key)
            + dot(grad_gram, key, (0, 0))
            + (beta * gamma) * grad_weighted
            + rest * grad_tail
        )
        pieces.append(beta * solved)
        by_beta = jnp.sum(grad_strict * gram, 1, keepdims=True)
        by_key = gamma * jnp.sum(grad_weighted * key, 1, keepdims=True)
        grad_beta = jnp.sum(solved * value, 1, keepdims=True) + by_key + by_beta
        by_gap = grad_gram * gram + grad_cross * cross
        by_tail = rest * jnp.sum(grad_tail * key, 1, keepdims=True)
        at_end = jnp.sum(by_tail, 0, keepdims=True) + jnp.exp(last) * jnp.sum(
            jnp.sum(state.astype(F32) * after.astype(F32), 1, keepdims=True), 0, keepdims=True
        )
        grad_cum = (
            jnp.sum(by_gap, 1, keepdims=True)
            + gamma * jnp.sum(grad_scaled * query, 1, keepdims=True)
            + beta * by_key
            - by_tail
            + jnp.where(row[:, 0:1] == DH - 1, at_end, 0.0)
        )
        columns = jnp.where(row == 2 + head, jnp.sum(by_gap, 0, keepdims=True), columns)
        sides.append((grad_beta, grad_cum))
    raw = ba_ref[...].astype(F32)
    rate, bias = gate_rows(decay_ref, bias_ref)
    sides = lanes_of([sides[0][0], sides[1][0], sides[0][1], sides[1][1]]) - columns.T
    upper = jnp.where(row <= col, 1.0, 0.0).astype(F32)
    grad_log = dot_exact(upper, sides)
    beta = cols
    gates_ref[...] = bf(
        jnp.where(
            col < 2,
            sides * beta * (1.0 - beta),
            jnp.where(col < 4, grad_log * rate * sigmoid(raw + bias), 0.0),
        )
    )
    key_act = act[:, DH : 2 * DH]
    query_act = act[:, :DH]
    query_size = lax.rsqrt(jnp.sum(query_act * query_act, 1, keepdims=True) + EPS)
    key_size = lax.rsqrt(jnp.sum(key_act * key_act, 1, keepdims=True) + EPS)
    query_dir = query_act * query_size
    grad_query = grad_query * SCALE
    grad_query = query_size * (
        grad_query - query_dir * jnp.sum(grad_query * query_dir, 1, keepdims=True)
    )
    grad_key = key_size * (grad_key - key * jnp.sum(grad_key * key, 1, keepdims=True))
    pad_ref[0:8] = jnp.zeros((8, 4 * DH), F32)
    pad_ref[8 + DH :] = jnp.zeros((8, 4 * DH), F32)
    for place, piece in enumerate([grad_query, grad_key] + pieces):
        span = slice(place * DH, (place + 1) * DH)
        pad_ref[8 : 8 + DH, span] = piece * slope[:, span]
    taps = jnp.concatenate(
        [fq_ref[...].astype(F32), fk_ref[...].astype(F32), fv_ref[...].astype(F32)], axis=1
    )
    total = jnp.zeros((8 + DH, 4 * DH), F32)
    for tap in range(CONV):
        start = CONV - 1 - tap
        total = total + taps[tap : tap + 1] * pad_ref[start : start + 8 + DH]
    halo_ref[...] = total[0:8]
    full_ref[...] = total[8:]


def spread_kernel(full_ref, halo_ref, gates_ref, wq_ref, wk_ref, wv_ref, wb_ref, wa_ref, out_ref):
    full = full_ref[...]
    end = full[DH - 8 :] + halo_ref[...]
    grads = bf(jnp.concatenate([full[: DH - 8], end], axis=0))
    gates = gates_ref[...]
    width = out_ref.shape[2]
    for part in range(out_ref.shape[0]):
        span = slice(part * width, (part + 1) * width)
        total = dot(grads[:, :DH], wq_ref[span, :], (1, 1))
        total = total + dot(grads[:, DH : 2 * DH], wk_ref[span, :], (1, 1))
        total = total + dot(grads[:, 2 * DH :], wv_ref[span, :], (1, 1))
        total = total + dot(gates[:, 0:2], wb_ref[:, span])
        total = total + dot(gates[:, 2:4], wa_ref[:, span])
        out_ref[part] = bf(total)


def call(kernel, outs, scratch=(), specs=None):
    extra = {} if specs is None else {"in_specs": specs}
    return pl.pallas_call(
        kernel,
        out_shape=[jax.ShapeDtypeStruct(shape, kind) for shape, kind in outs],
        scratch_shapes=list(scratch),
        compiler_params=pltpu.CompilerParams(vmem_limit_bytes=48 * 1024 * 1024),
        **extra,
    )


def project(gathered, weights):
    parts = gathered.shape[0]
    inside = pl.BlockSpec(memory_space=pltpu.VMEM)
    outside = pl.BlockSpec(memory_space=pl.ANY)
    return call(
        project_kernel,
        [((DH, 4 * DH), BF16), ((DH, DH), BF16), ((16, 4 * DH), BF16)],
        [
            pltpu.VMEM((weights[0].shape[0], 4 * DH), BF16),
            pltpu.SemaphoreType.DMA((parts, 3)),
        ],
        [inside] + [outside] * 3 + [inside] * 2,
    )(gathered, *weights)


def slab(proj, tail, gates, filters, decay, bias, grad):
    square = (DH, DH)
    return call(
        slab_kernel,
        [
            ((4, PACK, DH), BF16), ((DH, 4 * DH), F32), ((2,) + square, F32), (square, F32),
            ((2,) + square, BF16), ((2,) + square, F32), ((2,) + square, BF16),
            ((2,) + square, F32), ((2,) + square, F32), (square, F32), (square, F32),
        ],
        [pltpu.VMEM((8 + DH, 4 * DH), F32)],
    )(proj, tail, gates, *filters, decay, bias, grad)


def gradient(states, kept, gates, filters, decay, bias, grad):
    pre, unit, cols, inverse, mixed, weighted, back, gap, gram, cross = kept
    return call(
        gradient_kernel,
        [((DH, 4 * DH), F32), ((DH, DH), BF16), ((8, 4 * DH), F32)],
        [pltpu.VMEM((16 + DH, 4 * DH), F32)],
    )(
        states, pre, unit, cols, gates, inverse, mixed, weighted, back, gap, gram, cross,
        grad, *filters, decay, bias,
    )


def spread(full, halo, gates, weights, parts):
    width = weights[0].shape[0] // parts
    return call(spread_kernel, [((parts, DH, width), BF16)])(full, halo, gates, *weights)[0]


def local(
    inputs, query_weight, key_weight, value_weight, beta_weight, alpha_weight,
    query_filter, key_filter, value_filter, decay_log, step_bias, grad_core,
):
    weights = (query_weight, key_weight, value_weight, beta_weight.T, alpha_weight.T)
    filters = (query_filter, key_filter, value_filter)
    decay = decay_log.reshape(1, 2)
    bias = step_bias.reshape(1, 2)
    count = lax.axis_size("ctx")
    parts = lax.axis_size("tp")
    slabs = range(count)
    group = [[s for s in slabs if s // RADIX == g] for g in range(count // RADIX)]
    rank = [[s for s in slabs if s % 16 == z] for z in range(16)]

    def exchange(value, groups):
        return lax.all_to_all(value, "ctx", 0, 0, axis_index_groups=groups)

    def onward(value, distance):
        steps = [(s, s - distance if s % 2 else s + distance) for s in slabs]
        return lax.ppermute(value, "ctx", [(s, t) for s, t in steps if 0 <= t < count])

    gathered = lax.all_gather(inputs, "tp", axis=0)
    proj, gates, tail = project(gathered, weights)
    tail = lax.ppermute(tail, "ctx", [(s, s + 1) for s in range(count - 1)])
    send, *kept = slab(proj, tail, gates, filters, decay, bias, grad_core)
    got = exchange(send, group)
    total = call(group_kernel, [((PACK, DH), BF16)])(got)[0]
    earlier = [onward(total, RADIX * step) for step in range(1, RADIX)]
    total, before = call(
        window_kernel, [((RADIX, PACK, DH), BF16), ((2 * DH + 8, DH), F32)]
    )(total, *earlier)
    states = call(states_kernel, [((RADIX, DH, DH), BF16)])(exchange(total, rank), before, got)[0]
    states = exchange(states, group)
    full, grad_gates, halo = gradient(states, kept, gates, filters, decay, bias, grad_core)
    halo = lax.ppermute(halo, "ctx", [(s + 1, s) for s in range(count - 1)])
    shares = spread(full, halo, grad_gates, weights, parts)
    shares = lax.all_to_all(shares, "tp", 0, 0)
    return jnp.sum(shares.astype(F32), axis=0).astype(BF16)


def solution(mesh):
    sharded = P("ctx", "tp")
    kept = P(None, "tp")
    return jax.shard_map(
        local,
        mesh=mesh,
        in_specs=(sharded,) + (kept,) * 8 + (P("tp"), P("tp"), sharded),
        out_specs=sharded,
        check_vma=False,
    )
```

```python
import functools

import jax
import jax.numpy as jnp
from jax import lax
from jax.experimental import pallas as pl
from jax.experimental.pallas import tpu as pltpu
from jax.sharding import PartitionSpec as P

DH = 128
CONV = 4
EPS = 1e-06
SCALE = DH ** (-0.5)
RADIX = 4
PACK = 2 * DH + 16
F32 = jnp.float32
BF16 = jnp.bfloat16


def bf(value):
    return value.astype(BF16)


def dot(left, right, dims=(1, 0)):
    return lax.dot_general(
        bf(left), bf(right), (((dims[0],), (dims[1],)), ((), ())), preferred_element_type=F32
    )


def halves(value):
    high = bf(value)
    return high, bf(value - high.astype(F32))


def dot3(left, right, dims=(1, 0)):
    left_high, left_low = halves(left)
    right_high, right_low = halves(right)
    return dot(left_high, right_high, dims) + (
        dot(left_high, right_low, dims) + dot(left_low, right_high, dims)
    )


def dot_exact(left, right):
    return lax.dot_general(
        left, right, (((1,), (0,)), ((), ())),
        precision=lax.Precision.HIGHEST, preferred_element_type=F32,
    )


def positions(shape=(DH, DH)):
    return lax.broadcasted_iota(jnp.int32, shape, 0), lax.broadcasted_iota(jnp.int32, shape, 1)


def sigmoid(value):
    return 1.0 / (1.0 + jnp.exp(-value))


def softplus(value):
    return jnp.maximum(value, 0.0) + jnp.log1p(jnp.exp(-jnp.abs(value)))


def lanes_of(pieces):
    _, lane = positions()
    result = jnp.zeros((DH, DH), F32)
    for place, piece in enumerate(pieces):
        result = jnp.where(lane == place, piece, result)
    return result


def unit_lower_inverses(stricts):
    row, col = positions()
    identity = jnp.where(row == col, 1.0, 0.0).astype(F32)
    inners = [jnp.where(row // 8 == col // 8, strict, 0.0) for strict in stricts]
    squares = [dot3(inner, inner) for inner in inners]
    results = [dot3(identity - inner, identity + square) for inner, square in zip(inners, squares)]
    fourths = [dot3(square, square) for square in squares]
    results = [dot3(result, identity + fourth) for result, fourth in zip(results, fourths)]
    size = 8
    while size < DH:
        off = (row // (2 * size) == col // (2 * size)) & (row // size != col // size)
        products = [
            dot3(result, jnp.where(off, strict, 0.0)) for result, strict in zip(results, stricts)
        ]
        results = [
            result - dot3(product, result) for result, product in zip(results, products)
        ]
        size *= 2
    return results


def project_kernel(
    x_ref, wq_ref, wk_ref, wv_ref, wb_ref, wa_ref, fq_ref, fk_ref, fv_ref, decay_ref, bias_ref,
    proj_ref, ba_ref, tail_ref, taps_ref, scales_ref, held_ref, narrow_ref, filter_ref, pair_ref,
    sems,
):
    parts, _, width = x_ref.shape
    places = (slice(0, DH), slice(DH, 2 * DH), slice(2 * DH, 4 * DH))
    copies = []

    def fetch(source, target):
        copies.append(pltpu.make_async_copy(source, target, sems.at[len(copies)]))
        copies[-1].start()

    for part in range(parts):
        span = slice(part * width, (part + 1) * width)
        for place, weight in zip(places, (wq_ref, wk_ref, wv_ref)):
            fetch(weight.at[span, :], held_ref.at[span, place])
    fetch(wb_ref, narrow_ref.at[0])
    fetch(wa_ref, narrow_ref.at[1])
    for place, taps in zip(places, (fq_ref, fk_ref, fv_ref)):
        fetch(taps, filter_ref.at[:, place])
    fetch(decay_ref, pair_ref.at[0])
    fetch(bias_ref, pair_ref.at[1])
    total = jnp.zeros((DH, 4 * DH), F32)
    for part in range(parts):
        span = slice(part * width, (part + 1) * width)
        for copy in copies[3 * part : 3 * part + 3]:
            copy.wait()
        total = total + dot(x_ref[part], held_ref[span, :])
    for copy in copies[3 * parts :]:
        copy.wait()
    beta = jnp.zeros((DH, 2), F32)
    alpha = jnp.zeros((DH, 2), F32)
    for part in range(parts):
        span = slice(part * width, (part + 1) * width)
        beta = beta + dot(x_ref[part], narrow_ref[0, :, span], (1, 1))
        alpha = alpha + dot(x_ref[part], narrow_ref[1, :, span], (1, 1))
    proj_ref[...] = bf(total)
    tail_ref[...] = bf(total[DH - 16 :])
    ba_ref[...] = bf(lanes_of([beta[:, 0:1], beta[:, 1:2], alpha[:, 0:1], alpha[:, 1:2]]))
    taps_ref[0:CONV] = filter_ref[...].astype(F32)
    taps_ref[CONV:] = jnp.zeros((8 - CONV, 4 * DH), F32)
    decay = pair_ref[0]
    bias = pair_ref[1]
    scales_ref[0] = lanes_of([0.0, 0.0, -jnp.exp(decay[:, 0:1]), -jnp.exp(decay[:, 1:2])])
    scales_ref[1] = lanes_of([0.0, 0.0, bias[:, 0:1], bias[:, 1:2]])


def split_decay(value):
    high = bf(value).astype(F32)
    middle = bf(value - high).astype(F32)
    low = value - high - middle
    row = lax.broadcasted_iota(jnp.int32, (16, DH), 0)
    return bf(jnp.where(row == 0, high, jnp.where(row == 1, middle, jnp.where(row == 2, low, 0.0))))


def gate_kernel(ba_ref, scales_ref, cols_ref, gap_ref):
    row, col = positions()
    raw = ba_ref[...].astype(F32)
    log_decay = scales_ref[0] * softplus(raw + scales_ref[1])
    lower = jnp.where(row >= col, 1.0, 0.0).astype(F32)
    cols = jnp.where(col < 2, sigmoid(raw), dot_exact(lower, log_decay))
    cols_ref[...] = cols
    rows = cols.T
    for head in range(2):
        between = cols[:, 2 + head : 3 + head] - rows[2 + head : 3 + head, :]
        gap_ref[head] = jnp.where(row >= col, jnp.exp(jnp.where(row >= col, between, 0.0)), 0.0)


def slab_kernel(
    proj_ref, tail_ref, taps_ref, cols_ref, gap_ref, grad_ref,
    send_ref, pre_ref, unit_ref, inverse_ref, mixed_ref, weighted_ref,
    back_ref, gram_ref, cross_ref, pad_ref,
):
    row, col = positions()
    pad_ref[0:8] = tail_ref[8:16].astype(F32)
    pad_ref[8 : 8 + DH] = proj_ref[...].astype(F32)
    pre = jnp.zeros((DH, 4 * DH), F32)
    for tap in range(CONV):
        start = 8 - (CONV - 1) + tap
        pre = pre + taps_ref[tap : tap + 1] * pad_ref[start : start + DH]
    pre_ref[...] = pre
    act = pre * sigmoid(pre)
    query_act, key_act = act[:, :DH], act[:, DH : 2 * DH]
    query = query_act * (lax.rsqrt(jnp.sum(query_act * query_act, 1, keepdims=True) + EPS) * SCALE)
    key = key_act * lax.rsqrt(jnp.sum(key_act * key_act, 1, keepdims=True) + EPS)
    unit_ref[0] = query
    unit_ref[1] = key
    cols = cols_ref[...]
    gram = dot3(key, key, (1, 1))
    cross = dot3(query, key, (1, 1))
    gram_ref[...] = gram
    cross_ref[...] = cross
    betas = [cols[:, head : head + 1] for head in range(2)]
    inverses = unit_lower_inverses(
        [
            jnp.where(row > col, beta * gram * gap_ref[head], 0.0)
            for head, beta in enumerate(betas)
        ]
    )
    for head in range(2):
        beta = betas[head]
        inverse = inverses[head]
        cum = cols[:, 2 + head : 3 + head]
        value = act[:, (2 + head) * DH : (3 + head) * DH]
        grad = grad_ref[:, head * DH : (head + 1) * DH]
        gamma = jnp.exp(cum)
        last = cum[DH - 1 : DH, :]
        key_tail = jnp.exp(last - cum) * key
        both = dot3(inverse, jnp.concatenate([beta * value, (beta * gamma) * key], axis=1))
        mixed = both[:, :DH]
        weighted = both[:, DH:]
        back = dot(cross * gap_ref[head], grad, (0, 0))
        inverse_ref[head] = bf(inverse)
        mixed_ref[head] = mixed
        weighted_ref[head] = bf(weighted)
        back_ref[head] = back
        ahead = dot(key_tail, both, (0, 0))
        moved = ahead[:, DH:]
        decay_rows = split_decay(jnp.exp(last))
        send_ref[2 * head, 0:DH] = bf(moved)
        send_ref[2 * head, DH : 2 * DH] = bf(ahead[:, :DH])
        send_ref[2 * head, 2 * DH :] = decay_rows
        send_ref[2 * head + 1, 0:DH] = bf(moved.T)
        send_ref[2 * head + 1, DH : 2 * DH] = bf(
            dot(gamma * query, grad, (0, 0)) - dot(weighted, back, (0, 0))
        )
        send_ref[2 * head + 1, 2 * DH :] = decay_rows


def unpack(ref):
    decay = ref[2 * DH :].astype(F32)
    return (
        decay[0:1, 0:1] + decay[1:2, 0:1] + decay[2:3, 0:1],
        ref[0:DH].astype(F32),
        ref[DH : 2 * DH].astype(F32),
    )


def apply_map(later, state):
    decay, matrix, offset = later
    return decay * state - dot(matrix, state) + offset


def compose(later, earlier):
    decay, matrix, offset = later
    return (
        decay * earlier[0],
        decay * earlier[1] + earlier[0] * matrix - dot(matrix, earlier[1]),
        apply_map(later, earlier[2]),
    )


def pack(total):
    decay, matrix, offset = total
    return jnp.concatenate([bf(matrix), bf(offset), split_decay(decay)], axis=0)


def is_backward():
    return lax.axis_index("ctx") % 2 == 1


def in_order(step, backward):
    return jnp.where(backward, RADIX - 1 - step, step)


def group_kernel(got_ref, total_ref):
    backward = is_backward()
    total = unpack(got_ref.at[in_order(0, backward)])
    for step in range(1, RADIX):
        total = compose(unpack(got_ref.at[in_order(step, backward)]), total)
    total_ref[...] = pack(total)


def window_kernel(total_ref, last_ref, middle_ref, first_ref, wider_ref, before_ref):
    before = compose(unpack(last_ref), compose(unpack(middle_ref), unpack(first_ref)))
    before_ref[0:DH] = before[1]
    before_ref[DH : 2 * DH] = before[2]
    before_ref[2 * DH :] = jnp.broadcast_to(before[0], (8, DH))
    wider = pack(compose(unpack(total_ref), before))
    for place in range(RADIX):
        wider_ref[place] = wider


def states_kernel(rows_ref, before_ref, group_ref, out_ref):
    backward = is_backward()
    place = in_order(lax.axis_index("ctx") // (RADIX * RADIX), backward)
    state = jnp.zeros((DH, DH), F32)
    for step in range(RADIX - 1):
        later = apply_map(unpack(rows_ref.at[in_order(step, backward)]), state)
        state = jnp.where(step < place, later, state)
    before = (before_ref[2 * DH : 2 * DH + 1, 0:1], before_ref[0:DH], before_ref[DH : 2 * DH])
    state = apply_map(before, state)
    for step in range(RADIX):
        spot = in_order(step, backward)
        out_ref[spot] = bf(state)
        if step < RADIX - 1:
            state = apply_map(unpack(group_ref.at[spot]), state)


def gradient_kernel(
    states_ref, pre_ref, unit_ref, cols_ref, ba_ref, inverse_ref, mixed_ref, weighted_ref,
    back_ref, gap_ref, gram_ref, cross_ref, grad_ref, taps_ref, scales_ref,
    full_ref, gates_ref, halo_ref, pad_ref,
):
    row, col = positions()
    cols = cols_ref[...]
    gram = gram_ref[...]
    cross = cross_ref[...]
    query = unit_ref[0]
    key = unit_ref[1]
    pre = pre_ref[...]
    gate = sigmoid(pre)
    act = pre * gate
    slope = gate * (1.0 + pre * (1.0 - gate))
    grad_query = jnp.zeros((DH, DH), F32)
    grad_key = jnp.zeros((DH, DH), F32)
    pieces = []
    columns = jnp.zeros((DH, DH), F32)
    sides = []
    for head in range(2):
        state = states_ref[2 * head]
        after = states_ref[2 * head + 1]
        beta = cols[:, head : head + 1]
        cum = cols[:, 2 + head : 3 + head]
        gamma = jnp.exp(cum)
        last = cum[DH - 1 : DH, :]
        rest = jnp.exp(last - cum)
        value = act[:, (2 + head) * DH : (3 + head) * DH]
        grad = grad_ref[:, head * DH : (head + 1) * DH]
        gap = gap_ref[head]
        fresh = mixed_ref[head] - dot(weighted_ref[head], state)
        grad_fresh = back_ref[head] + dot(rest * key, after)
        solved = dot(inverse_ref[head], grad_fresh, (0, 0))
        grad_strict = jnp.where(row > col, -dot(solved, fresh, (1, 1)), 0.0) * gap
        grad_cross = dot(grad, fresh, (1, 1)) * gap
        grad_weighted = -dot(solved, state, (1, 1))
        grad_scaled = dot(grad, state, (1, 1))
        grad_tail = dot(fresh, after, (1, 1))
        grad_query = grad_query + gamma * grad_scaled + dot(grad_cross, key)
        grad_gram = beta * grad_strict
        grad_key = grad_key + (
            dot(grad_cross, query, (0, 0))
            + dot(grad_gram, key)
            + dot(grad_gram, key, (0, 0))
            + (beta * gamma) * grad_weighted
            + rest * grad_tail
        )
        pieces.append(beta * solved)
        by_beta = jnp.sum(grad_strict * gram, 1, keepdims=True)
        by_key = gamma * jnp.sum(grad_weighted * key, 1, keepdims=True)
        grad_beta = jnp.sum(solved * value, 1, keepdims=True) + by_key + by_beta
        by_gap = grad_gram * gram + grad_cross * cross
        by_tail = rest * jnp.sum(grad_tail * key, 1, keepdims=True)
        at_end = jnp.sum(by_tail, 0, keepdims=True) + jnp.exp(last) * jnp.sum(
            jnp.sum(state.astype(F32) * after.astype(F32), 1, keepdims=True), 0, keepdims=True
        )
        grad_cum = (
            jnp.sum(by_gap, 1, keepdims=True)
            + gamma * jnp.sum(grad_scaled * query, 1, keepdims=True)
            + beta * by_key
            - by_tail
            + jnp.where(row[:, 0:1] == DH - 1, at_end, 0.0)
        )
        columns = jnp.where(row == 2 + head, jnp.sum(by_gap, 0, keepdims=True), columns)
        sides.append((grad_beta, grad_cum))
    raw = ba_ref[...].astype(F32)
    rate = scales_ref[0]
    bias = scales_ref[1]
    sides = lanes_of([sides[0][0], sides[1][0], sides[0][1], sides[1][1]]) - columns.T
    upper = jnp.where(row <= col, 1.0, 0.0).astype(F32)
    grad_log = dot_exact(upper, sides)
    beta = cols
    gates_ref[...] = bf(
        jnp.where(
            col < 2,
            sides * beta * (1.0 - beta),
            jnp.where(col < 4, grad_log * rate * sigmoid(raw + bias), 0.0),
        )
    )
    key_act = act[:, DH : 2 * DH]
    query_act = act[:, :DH]
    query_size = lax.rsqrt(jnp.sum(query_act * query_act, 1, keepdims=True) + EPS)
    key_size = lax.rsqrt(jnp.sum(key_act * key_act, 1, keepdims=True) + EPS)
    query_dir = query_act * query_size
    grad_query = grad_query * SCALE
    grad_query = query_size * (
        grad_query - query_dir * jnp.sum(grad_query * query_dir, 1, keepdims=True)
    )
    grad_key = key_size * (grad_key - key * jnp.sum(grad_key * key, 1, keepdims=True))
    pad_ref[0:8] = jnp.zeros((8, 4 * DH), F32)
    pad_ref[8 + DH :] = jnp.zeros((8, 4 * DH), F32)
    for place, piece in enumerate([grad_query, grad_key] + pieces):
        span = slice(place * DH, (place + 1) * DH)
        pad_ref[8 : 8 + DH, span] = piece * slope[:, span]
    total = jnp.zeros((8 + DH, 4 * DH), F32)
    for tap in range(CONV):
        start = CONV - 1 - tap
        total = total + taps_ref[tap : tap + 1] * pad_ref[start : start + 8 + DH]
    halo_ref[...] = total[0:8]
    full_ref[...] = total[8:]


def spread_kernel(full_ref, halo_ref, gates_ref, wq_ref, wk_ref, wv_ref, wb_ref, wa_ref, out_ref):
    full = full_ref[...]
    end = full[DH - 8 :] + halo_ref[...]
    grads = bf(jnp.concatenate([full[: DH - 8], end], axis=0))
    gates = gates_ref[...]
    width = out_ref.shape[2]
    for part in range(out_ref.shape[0]):
        span = slice(part * width, (part + 1) * width)
        total = dot(grads[:, :DH], wq_ref[span, :], (1, 1))
        total = total + dot(grads[:, DH : 2 * DH], wk_ref[span, :], (1, 1))
        total = total + dot(grads[:, 2 * DH :], wv_ref[span, :], (1, 1))
        total = total + dot(gates[:, 0:2], wb_ref[:, span])
        total = total + dot(gates[:, 2:4], wa_ref[:, span])
        out_ref[part] = bf(total)


def call(kernel, outs, scratch=(), specs=None):
    extra = {} if specs is None else {"in_specs": specs}
    return pl.pallas_call(
        kernel,
        out_shape=[jax.ShapeDtypeStruct(shape, kind) for shape, kind in outs],
        scratch_shapes=list(scratch),
        compiler_params=pltpu.CompilerParams(vmem_limit_bytes=48 * 1024 * 1024),
        **extra,
    )


def stay(array):
    return pltpu.with_memory_space_constraint(array, pltpu.HBM)


def project(gathered, weights, filters, decay, bias):
    parts = gathered.shape[0]
    inside = pl.BlockSpec(memory_space=pltpu.VMEM)
    outside = pl.BlockSpec(memory_space=pltpu.HBM)
    model = weights[0].shape[0]
    return call(
        project_kernel,
        [
            ((DH, 4 * DH), BF16), ((DH, DH), BF16), ((16, 4 * DH), BF16), ((8, 4 * DH), F32),
            ((2, DH, DH), F32),
        ],
        [
            pltpu.VMEM((model, 4 * DH), BF16),
            pltpu.VMEM((2, 2, model), BF16),
            pltpu.VMEM((CONV, 4 * DH), BF16),
            pltpu.VMEM((2, 1, 2), F32),
            pltpu.SemaphoreType.DMA((3 * parts + 7,)),
        ],
        [inside] + [outside] * 10,
    )(gathered, *[stay(array) for array in (*weights, *filters, decay, bias)])


def slab(proj, tail, taps, cols, gap, grad):
    square = (DH, DH)
    return call(
        slab_kernel,
        [
            ((4, PACK, DH), BF16), ((DH, 4 * DH), F32), ((2,) + square, F32),
            ((2,) + square, BF16), ((2,) + square, F32), ((2,) + square, BF16),
            ((2,) + square, F32), (square, F32), (square, F32),
        ],
        [pltpu.VMEM((8 + DH, 4 * DH), F32)],
    )(proj, tail, taps, cols, gap, grad)


def gradient(states, kept, cols, gap, gates, taps, scales, grad):
    pre, unit, inverse, mixed, weighted, back, gram, cross = kept
    return call(
        gradient_kernel,
        [((DH, 4 * DH), F32), ((DH, DH), BF16), ((8, 4 * DH), F32)],
        [pltpu.VMEM((16 + DH, 4 * DH), F32)],
    )(
        states, pre, unit, cols, gates, inverse, mixed, weighted, back, gap, gram, cross,
        grad, taps, scales,
    )


def spread(full, halo, gates, weights, parts):
    width = weights[0].shape[0] // parts
    return call(spread_kernel, [((parts, DH, width), BF16)])(full, halo, gates, *weights)[0]


def local(
    inputs, query_weight, key_weight, value_weight, beta_weight, alpha_weight,
    query_filter, key_filter, value_filter, decay_log, step_bias, grad_core,
):
    weights = (query_weight, key_weight, value_weight, beta_weight.T, alpha_weight.T)
    filters = (query_filter, key_filter, value_filter)
    decay = decay_log.reshape(1, 2)
    bias = step_bias.reshape(1, 2)
    count = lax.axis_size("ctx")
    parts = lax.axis_size("tp")
    slabs = range(count)
    group = [[s for s in slabs if s // RADIX == g] for g in range(count // RADIX)]
    rank = [[s for s in slabs if s % 16 == z] for z in range(16)]

    def exchange(value, groups):
        return lax.all_to_all(value, "ctx", 0, 0, axis_index_groups=groups)

    def onward(value, distance):
        steps = [(s, s - distance if s % 2 else s + distance) for s in slabs]
        return lax.ppermute(value, "ctx", [(s, t) for s, t in steps if 0 <= t < count])

    gathered = lax.all_gather(inputs, "tp", axis=0)
    proj, gates, tail, taps, scales = project(gathered, weights, filters, decay, bias)
    tail = lax.ppermute(tail, "ctx", [(s, s + 1) for s in range(count - 1)])
    square = (DH, DH)
    cols, gap = call(gate_kernel, [(square, F32), ((2,) + square, F32)])(gates, scales)
    send, *kept = slab(proj, tail, taps, cols, gap, grad_core)
    got = exchange(send, group)
    total = call(group_kernel, [((PACK, DH), BF16)])(got)[0]
    earlier = [onward(total, RADIX * step) for step in range(1, RADIX)]
    total, before = call(
        window_kernel, [((RADIX, PACK, DH), BF16), ((2 * DH + 8, DH), F32)]
    )(total, *earlier)
    states = call(states_kernel, [((RADIX, DH, DH), BF16)])(exchange(total, rank), before, got)[0]
    states = exchange(states, group)
    full, grad_gates, halo = gradient(
        states, kept, cols, gap, gates, taps, scales, grad_core
    )
    halo = lax.ppermute(halo, "ctx", [(s + 1, s) for s in range(count - 1)])
    shares = spread(full, halo, grad_gates, weights, parts)
    shares = lax.all_to_all(shares, "tp", 0, 0)
    return jnp.sum(shares.astype(F32), axis=0).astype(BF16)


def solution(mesh):
    sharded = P("ctx", "tp")
    kept = P(None, "tp")
    return jax.shard_map(
        local,
        mesh=mesh,
        in_specs=(sharded,) + (kept,) * 8 + (P("tp"), P("tp"), sharded),
        out_specs=sharded,
        check_vma=False,
    )
```

```python
import functools

import jax
import jax.numpy as jnp
from jax import lax
from jax.experimental import pallas as pl
from jax.experimental.pallas import tpu as pltpu
from jax.sharding import PartitionSpec as P

DH = 128
CONV = 4
EPS = 1e-06
SCALE = DH ** (-0.5)
RADIX = 4
PACK = 2 * DH + 16
F32 = jnp.float32
BF16 = jnp.bfloat16


def bf(value):
    return value.astype(BF16)


def dot(left, right, dims=(1, 0)):
    return lax.dot_general(
        bf(left), bf(right), (((dims[0],), (dims[1],)), ((), ())), preferred_element_type=F32
    )


def halves(value):
    high = bf(value)
    return high, bf(value - high.astype(F32))


def dot3(left, right, dims=(1, 0)):
    left_high, left_low = halves(left)
    right_high, right_low = halves(right)
    return dot(left_high, right_high, dims) + (
        dot(left_high, right_low, dims) + dot(left_low, right_high, dims)
    )


def dot_exact(left, right):
    return lax.dot_general(
        left, right, (((1,), (0,)), ((), ())),
        precision=lax.Precision.HIGHEST, preferred_element_type=F32,
    )


def positions(shape=(DH, DH)):
    return lax.broadcasted_iota(jnp.int32, shape, 0), lax.broadcasted_iota(jnp.int32, shape, 1)


def sigmoid(value):
    return 1.0 / (1.0 + jnp.exp(-value))


def softplus(value):
    return jnp.maximum(value, 0.0) + jnp.log1p(jnp.exp(-jnp.abs(value)))


def lanes_of(pieces):
    _, lane = positions()
    result = jnp.zeros((DH, DH), F32)
    for place, piece in enumerate(pieces):
        result = jnp.where(lane == place, piece, result)
    return result


def unit_lower_inverses(stricts):
    row, col = positions()
    identity = jnp.where(row == col, 1.0, 0.0).astype(F32)
    inners = [jnp.where(row // 8 == col // 8, strict, 0.0) for strict in stricts]
    squares = [dot3(inner, inner) for inner in inners]
    results = [dot3(identity - inner, identity + square) for inner, square in zip(inners, squares)]
    fourths = [dot3(square, square) for square in squares]
    results = [dot3(result, identity + fourth) for result, fourth in zip(results, fourths)]
    size = 8
    while size < DH:
        off = (row // (2 * size) == col // (2 * size)) & (row // size != col // size)
        products = [
            dot3(result, jnp.where(off, strict, 0.0)) for result, strict in zip(results, stricts)
        ]
        results = [
            result - dot3(product, result) for result, product in zip(results, products)
        ]
        size *= 2
    return results


def core_place():
    return lax.axis_index("tp") % 2


def part_span(part, core, width):
    return pl.ds(pl.multiple_of((2 * part + core) * width, width), width)


def narrow_sums(x_ref, narrow_ref, core):
    parts, _, width = x_ref.shape
    beta = jnp.zeros((DH, 2), F32)
    alpha = jnp.zeros((DH, 2), F32)
    for part in range(parts):
        span = part_span(part, core, width)
        beta = beta + dot(x_ref[part], narrow_ref[0, :, span], (1, 1))
        alpha = alpha + dot(x_ref[part], narrow_ref[1, :, span], (1, 1))
    return lanes_of([beta[:, 0:1], beta[:, 1:2], alpha[:, 0:1], alpha[:, 1:2]])


def first_project_kernel(
    x_ref, wq_ref, wk_ref, wv_ref, wb_ref, wa_ref, fq_ref, fk_ref, fv_ref, decay_ref, bias_ref,
    total_ref, gates_ref, taps_ref, scales_ref, rest_ref, narrow_ref,
    held_ref, filter_ref, pair_ref, sems,
):
    core = core_place()
    places = (slice(0, DH), slice(DH, 2 * DH), slice(2 * DH, 4 * DH))
    copies = []

    def fetch(source, target):
        copies.append(pltpu.make_async_copy(source, target, sems.at[len(copies)]))
        copies[-1].start()

    for place, weight in zip(places, (wq_ref, wk_ref, wv_ref)):
        fetch(weight.at[:, core], held_ref.at[:, :, place])
    fetch(wb_ref, narrow_ref.at[0])
    fetch(wa_ref, narrow_ref.at[1])
    for place, taps in zip(places, (fq_ref, fk_ref, fv_ref)):
        fetch(taps, filter_ref.at[:, place])
    fetch(decay_ref, pair_ref.at[0])
    fetch(bias_ref, pair_ref.at[1])
    ready = len(copies)
    for place, weight in zip(places, (wq_ref, wk_ref, wv_ref)):
        fetch(weight.at[:, 1 - core], rest_ref.at[:, :, place])
    for copy in copies[:ready]:
        copy.wait()
    total = jnp.zeros((DH, 4 * DH), F32)
    for part in range(x_ref.shape[0]):
        total = total + dot(x_ref[part], held_ref[part])
    total_ref[...] = total
    gates_ref[...] = narrow_sums(x_ref, narrow_ref, core)
    taps_ref[0:CONV] = filter_ref[...].astype(F32)
    taps_ref[CONV:] = jnp.zeros((8 - CONV, 4 * DH), F32)
    decay = pair_ref[0]
    bias = pair_ref[1]
    scales_ref[0] = lanes_of([0.0, 0.0, -jnp.exp(decay[:, 0:1]), -jnp.exp(decay[:, 1:2])])
    scales_ref[1] = lanes_of([0.0, 0.0, bias[:, 0:1], bias[:, 1:2]])
    for copy in copies[ready:]:
        copy.wait()


def second_project_kernel(
    x_ref, total_ref, part_ref, rest_ref, narrow_ref, proj_ref, ba_ref, tail_ref
):
    total = total_ref[...]
    for part in range(x_ref.shape[0]):
        total = total + dot(x_ref[part], rest_ref[part])
    proj_ref[...] = bf(total)
    tail_ref[...] = bf(total[DH - 16 :])
    ba_ref[...] = bf(part_ref[...] + narrow_sums(x_ref, narrow_ref, 1 - core_place()))


def split_decay(value):
    high = bf(value).astype(F32)
    middle = bf(value - high).astype(F32)
    low = value - high - middle
    row = lax.broadcasted_iota(jnp.int32, (16, DH), 0)
    return bf(jnp.where(row == 0, high, jnp.where(row == 1, middle, jnp.where(row == 2, low, 0.0))))


def gate_kernel(ba_ref, scales_ref, cols_ref, gap_ref):
    row, col = positions()
    raw = ba_ref[...].astype(F32)
    log_decay = scales_ref[0] * softplus(raw + scales_ref[1])
    lower = jnp.where(row >= col, 1.0, 0.0).astype(F32)
    cols = jnp.where(col < 2, sigmoid(raw), dot_exact(lower, log_decay))
    cols_ref[...] = cols
    rows = cols.T
    for head in range(2):
        between = cols[:, 2 + head : 3 + head] - rows[2 + head : 3 + head, :]
        gap_ref[head] = jnp.where(row >= col, jnp.exp(jnp.where(row >= col, between, 0.0)), 0.0)


def slab_kernel(
    proj_ref, tail_ref, taps_ref, cols_ref, gap_ref, grad_ref,
    send_ref, pre_ref, unit_ref, inverse_ref, mixed_ref, weighted_ref,
    back_ref, gram_ref, cross_ref, pad_ref,
):
    row, col = positions()
    pad_ref[0:8] = tail_ref[8:16].astype(F32)
    pad_ref[8 : 8 + DH] = proj_ref[...].astype(F32)
    pre = jnp.zeros((DH, 4 * DH), F32)
    for tap in range(CONV):
        start = 8 - (CONV - 1) + tap
        pre = pre + taps_ref[tap : tap + 1] * pad_ref[start : start + DH]
    pre_ref[...] = pre
    act = pre * sigmoid(pre)
    query_act, key_act = act[:, :DH], act[:, DH : 2 * DH]
    query = query_act * (lax.rsqrt(jnp.sum(query_act * query_act, 1, keepdims=True) + EPS) * SCALE)
    key = key_act * lax.rsqrt(jnp.sum(key_act * key_act, 1, keepdims=True) + EPS)
    unit_ref[0] = query
    unit_ref[1] = key
    cols = cols_ref[...]
    gram = dot3(key, key, (1, 1))
    cross = dot3(query, key, (1, 1))
    gram_ref[...] = gram
    cross_ref[...] = cross
    betas = [cols[:, head : head + 1] for head in range(2)]
    inverses = unit_lower_inverses(
        [
            jnp.where(row > col, beta * gram * gap_ref[head], 0.0)
            for head, beta in enumerate(betas)
        ]
    )
    for head in range(2):
        beta = betas[head]
        inverse = inverses[head]
        cum = cols[:, 2 + head : 3 + head]
        value = act[:, (2 + head) * DH : (3 + head) * DH]
        grad = grad_ref[:, head * DH : (head + 1) * DH]
        gamma = jnp.exp(cum)
        last = cum[DH - 1 : DH, :]
        key_tail = jnp.exp(last - cum) * key
        both = dot3(inverse, jnp.concatenate([beta * value, (beta * gamma) * key], axis=1))
        mixed = both[:, :DH]
        weighted = both[:, DH:]
        back = dot(cross * gap_ref[head], grad, (0, 0))
        inverse_ref[head] = bf(inverse)
        mixed_ref[head] = mixed
        weighted_ref[head] = bf(weighted)
        back_ref[head] = back
        ahead = dot(key_tail, both, (0, 0))
        moved = ahead[:, DH:]
        decay_rows = split_decay(jnp.exp(last))
        send_ref[2 * head, 0:DH] = bf(moved)
        send_ref[2 * head, DH : 2 * DH] = bf(ahead[:, :DH])
        send_ref[2 * head, 2 * DH :] = decay_rows
        send_ref[2 * head + 1, 0:DH] = bf(moved.T)
        send_ref[2 * head + 1, DH : 2 * DH] = bf(
            dot(gamma * query, grad, (0, 0)) - dot(weighted, back, (0, 0))
        )
        send_ref[2 * head + 1, 2 * DH :] = decay_rows


def unpack(ref):
    decay = ref[2 * DH :].astype(F32)
    return (
        decay[0:1, 0:1] + decay[1:2, 0:1] + decay[2:3, 0:1],
        ref[0:DH].astype(F32),
        ref[DH : 2 * DH].astype(F32),
    )


def apply_map(later, state):
    decay, matrix, offset = later
    return decay * state - dot(matrix, state) + offset


def compose(later, earlier):
    decay, matrix, offset = later
    return (
        decay * earlier[0],
        decay * earlier[1] + earlier[0] * matrix - dot(matrix, earlier[1]),
        apply_map(later, earlier[2]),
    )


def pack(total):
    decay, matrix, offset = total
    return jnp.concatenate([bf(matrix), bf(offset), split_decay(decay)], axis=0)


def is_backward():
    return lax.axis_index("ctx") % 2 == 1


def in_order(step, backward):
    return jnp.where(backward, RADIX - 1 - step, step)


def group_kernel(got_ref, total_ref):
    backward = is_backward()
    total = unpack(got_ref.at[in_order(0, backward)])
    for step in range(1, RADIX):
        total = compose(unpack(got_ref.at[in_order(step, backward)]), total)
    total_ref[...] = pack(total)


def window_kernel(total_ref, last_ref, middle_ref, first_ref, wider_ref, before_ref):
    before = compose(unpack(last_ref), compose(unpack(middle_ref), unpack(first_ref)))
    before_ref[0:DH] = before[1]
    before_ref[DH : 2 * DH] = before[2]
    before_ref[2 * DH :] = jnp.broadcast_to(before[0], (8, DH))
    wider = pack(compose(unpack(total_ref), before))
    for place in range(RADIX):
        wider_ref[place] = wider


def states_kernel(rows_ref, before_ref, group_ref, out_ref):
    backward = is_backward()
    place = in_order(lax.axis_index("ctx") // (RADIX * RADIX), backward)
    state = jnp.zeros((DH, DH), F32)
    for step in range(RADIX - 1):
        later = apply_map(unpack(rows_ref.at[in_order(step, backward)]), state)
        state = jnp.where(step < place, later, state)
    before = (before_ref[2 * DH : 2 * DH + 1, 0:1], before_ref[0:DH], before_ref[DH : 2 * DH])
    state = apply_map(before, state)
    for step in range(RADIX):
        spot = in_order(step, backward)
        out_ref[spot] = bf(state)
        if step < RADIX - 1:
            state = apply_map(unpack(group_ref.at[spot]), state)


def gradient_kernel(
    states_ref, pre_ref, unit_ref, cols_ref, ba_ref, inverse_ref, mixed_ref, weighted_ref,
    back_ref, gap_ref, gram_ref, cross_ref, grad_ref, taps_ref, scales_ref,
    full_ref, gates_ref, halo_ref, pad_ref,
):
    row, col = positions()
    cols = cols_ref[...]
    gram = gram_ref[...]
    cross = cross_ref[...]
    query = unit_ref[0]
    key = unit_ref[1]
    pre = pre_ref[...]
    gate = sigmoid(pre)
    act = pre * gate
    slope = gate * (1.0 + pre * (1.0 - gate))
    grad_query = jnp.zeros((DH, DH), F32)
    grad_key = jnp.zeros((DH, DH), F32)
    pieces = []
    columns = jnp.zeros((DH, DH), F32)
    sides = []
    for head in range(2):
        state = states_ref[2 * head]
        after = states_ref[2 * head + 1]
        beta = cols[:, head : head + 1]
        cum = cols[:, 2 + head : 3 + head]
        gamma = jnp.exp(cum)
        last = cum[DH - 1 : DH, :]
        rest = jnp.exp(last - cum)
        value = act[:, (2 + head) * DH : (3 + head) * DH]
        grad = grad_ref[:, head * DH : (head + 1) * DH]
        gap = gap_ref[head]
        fresh = mixed_ref[head] - dot(weighted_ref[head], state)
        grad_fresh = back_ref[head] + dot(rest * key, after)
        solved = dot(inverse_ref[head], grad_fresh, (0, 0))
        grad_strict = jnp.where(row > col, -dot(solved, fresh, (1, 1)), 0.0) * gap
        grad_cross = dot(grad, fresh, (1, 1)) * gap
        grad_weighted = -dot(solved, state, (1, 1))
        grad_scaled = dot(grad, state, (1, 1))
        grad_tail = dot(fresh, after, (1, 1))
        grad_query = grad_query + gamma * grad_scaled + dot(grad_cross, key)
        grad_gram = beta * grad_strict
        grad_key = grad_key + (
            dot(grad_cross, query, (0, 0))
            + dot(grad_gram, key)
            + dot(grad_gram, key, (0, 0))
            + (beta * gamma) * grad_weighted
            + rest * grad_tail
        )
        pieces.append(beta * solved)
        by_beta = jnp.sum(grad_strict * gram, 1, keepdims=True)
        by_key = gamma * jnp.sum(grad_weighted * key, 1, keepdims=True)
        grad_beta = jnp.sum(solved * value, 1, keepdims=True) + by_key + by_beta
        by_gap = grad_gram * gram + grad_cross * cross
        by_tail = rest * jnp.sum(grad_tail * key, 1, keepdims=True)
        at_end = jnp.sum(by_tail, 0, keepdims=True) + jnp.exp(last) * jnp.sum(
            jnp.sum(state.astype(F32) * after.astype(F32), 1, keepdims=True), 0, keepdims=True
        )
        grad_cum = (
            jnp.sum(by_gap, 1, keepdims=True)
            + gamma * jnp.sum(grad_scaled * query, 1, keepdims=True)
            + beta * by_key
            - by_tail
            + jnp.where(row[:, 0:1] == DH - 1, at_end, 0.0)
        )
        columns = jnp.where(row == 2 + head, jnp.sum(by_gap, 0, keepdims=True), columns)
        sides.append((grad_beta, grad_cum))
    raw = ba_ref[...].astype(F32)
    rate = scales_ref[0]
    bias = scales_ref[1]
    sides = lanes_of([sides[0][0], sides[1][0], sides[0][1], sides[1][1]]) - columns.T
    upper = jnp.where(row <= col, 1.0, 0.0).astype(F32)
    grad_log = dot_exact(upper, sides)
    beta = cols
    gates_ref[...] = bf(
        jnp.where(
            col < 2,
            sides * beta * (1.0 - beta),
            jnp.where(col < 4, grad_log * rate * sigmoid(raw + bias), 0.0),
        )
    )
    key_act = act[:, DH : 2 * DH]
    query_act = act[:, :DH]
    query_size = lax.rsqrt(jnp.sum(query_act * query_act, 1, keepdims=True) + EPS)
    key_size = lax.rsqrt(jnp.sum(key_act * key_act, 1, keepdims=True) + EPS)
    query_dir = query_act * query_size
    grad_query = grad_query * SCALE
    grad_query = query_size * (
        grad_query - query_dir * jnp.sum(grad_query * query_dir, 1, keepdims=True)
    )
    grad_key = key_size * (grad_key - key * jnp.sum(grad_key * key, 1, keepdims=True))
    pad_ref[0:8] = jnp.zeros((8, 4 * DH), F32)
    pad_ref[8 + DH :] = jnp.zeros((8, 4 * DH), F32)
    for place, piece in enumerate([grad_query, grad_key] + pieces):
        span = slice(place * DH, (place + 1) * DH)
        pad_ref[8 : 8 + DH, span] = piece * slope[:, span]
    total = jnp.zeros((8 + DH, 4 * DH), F32)
    for tap in range(CONV):
        start = CONV - 1 - tap
        total = total + taps_ref[tap : tap + 1] * pad_ref[start : start + 8 + DH]
    halo_ref[...] = total[0:8]
    full_ref[...] = total[8:]


def spread_kernel(
    other, full_ref, halo_ref, gates_ref, wq_ref, wk_ref, wv_ref, wb_ref, wa_ref, out_ref
):
    core = core_place()
    core = 1 - core if other else core
    full = full_ref[...]
    end = full[DH - 8 :] + halo_ref[...]
    grads = bf(jnp.concatenate([full[: DH - 8], end], axis=0))
    gates = gates_ref[...]
    parts, _, width = out_ref.shape
    for part in range(parts):
        span = part_span(part, core, width)
        total = dot(grads[:, :DH], wq_ref[span, :], (1, 1))
        total = total + dot(grads[:, DH : 2 * DH], wk_ref[span, :], (1, 1))
        total = total + dot(grads[:, 2 * DH :], wv_ref[span, :], (1, 1))
        total = total + dot(gates[:, 0:2], wb_ref[:, span])
        total = total + dot(gates[:, 2:4], wa_ref[:, span])
        out_ref[part] = total.astype(out_ref.dtype)


def merge_kernel(kept_ref, got_ref, out_ref):
    out_ref[...] = bf(kept_ref[...] + got_ref[...].astype(F32))


def call(kernel, outs, scratch=(), specs=None):
    extra = {} if specs is None else {"in_specs": specs}
    return pl.pallas_call(
        kernel,
        out_shape=[jax.ShapeDtypeStruct(shape, kind) for shape, kind in outs],
        scratch_shapes=list(scratch),
        compiler_params=pltpu.CompilerParams(vmem_limit_bytes=48 * 1024 * 1024),
        **extra,
    )


def stay(array):
    return pltpu.with_memory_space_constraint(array, pltpu.HBM)


def first_project(mine, weights, filters, decay, bias):
    parts, rows, width = mine.shape
    inside = pl.BlockSpec(memory_space=pltpu.VMEM)
    outside = pl.BlockSpec(memory_space=pltpu.HBM)
    model = 2 * parts * width
    wide = [weight.reshape(parts, 2, width, weight.shape[1]) for weight in weights[:3]]
    return call(
        first_project_kernel,
        [
            ((rows, 4 * DH), F32), ((DH, DH), F32), ((8, 4 * DH), F32), ((2, DH, DH), F32),
            ((parts, width, 4 * DH), BF16), ((2, 2, model), BF16),
        ],
        [
            pltpu.VMEM((parts, width, 4 * DH), BF16),
            pltpu.VMEM((CONV, 4 * DH), BF16),
            pltpu.VMEM((2, 1, 2), F32),
            pltpu.SemaphoreType.DMA((13,)),
        ],
        [inside] + [outside] * 10,
    )(mine, *[stay(array) for array in (*wide, *weights[3:], *filters, decay, bias)])


def second_project(other, total, part, rest, narrow):
    return call(
        second_project_kernel,
        [((DH, 4 * DH), BF16), ((DH, DH), BF16), ((16, 4 * DH), BF16)],
    )(other, total, part, rest, narrow)


def slab(proj, tail, taps, cols, gap, grad):
    square = (DH, DH)
    return call(
        slab_kernel,
        [
            ((4, PACK, DH), BF16), ((DH, 4 * DH), F32), ((2,) + square, F32),
            ((2,) + square, BF16), ((2,) + square, F32), ((2,) + square, BF16),
            ((2,) + square, F32), (square, F32), (square, F32),
        ],
        [pltpu.VMEM((8 + DH, 4 * DH), F32)],
    )(proj, tail, taps, cols, gap, grad)


def gradient(states, kept, cols, gap, gates, taps, scales, grad):
    pre, unit, inverse, mixed, weighted, back, gram, cross = kept
    return call(
        gradient_kernel,
        [((DH, 4 * DH), F32), ((DH, DH), BF16), ((8, 4 * DH), F32)],
        [pltpu.VMEM((16 + DH, 4 * DH), F32)],
    )(
        states, pre, unit, cols, gates, inverse, mixed, weighted, back, gap, gram, cross,
        grad, taps, scales,
    )


def spread(full, halo, gates, weights, parts, other):
    width = weights[0].shape[0] // (2 * parts)
    return call(
        functools.partial(spread_kernel, other),
        [((parts, DH, width), BF16 if other else F32)],
    )(full, halo, gates, *weights)[0]


def local(
    inputs, query_weight, key_weight, value_weight, beta_weight, alpha_weight,
    query_filter, key_filter, value_filter, decay_log, step_bias, grad_core,
):
    weights = (query_weight, key_weight, value_weight, beta_weight.T, alpha_weight.T)
    filters = (query_filter, key_filter, value_filter)
    decay = decay_log.reshape(1, 2)
    bias = step_bias.reshape(1, 2)
    count = lax.axis_size("ctx")
    parts = lax.axis_size("tp")
    slabs = range(count)
    group = [[s for s in slabs if s // RADIX == g] for g in range(count // RADIX)]
    rank = [[s for s in slabs if s % 16 == z] for z in range(16)]

    def exchange(value, groups):
        return lax.all_to_all(value, "ctx", 0, 0, axis_index_groups=groups)

    def onward(value, distance):
        steps = [(s, s - distance if s % 2 else s + distance) for s in slabs]
        return lax.ppermute(value, "ctx", [(s, t) for s, t in steps if 0 <= t < count])

    chips = [[2 * chip + core for chip in range(parts // 2)] for core in range(2)]

    def across(value):
        return lax.all_to_all(value, "tp", 0, 0, axis_index_groups=chips)

    def between(value):
        return lax.ppermute(value, "tp", [(t, t ^ 1) for t in range(parts)])

    mine = across(jnp.broadcast_to(inputs[None], (parts // 2,) + inputs.shape))
    other = between(mine)
    total, part, taps, scales, rest, narrow = first_project(mine, weights, filters, decay, bias)
    proj, gates, tail = second_project(other, total, part, rest, narrow)
    tail = lax.ppermute(tail, "ctx", [(s, s + 1) for s in range(count - 1)])
    square = (DH, DH)
    cols, gap = call(gate_kernel, [(square, F32), ((2,) + square, F32)])(gates, scales)
    send, *kept = slab(proj, tail, taps, cols, gap, grad_core)
    got = exchange(send, group)
    total = call(group_kernel, [((PACK, DH), BF16)])(got)[0]
    earlier = [onward(total, RADIX * step) for step in range(1, RADIX)]
    total, before = call(
        window_kernel, [((RADIX, PACK, DH), BF16), ((2 * DH + 8, DH), F32)]
    )(total, *earlier)
    states = call(states_kernel, [((RADIX, DH, DH), BF16)])(exchange(total, rank), before, got)[0]
    states = exchange(states, group)
    full, grad_gates, halo = gradient(
        states, kept, cols, gap, gates, taps, scales, grad_core
    )
    halo = lax.ppermute(halo, "ctx", [(s + 1, s) for s in range(count - 1)])
    given = between(spread(full, halo, grad_gates, weights, parts // 2, True))
    kept = spread(full, halo, grad_gates, weights, parts // 2, False)
    shares = call(merge_kernel, [(given.shape, BF16)])(kept, given)[0]
    return jnp.sum(across(shares).astype(F32), axis=0).astype(BF16)


def solution(mesh):
    sharded = P("ctx", "tp")
    kept = P(None, "tp")
    return jax.shard_map(
        local,
        mesh=mesh,
        in_specs=(sharded,) + (kept,) * 8 + (P("tp"), P("tp"), sharded),
        out_specs=sharded,
        check_vma=False,
    )
```

```python
import functools

import jax
import jax.numpy as jnp
from jax import lax
from jax.experimental import pallas as pl
from jax.experimental.pallas import tpu as pltpu
from jax.sharding import PartitionSpec as P

DH = 128
CONV = 4
EPS = 1e-06
SCALE = DH ** (-0.5)
RADIX = 4
PACK = 2 * DH
F32 = jnp.float32
BF16 = jnp.bfloat16


def bf(value):
    return value.astype(BF16)


def dot(left, right, dims=(1, 0)):
    return lax.dot_general(
        bf(left), bf(right), (((dims[0],), (dims[1],)), ((), ())), preferred_element_type=F32
    )


def halves(value):
    high = bf(value)
    return high, bf(value - high.astype(F32))


def dot3(left, right, dims=(1, 0)):
    left_high, left_low = halves(left)
    right_high, right_low = halves(right)
    return dot(left_high, right_high, dims) + (
        dot(left_high, right_low, dims) + dot(left_low, right_high, dims)
    )


def dot_exact(left, right):
    return lax.dot_general(
        left, right, (((1,), (0,)), ((), ())),
        precision=lax.Precision.HIGHEST, preferred_element_type=F32,
    )


def positions(shape=(DH, DH)):
    return lax.broadcasted_iota(jnp.int32, shape, 0), lax.broadcasted_iota(jnp.int32, shape, 1)


def sigmoid(value):
    return 1.0 / (1.0 + jnp.exp(-value))


def softplus(value):
    return jnp.maximum(value, 0.0) + jnp.log1p(jnp.exp(-jnp.abs(value)))


def lanes_of(pieces):
    _, lane = positions()
    result = jnp.zeros((DH, DH), F32)
    for place, piece in enumerate(pieces):
        result = jnp.where(lane == place, piece, result)
    return result


def unit_lower_inverses(stricts):
    row, col = positions()
    identity = jnp.where(row == col, 1.0, 0.0).astype(F32)
    inners = [jnp.where(row // 8 == col // 8, strict, 0.0) for strict in stricts]
    squares = [dot3(inner, inner) for inner in inners]
    results = [dot3(identity - inner, identity + square) for inner, square in zip(inners, squares)]
    fourths = [dot3(square, square) for square in squares]
    results = [dot3(result, identity + fourth) for result, fourth in zip(results, fourths)]
    size = 8
    while size < DH:
        off = (row // (2 * size) == col // (2 * size)) & (row // size != col // size)
        products = [
            dot3(result, jnp.where(off, strict, 0.0)) for result, strict in zip(results, stricts)
        ]
        results = [
            result - dot3(product, result) for result, product in zip(results, products)
        ]
        size *= 2
    return results


def core_place():
    return lax.axis_index("tp") % 2


def part_span(part, core, width):
    return pl.ds(pl.multiple_of((2 * part + core) * width, width), width)


def narrow_sums(x_ref, narrow_ref, core):
    parts, _, width = x_ref.shape
    beta = jnp.zeros((DH, 2), F32)
    alpha = jnp.zeros((DH, 2), F32)
    for part in range(parts):
        span = part_span(part, core, width)
        beta = beta + dot(x_ref[part], narrow_ref[0, :, span], (1, 1))
        alpha = alpha + dot(x_ref[part], narrow_ref[1, :, span], (1, 1))
    return lanes_of([beta[:, 0:1], beta[:, 1:2], alpha[:, 0:1], alpha[:, 1:2]])


def first_project_kernel(
    x_ref, wq_ref, wk_ref, wv_ref, wb_ref, wa_ref, fq_ref, fk_ref, fv_ref, decay_ref, bias_ref,
    total_ref, gates_ref, taps_ref, scales_ref, rest_ref, narrow_ref,
    held_ref, filter_ref, pair_ref, sems,
):
    core = core_place()
    places = (slice(0, DH), slice(DH, 2 * DH), slice(2 * DH, 4 * DH))
    copies = []

    def fetch(source, target):
        copies.append(pltpu.make_async_copy(source, target, sems.at[len(copies)]))
        copies[-1].start()

    for place, weight in zip(places, (wq_ref, wk_ref, wv_ref)):
        fetch(weight.at[:, core], held_ref.at[:, :, place])
    fetch(wb_ref, narrow_ref.at[0])
    fetch(wa_ref, narrow_ref.at[1])
    for place, taps in zip(places, (fq_ref, fk_ref, fv_ref)):
        fetch(taps, filter_ref.at[:, place])
    fetch(decay_ref, pair_ref.at[0])
    fetch(bias_ref, pair_ref.at[1])
    ready = len(copies)
    for place, weight in zip(places, (wq_ref, wk_ref, wv_ref)):
        fetch(weight.at[:, 1 - core], rest_ref.at[:, :, place])
    for copy in copies[:ready]:
        copy.wait()
    total = jnp.zeros((DH, 4 * DH), F32)
    for part in range(x_ref.shape[0]):
        total = total + dot(x_ref[part], held_ref[part])
    total_ref[...] = total
    gates_ref[...] = narrow_sums(x_ref, narrow_ref, core)
    taps_ref[0:CONV] = filter_ref[...].astype(F32)
    taps_ref[CONV:] = jnp.zeros((8 - CONV, 4 * DH), F32)
    decay = pair_ref[0]
    bias = pair_ref[1]
    scales_ref[0] = lanes_of([0.0, 0.0, -jnp.exp(decay[:, 0:1]), -jnp.exp(decay[:, 1:2])])
    scales_ref[1] = lanes_of([0.0, 0.0, bias[:, 0:1], bias[:, 1:2]])
    for copy in copies[ready:]:
        copy.wait()


def copies_kernel(x_ref, out_ref, sems):
    copies = [
        pltpu.make_async_copy(x_ref, out_ref.at[part], sems.at[part])
        for part in range(out_ref.shape[0])
    ]
    for copy in copies:
        copy.start()
    for copy in copies:
        copy.wait()


def second_project_kernel(
    x_ref, total_ref, part_ref, rest_ref, narrow_ref, proj_ref, ba_ref, tail_ref
):
    total = total_ref[...]
    for part in range(x_ref.shape[0]):
        total = total + dot(x_ref[part], rest_ref[part])
    proj_ref[...] = bf(total)
    tail_ref[...] = bf(total[DH - 16 :])
    ba_ref[...] = bf(part_ref[...] + narrow_sums(x_ref, narrow_ref, 1 - core_place()))


def gate_kernel(ba_ref, scales_ref, cols_ref, gap_ref):
    row, col = positions()
    raw = ba_ref[...].astype(F32)
    log_decay = scales_ref[0] * softplus(raw + scales_ref[1])
    lower = jnp.where(row >= col, 1.0, 0.0).astype(F32)
    cols = jnp.where(col < 2, sigmoid(raw), dot_exact(lower, log_decay))
    cols_ref[...] = cols
    rows = cols.T
    for head in range(2):
        between = cols[:, 2 + head : 3 + head] - rows[2 + head : 3 + head, :]
        gap_ref[head] = jnp.where(row >= col, jnp.exp(jnp.where(row >= col, between, 0.0)), 0.0)


def slab_kernel(
    proj_ref, tail_ref, taps_ref, cols_ref, gap_ref, grad_ref,
    send_ref, pre_ref, unit_ref, inverse_ref, mixed_ref, weighted_ref,
    back_ref, gram_ref, cross_ref, pad_ref,
):
    row, col = positions()
    pad_ref[0:8] = tail_ref[8:16].astype(F32)
    pad_ref[8 : 8 + DH] = proj_ref[...].astype(F32)
    pre = jnp.zeros((DH, 4 * DH), F32)
    for tap in range(CONV):
        start = 8 - (CONV - 1) + tap
        pre = pre + taps_ref[tap : tap + 1] * pad_ref[start : start + DH]
    pre_ref[...] = pre
    act = pre * sigmoid(pre)
    query_act, key_act = act[:, :DH], act[:, DH : 2 * DH]
    query = query_act * (lax.rsqrt(jnp.sum(query_act * query_act, 1, keepdims=True) + EPS) * SCALE)
    key = key_act * lax.rsqrt(jnp.sum(key_act * key_act, 1, keepdims=True) + EPS)
    unit_ref[0] = query
    unit_ref[1] = key
    cols = cols_ref[...]
    gram = dot3(key, key, (1, 1))
    cross = dot(query, key, (1, 1))
    gram_ref[...] = gram
    cross_ref[...] = cross
    betas = [cols[:, head : head + 1] for head in range(2)]
    inverses = unit_lower_inverses(
        [
            jnp.where(row > col, beta * gram * gap_ref[head], 0.0)
            for head, beta in enumerate(betas)
        ]
    )
    for head in range(2):
        beta = betas[head]
        inverse = inverses[head]
        cum = cols[:, 2 + head : 3 + head]
        value = act[:, (2 + head) * DH : (3 + head) * DH]
        grad = grad_ref[:, head * DH : (head + 1) * DH]
        gamma = jnp.exp(cum)
        last = cum[DH - 1 : DH, :]
        key_tail = jnp.exp(last - cum) * key
        both = dot3(inverse, jnp.concatenate([beta * value, (beta * gamma) * key], axis=1))
        mixed = both[:, :DH]
        weighted = both[:, DH:]
        back = dot(cross * gap_ref[head], grad, (0, 0))
        inverse_ref[head] = bf(inverse)
        mixed_ref[head] = mixed
        weighted_ref[head] = bf(weighted)
        back_ref[head] = back
        ahead = dot(key_tail, both, (0, 0))
        lost = jnp.where(row == col, 1.0 - jnp.exp(last), 0.0) + ahead[:, DH:]
        send_ref[2 * head, 0:DH] = bf(lost)
        send_ref[2 * head, DH:] = bf(ahead[:, :DH])
        send_ref[2 * head + 1, 0:DH] = bf(lost.T)
        send_ref[2 * head + 1, DH:] = bf(
            dot(gamma * query, grad, (0, 0)) - dot(weighted, back, (0, 0))
        )


def unpack(ref):
    return ref[0:DH], ref[DH:].astype(F32)


def dot_wide(matrix, value):
    high, low = halves(value)
    return dot(matrix, high) + dot(matrix, low)


def apply_map(later, state):
    matrix, offset = later
    return state - dot_wide(matrix, state) + offset


def compose(later, earlier):
    matrix, offset = later
    before = earlier[0].astype(F32)
    return (
        before + matrix.astype(F32) - dot_wide(matrix, before),
        apply_map(later, earlier[1]),
    )


def pack(total):
    return jnp.concatenate([bf(total[0]), bf(total[1])], axis=0)


def is_backward():
    return lax.axis_index("ctx") % 2 == 1


def in_order(step, backward):
    return jnp.where(backward, RADIX - 1 - step, step)


def group_kernel(got_ref, total_ref):
    backward = is_backward()
    total = unpack(got_ref.at[in_order(0, backward)])
    for step in range(1, RADIX):
        total = compose(unpack(got_ref.at[in_order(step, backward)]), total)
    total_ref[...] = pack(total)


def window_kernel(total_ref, last_ref, middle_ref, first_ref, wider_ref, before_ref):
    before = compose(unpack(last_ref), compose(unpack(middle_ref), unpack(first_ref)))
    before_ref[0:DH] = before[0]
    before_ref[DH:] = before[1]
    wider = pack(compose(unpack(total_ref), before))
    for place in range(RADIX):
        wider_ref[place] = wider


def states_kernel(rows_ref, before_ref, group_ref, out_ref):
    backward = is_backward()
    place = in_order(lax.axis_index("ctx") // (RADIX * RADIX), backward)
    state = jnp.zeros((DH, DH), F32)
    for step in range(RADIX - 1):
        later = apply_map(unpack(rows_ref.at[in_order(step, backward)]), state)
        state = jnp.where(step < place, later, state)
    state = apply_map((before_ref[0:DH], before_ref[DH:]), state)
    for step in range(RADIX):
        spot = in_order(step, backward)
        out_ref[spot] = bf(state)
        if step < RADIX - 1:
            state = apply_map(unpack(group_ref.at[spot]), state)


def gradient_kernel(
    states_ref, pre_ref, unit_ref, cols_ref, ba_ref, inverse_ref, mixed_ref, weighted_ref,
    back_ref, gap_ref, gram_ref, cross_ref, grad_ref, taps_ref, scales_ref,
    full_ref, gates_ref, halo_ref, pad_ref,
):
    row, col = positions()
    cols = cols_ref[...]
    gram = gram_ref[...]
    cross = cross_ref[...]
    query = unit_ref[0]
    key = unit_ref[1]
    pre = pre_ref[...]
    gate = sigmoid(pre)
    act = pre * gate
    slope = gate * (1.0 + pre * (1.0 - gate))
    grad_query = jnp.zeros((DH, DH), F32)
    grad_key = jnp.zeros((DH, DH), F32)
    pieces = []
    columns = jnp.zeros((DH, DH), F32)
    sides = []
    for head in range(2):
        state = states_ref[2 * head]
        after = states_ref[2 * head + 1]
        beta = cols[:, head : head + 1]
        cum = cols[:, 2 + head : 3 + head]
        gamma = jnp.exp(cum)
        last = cum[DH - 1 : DH, :]
        rest = jnp.exp(last - cum)
        value = act[:, (2 + head) * DH : (3 + head) * DH]
        grad = grad_ref[:, head * DH : (head + 1) * DH]
        gap = gap_ref[head]
        fresh = mixed_ref[head] - dot(weighted_ref[head], state)
        grad_fresh = back_ref[head] + dot(rest * key, after)
        solved = dot(inverse_ref[head], grad_fresh, (0, 0))
        grad_strict = jnp.where(row > col, -dot(solved, fresh, (1, 1)), 0.0) * gap
        grad_cross = dot(grad, fresh, (1, 1)) * gap
        grad_weighted = -dot(solved, state, (1, 1))
        grad_scaled = dot(grad, state, (1, 1))
        grad_tail = dot(fresh, after, (1, 1))
        grad_query = grad_query + gamma * grad_scaled + dot(grad_cross, key)
        grad_gram = beta * grad_strict
        grad_key = grad_key + (
            dot(grad_cross, query, (0, 0))
            + dot(grad_gram, key)
            + dot(grad_gram, key, (0, 0))
            + (beta * gamma) * grad_weighted
            + rest * grad_tail
        )
        pieces.append(beta * solved)
        by_beta = jnp.sum(grad_strict * gram, 1, keepdims=True)
        by_key = gamma * jnp.sum(grad_weighted * key, 1, keepdims=True)
        grad_beta = jnp.sum(solved * value, 1, keepdims=True) + by_key + by_beta
        by_gap = grad_gram * gram + grad_cross * cross
        by_tail = rest * jnp.sum(grad_tail * key, 1, keepdims=True)
        at_end = jnp.sum(by_tail, 0, keepdims=True) + jnp.exp(last) * jnp.sum(
            jnp.sum(state.astype(F32) * after.astype(F32), 1, keepdims=True), 0, keepdims=True
        )
        grad_cum = (
            jnp.sum(by_gap, 1, keepdims=True)
            + gamma * jnp.sum(grad_scaled * query, 1, keepdims=True)
            + beta * by_key
            - by_tail
            + jnp.where(row[:, 0:1] == DH - 1, at_end, 0.0)
        )
        columns = jnp.where(row == 2 + head, jnp.sum(by_gap, 0, keepdims=True), columns)
        sides.append((grad_beta, grad_cum))
    raw = ba_ref[...].astype(F32)
    rate = scales_ref[0]
    bias = scales_ref[1]
    sides = lanes_of([sides[0][0], sides[1][0], sides[0][1], sides[1][1]]) - columns.T
    upper = jnp.where(row <= col, 1.0, 0.0).astype(F32)
    grad_log = dot_exact(upper, sides)
    beta = cols
    gates_ref[...] = bf(
        jnp.where(
            col < 2,
            sides * beta * (1.0 - beta),
            jnp.where(col < 4, grad_log * rate * sigmoid(raw + bias), 0.0),
        )
    )
    key_act = act[:, DH : 2 * DH]
    query_act = act[:, :DH]
    query_size = lax.rsqrt(jnp.sum(query_act * query_act, 1, keepdims=True) + EPS)
    key_size = lax.rsqrt(jnp.sum(key_act * key_act, 1, keepdims=True) + EPS)
    query_dir = query_act * query_size
    grad_query = grad_query * SCALE
    grad_query = query_size * (
        grad_query - query_dir * jnp.sum(grad_query * query_dir, 1, keepdims=True)
    )
    grad_key = key_size * (grad_key - key * jnp.sum(grad_key * key, 1, keepdims=True))
    pad_ref[0:8] = jnp.zeros((8, 4 * DH), F32)
    pad_ref[8 + DH :] = jnp.zeros((8, 4 * DH), F32)
    for place, piece in enumerate([grad_query, grad_key] + pieces):
        span = slice(place * DH, (place + 1) * DH)
        pad_ref[8 : 8 + DH, span] = piece * slope[:, span]
    total = jnp.zeros((8 + DH, 4 * DH), F32)
    for tap in range(CONV):
        start = CONV - 1 - tap
        total = total + taps_ref[tap : tap + 1] * pad_ref[start : start + 8 + DH]
    halo_ref[...] = total[0:8]
    full_ref[...] = total[8:]


def spread_kernel(
    other, full_ref, halo_ref, gates_ref, wq_ref, wk_ref, wv_ref, wb_ref, wa_ref, out_ref
):
    core = core_place()
    core = 1 - core if other else core
    full = full_ref[...]
    end = full[DH - 8 :] + halo_ref[...]
    grads = bf(jnp.concatenate([full[: DH - 8], end], axis=0))
    gates = gates_ref[...]
    parts, _, width = out_ref.shape
    for part in range(parts):
        span = part_span(part, core, width)
        total = dot(grads[:, :DH], wq_ref[span, :], (1, 1))
        total = total + dot(grads[:, DH : 2 * DH], wk_ref[span, :], (1, 1))
        total = total + dot(grads[:, 2 * DH :], wv_ref[span, :], (1, 1))
        total = total + dot(gates[:, 0:2], wb_ref[:, span])
        total = total + dot(gates[:, 2:4], wa_ref[:, span])
        out_ref[part] = total.astype(out_ref.dtype)


def merge_kernel(kept_ref, got_ref, out_ref):
    out_ref[...] = bf(kept_ref[...] + got_ref[...].astype(F32))


def call(kernel, outs, scratch=(), specs=None):
    extra = {} if specs is None else {"in_specs": specs}
    return pl.pallas_call(
        kernel,
        out_shape=[jax.ShapeDtypeStruct(shape, kind) for shape, kind in outs],
        scratch_shapes=list(scratch),
        compiler_params=pltpu.CompilerParams(vmem_limit_bytes=48 * 1024 * 1024),
        **extra,
    )


def stay(array):
    return pltpu.with_memory_space_constraint(array, pltpu.HBM)


def first_project(mine, weights, filters, decay, bias):
    parts, rows, width = mine.shape
    inside = pl.BlockSpec(memory_space=pltpu.VMEM)
    outside = pl.BlockSpec(memory_space=pltpu.HBM)
    model = 2 * parts * width
    wide = [weight.reshape(parts, 2, width, weight.shape[1]) for weight in weights[:3]]
    return call(
        first_project_kernel,
        [
            ((rows, 4 * DH), F32), ((DH, DH), F32), ((8, 4 * DH), F32), ((2, DH, DH), F32),
            ((parts, width, 4 * DH), BF16), ((2, 2, model), BF16),
        ],
        [
            pltpu.VMEM((parts, width, 4 * DH), BF16),
            pltpu.VMEM((CONV, 4 * DH), BF16),
            pltpu.VMEM((2, 1, 2), F32),
            pltpu.SemaphoreType.DMA((13,)),
        ],
        [inside] + [outside] * 10,
    )(mine, *[stay(array) for array in (*wide, *weights[3:], *filters, decay, bias)])


def second_project(other, total, part, rest, narrow):
    return call(
        second_project_kernel,
        [((DH, 4 * DH), BF16), ((DH, DH), BF16), ((16, 4 * DH), BF16)],
    )(other, total, part, rest, narrow)


def slab(proj, tail, taps, cols, gap, grad):
    square = (DH, DH)
    return call(
        slab_kernel,
        [
            ((4, PACK, DH), BF16), ((DH, 4 * DH), F32), ((2,) + square, F32),
            ((2,) + square, BF16), ((2,) + square, F32), ((2,) + square, BF16),
            ((2,) + square, F32), (square, F32), (square, F32),
        ],
        [pltpu.VMEM((8 + DH, 4 * DH), F32)],
    )(proj, tail, taps, cols, gap, grad)


def gradient(states, kept, cols, gap, gates, taps, scales, grad):
    pre, unit, inverse, mixed, weighted, back, gram, cross = kept
    return call(
        gradient_kernel,
        [((DH, 4 * DH), F32), ((DH, DH), BF16), ((8, 4 * DH), F32)],
        [pltpu.VMEM((16 + DH, 4 * DH), F32)],
    )(
        states, pre, unit, cols, gates, inverse, mixed, weighted, back, gap, gram, cross,
        grad, taps, scales,
    )


def spread(full, halo, gates, weights, parts, other):
    width = weights[0].shape[0] // (2 * parts)
    return call(
        functools.partial(spread_kernel, other),
        [((parts, DH, width), BF16 if other else F32)],
    )(full, halo, gates, *weights)[0]


def local(
    inputs, query_weight, key_weight, value_weight, beta_weight, alpha_weight,
    query_filter, key_filter, value_filter, decay_log, step_bias, grad_core,
):
    weights = (query_weight, key_weight, value_weight, beta_weight.T, alpha_weight.T)
    filters = (query_filter, key_filter, value_filter)
    decay = decay_log.reshape(1, 2)
    bias = step_bias.reshape(1, 2)
    count = lax.axis_size("ctx")
    parts = lax.axis_size("tp")
    slabs = range(count)
    group = [[s for s in slabs if s // RADIX == g] for g in range(count // RADIX)]
    rank = [[s for s in slabs if s % 16 == z] for z in range(16)]

    def exchange(value, groups):
        return lax.all_to_all(value, "ctx", 0, 0, axis_index_groups=groups)

    def onward(value, distance):
        steps = [(s, s - distance if s % 2 else s + distance) for s in slabs]
        return lax.ppermute(value, "ctx", [(s, t) for s, t in steps if 0 <= t < count])

    chips = [[2 * chip + core for chip in range(parts // 2)] for core in range(2)]

    def across(value):
        return lax.all_to_all(value, "tp", 0, 0, axis_index_groups=chips)

    def between(value):
        return lax.ppermute(value, "tp", [(t, t ^ 1) for t in range(parts)])

    copies = call(
        copies_kernel,
        [((parts // 2,) + inputs.shape, BF16)],
        [pltpu.SemaphoreType.DMA((parts // 2,))],
        [pl.BlockSpec(memory_space=pltpu.HBM)],
    )(stay(inputs))[0]
    mine = across(copies)
    other = between(mine)
    total, part, taps, scales, rest, narrow = first_project(mine, weights, filters, decay, bias)
    proj, gates, tail = second_project(other, total, part, rest, narrow)
    tail = lax.ppermute(tail, "ctx", [(s, s + 1) for s in range(count - 1)])
    square = (DH, DH)
    cols, gap = call(gate_kernel, [(square, F32), ((2,) + square, F32)])(gates, scales)
    send, *kept = slab(proj, tail, taps, cols, gap, grad_core)
    got = exchange(send, group)
    total = call(group_kernel, [((PACK, DH), BF16)])(got)[0]
    earlier = [onward(total, RADIX * step) for step in range(1, RADIX)]
    total, before = call(
        window_kernel, [((RADIX, PACK, DH), BF16), ((PACK, DH), F32)]
    )(total, *earlier)
    states = call(states_kernel, [((RADIX, DH, DH), BF16)])(exchange(total, rank), before, got)[0]
    states = exchange(states, group)
    full, grad_gates, halo = gradient(
        states, kept, cols, gap, gates, taps, scales, grad_core
    )
    halo = lax.ppermute(halo, "ctx", [(s + 1, s) for s in range(count - 1)])
    given = between(spread(full, halo, grad_gates, weights, parts // 2, True))
    kept = spread(full, halo, grad_gates, weights, parts // 2, False)
    shares = call(merge_kernel, [(given.shape, BF16)])(kept, given)[0]
    return jnp.sum(across(shares).astype(F32), axis=0).astype(BF16)


def solution(mesh):
    sharded = P("ctx", "tp")
    kept = P(None, "tp")
    return jax.shard_map(
        local,
        mesh=mesh,
        in_specs=(sharded,) + (kept,) * 8 + (P("tp"), P("tp"), sharded),
        out_specs=sharded,
        check_vma=False,
    )
```

```python
import functools

import jax
import jax.numpy as jnp
from jax import lax
from jax.experimental import pallas as pl
from jax.experimental.pallas import tpu as pltpu
from jax.sharding import PartitionSpec as P

DH = 128
CONV = 4
EPS = 1e-06
SCALE = DH ** (-0.5)
RADIX = 4
PACK = 2 * DH
F32 = jnp.float32
BF16 = jnp.bfloat16


def bf(value):
    return value.astype(BF16)


def dot(left, right, dims=(1, 0)):
    return lax.dot_general(
        bf(left), bf(right), (((dims[0],), (dims[1],)), ((), ())), preferred_element_type=F32
    )


def halves(value):
    high = bf(value)
    return high, bf(value - high.astype(F32))


def dot3(left, right, dims=(1, 0)):
    left_high, left_low = halves(left)
    right_high, right_low = halves(right)
    return dot(left_high, right_high, dims) + (
        dot(left_high, right_low, dims) + dot(left_low, right_high, dims)
    )


def dot_exact(left, right):
    return lax.dot_general(
        left, right, (((1,), (0,)), ((), ())),
        precision=lax.Precision.HIGHEST, preferred_element_type=F32,
    )


def positions(shape=(DH, DH)):
    return lax.broadcasted_iota(jnp.int32, shape, 0), lax.broadcasted_iota(jnp.int32, shape, 1)


def sigmoid(value):
    return 1.0 / (1.0 + jnp.exp(-value))


def softplus(value):
    return jnp.maximum(value, 0.0) + jnp.log1p(jnp.exp(-jnp.abs(value)))


def lanes_of(pieces):
    _, lane = positions()
    result = jnp.zeros((DH, DH), F32)
    for place, piece in enumerate(pieces):
        result = jnp.where(lane == place, piece, result)
    return result


def unit_lower_inverses(stricts):
    row, col = positions()
    identity = jnp.where(row == col, 1.0, 0.0).astype(F32)
    inners = [jnp.where(row // 8 == col // 8, strict, 0.0) for strict in stricts]
    squares = [dot3(inner, inner) for inner in inners]
    results = [dot3(identity - inner, identity + square) for inner, square in zip(inners, squares)]
    fourths = [dot3(square, square) for square in squares]
    results = [dot3(result, identity + fourth) for result, fourth in zip(results, fourths)]
    size = 8
    while size < DH:
        off = (row // (2 * size) == col // (2 * size)) & (row // size != col // size)
        products = [
            dot3(result, jnp.where(off, strict, 0.0)) for result, strict in zip(results, stricts)
        ]
        results = [
            result - dot3(product, result) for result, product in zip(results, products)
        ]
        size *= 2
    return results


def core_place():
    return lax.axis_index("tp") % 2


def part_span(part, core, width):
    return pl.ds(pl.multiple_of((2 * part + core) * width, width), width)


def narrow_sums(x_ref, narrow_ref, core):
    parts, _, width = x_ref.shape
    beta = jnp.zeros((DH, 2), F32)
    alpha = jnp.zeros((DH, 2), F32)
    for part in range(parts):
        span = part_span(part, core, width)
        beta = beta + dot(x_ref[part], narrow_ref[0, :, span], (1, 1))
        alpha = alpha + dot(x_ref[part], narrow_ref[1, :, span], (1, 1))
    return lanes_of([beta[:, 0:1], beta[:, 1:2], alpha[:, 0:1], alpha[:, 1:2]])


def first_project_kernel(
    x_ref, wq_ref, wk_ref, wv_ref, wb_ref, wa_ref, fq_ref, fk_ref, fv_ref, decay_ref, bias_ref,
    total_ref, gates_ref, taps_ref, scales_ref, rest_ref, narrow_ref,
    held_ref, filter_ref, pair_ref, sems,
):
    core = core_place()
    places = (slice(0, DH), slice(DH, 2 * DH), slice(2 * DH, 4 * DH))
    copies = []

    def fetch(source, target):
        copies.append(pltpu.make_async_copy(source, target, sems.at[len(copies)]))
        copies[-1].start()

    for place, weight in zip(places, (wq_ref, wk_ref, wv_ref)):
        fetch(weight.at[:, core], held_ref.at[:, :, place])
    fetch(wb_ref, narrow_ref.at[0])
    fetch(wa_ref, narrow_ref.at[1])
    for place, taps in zip(places, (fq_ref, fk_ref, fv_ref)):
        fetch(taps, filter_ref.at[:, place])
    fetch(decay_ref, pair_ref.at[0])
    fetch(bias_ref, pair_ref.at[1])
    ready = len(copies)
    for place, weight in zip(places, (wq_ref, wk_ref, wv_ref)):
        fetch(weight.at[:, 1 - core], rest_ref.at[:, :, place])
    for copy in copies[:ready]:
        copy.wait()
    total = jnp.zeros((DH, 4 * DH), F32)
    for part in range(x_ref.shape[0]):
        total = total + dot(x_ref[part], held_ref[part])
    total_ref[...] = total
    gates_ref[...] = narrow_sums(x_ref, narrow_ref, core)
    taps_ref[0:CONV] = filter_ref[...].astype(F32)
    taps_ref[CONV:] = jnp.zeros((8 - CONV, 4 * DH), F32)
    decay = pair_ref[0]
    bias = pair_ref[1]
    scales_ref[0] = lanes_of([0.0, 0.0, -jnp.exp(decay[:, 0:1]), -jnp.exp(decay[:, 1:2])])
    scales_ref[1] = lanes_of([0.0, 0.0, bias[:, 0:1], bias[:, 1:2]])
    for copy in copies[ready:]:
        copy.wait()


def second_project_kernel(
    x_ref, total_ref, part_ref, rest_ref, narrow_ref, proj_ref, ba_ref, tail_ref
):
    total = total_ref[...]
    for part in range(x_ref.shape[0]):
        total = total + dot(x_ref[part], rest_ref[part])
    proj_ref[...] = bf(total)
    tail_ref[...] = bf(total[DH - 16 :])
    ba_ref[...] = bf(part_ref[...] + narrow_sums(x_ref, narrow_ref, 1 - core_place()))


def gate_kernel(ba_ref, scales_ref, cols_ref, gap_ref):
    row, col = positions()
    raw = ba_ref[...].astype(F32)
    log_decay = scales_ref[0] * softplus(raw + scales_ref[1])
    lower = jnp.where(row >= col, 1.0, 0.0).astype(F32)
    cols = jnp.where(col < 2, sigmoid(raw), dot_exact(lower, log_decay))
    cols_ref[...] = cols
    rows = cols.T
    for head in range(2):
        between = cols[:, 2 + head : 3 + head] - rows[2 + head : 3 + head, :]
        gap_ref[head] = jnp.where(row >= col, jnp.exp(jnp.where(row >= col, between, 0.0)), 0.0)


def slab_kernel(
    proj_ref, tail_ref, taps_ref, cols_ref, gap_ref, grad_ref,
    send_ref, pre_ref, unit_ref, inverse_ref, mixed_ref, weighted_ref,
    back_ref, gram_ref, cross_ref, pad_ref,
):
    row, col = positions()
    pad_ref[0:8] = tail_ref[8:16].astype(F32)
    pad_ref[8 : 8 + DH] = proj_ref[...].astype(F32)
    pre = jnp.zeros((DH, 4 * DH), F32)
    for tap in range(CONV):
        start = 8 - (CONV - 1) + tap
        pre = pre + taps_ref[tap : tap + 1] * pad_ref[start : start + DH]
    pre_ref[...] = pre
    act = pre * sigmoid(pre)
    query_act, key_act = act[:, :DH], act[:, DH : 2 * DH]
    query = query_act * (lax.rsqrt(jnp.sum(query_act * query_act, 1, keepdims=True) + EPS) * SCALE)
    key = key_act * lax.rsqrt(jnp.sum(key_act * key_act, 1, keepdims=True) + EPS)
    unit_ref[0] = query
    unit_ref[1] = key
    cols = cols_ref[...]
    gram = dot3(key, key, (1, 1))
    cross = dot(query, key, (1, 1))
    gram_ref[...] = gram
    cross_ref[...] = cross
    betas = [cols[:, head : head + 1] for head in range(2)]
    inverses = unit_lower_inverses(
        [
            jnp.where(row > col, beta * gram * gap_ref[head], 0.0)
            for head, beta in enumerate(betas)
        ]
    )
    for head in range(2):
        beta = betas[head]
        inverse = inverses[head]
        cum = cols[:, 2 + head : 3 + head]
        value = act[:, (2 + head) * DH : (3 + head) * DH]
        grad = grad_ref[:, head * DH : (head + 1) * DH]
        gamma = jnp.exp(cum)
        last = cum[DH - 1 : DH, :]
        key_tail = jnp.exp(last - cum) * key
        both = dot3(inverse, jnp.concatenate([beta * value, (beta * gamma) * key], axis=1))
        mixed = both[:, :DH]
        weighted = both[:, DH:]
        back = dot(cross * gap_ref[head], grad, (0, 0))
        inverse_ref[head] = bf(inverse)
        mixed_ref[head] = mixed
        weighted_ref[head] = bf(weighted)
        back_ref[head] = back
        ahead = dot(key_tail, both, (0, 0))
        lost = jnp.where(row == col, 1.0 - jnp.exp(last), 0.0) + ahead[:, DH:]
        send_ref[2 * head, 0:DH] = bf(lost)
        send_ref[2 * head, DH:] = bf(ahead[:, :DH])
        send_ref[2 * head + 1, 0:DH] = bf(lost.T)
        send_ref[2 * head + 1, DH:] = bf(
            dot(gamma * query, grad, (0, 0)) - dot(weighted, back, (0, 0))
        )


def unpack(ref):
    return ref[0:DH], ref[DH:].astype(F32)


def apply_map(later, state):
    matrix, offset = later
    return state - dot(matrix, state) + offset


def compose(later, earlier):
    matrix, offset = later
    before = earlier[0].astype(F32)
    return (
        before + matrix.astype(F32) - dot(matrix, before),
        apply_map(later, earlier[1]),
    )


def pack(total):
    return jnp.concatenate([bf(total[0]), bf(total[1])], axis=0)


def is_backward():
    return lax.axis_index("ctx") % 2 == 1


def in_order(step, backward):
    return jnp.where(backward, RADIX - 1 - step, step)


def group_kernel(got_ref, total_ref):
    backward = is_backward()
    total = unpack(got_ref.at[in_order(0, backward)])
    for step in range(1, RADIX):
        total = compose(unpack(got_ref.at[in_order(step, backward)]), total)
    total_ref[...] = pack(total)


def window_kernel(total_ref, last_ref, middle_ref, first_ref, wider_ref, before_ref):
    before = compose(unpack(last_ref), compose(unpack(middle_ref), unpack(first_ref)))
    before_ref[0:DH] = before[0]
    before_ref[DH:] = before[1]
    wider = pack(compose(unpack(total_ref), before))
    for place in range(RADIX):
        wider_ref[place] = wider


def states_kernel(rows_ref, before_ref, group_ref, out_ref):
    backward = is_backward()
    place = in_order(lax.axis_index("ctx") // (RADIX * RADIX), backward)
    state = jnp.zeros((DH, DH), F32)
    for step in range(RADIX - 1):
        later = apply_map(unpack(rows_ref.at[in_order(step, backward)]), state)
        state = jnp.where(step < place, later, state)
    state = apply_map((before_ref[0:DH], before_ref[DH:]), state)
    for step in range(RADIX):
        spot = in_order(step, backward)
        out_ref[spot] = bf(state)
        if step < RADIX - 1:
            state = apply_map(unpack(group_ref.at[spot]), state)


def gradient_kernel(
    states_ref, pre_ref, unit_ref, cols_ref, ba_ref, inverse_ref, mixed_ref, weighted_ref,
    back_ref, gap_ref, gram_ref, cross_ref, grad_ref, taps_ref, scales_ref,
    full_ref, gates_ref, halo_ref, pad_ref,
):
    row, col = positions()
    cols = cols_ref[...]
    gram = gram_ref[...]
    cross = cross_ref[...]
    query = unit_ref[0]
    key = unit_ref[1]
    pre = pre_ref[...]
    gate = sigmoid(pre)
    act = pre * gate
    slope = gate * (1.0 + pre * (1.0 - gate))
    grad_query = jnp.zeros((DH, DH), F32)
    grad_key = jnp.zeros((DH, DH), F32)
    pieces = []
    columns = jnp.zeros((DH, DH), F32)
    sides = []
    for head in range(2):
        state = states_ref[2 * head]
        after = states_ref[2 * head + 1]
        beta = cols[:, head : head + 1]
        cum = cols[:, 2 + head : 3 + head]
        gamma = jnp.exp(cum)
        last = cum[DH - 1 : DH, :]
        rest = jnp.exp(last - cum)
        value = act[:, (2 + head) * DH : (3 + head) * DH]
        grad = grad_ref[:, head * DH : (head + 1) * DH]
        gap = gap_ref[head]
        fresh = mixed_ref[head] - dot(weighted_ref[head], state)
        grad_fresh = back_ref[head] + dot(rest * key, after)
        solved = dot(inverse_ref[head], grad_fresh, (0, 0))
        grad_strict = jnp.where(row > col, -dot(solved, fresh, (1, 1)), 0.0) * gap
        grad_cross = dot(grad, fresh, (1, 1)) * gap
        grad_weighted = -dot(solved, state, (1, 1))
        grad_scaled = dot(grad, state, (1, 1))
        grad_tail = dot(fresh, after, (1, 1))
        grad_query = grad_query + gamma * grad_scaled + dot(grad_cross, key)
        grad_gram = beta * grad_strict
        grad_key = grad_key + (
            dot(grad_cross, query, (0, 0))
            + dot(grad_gram, key)
            + dot(grad_gram, key, (0, 0))
            + (beta * gamma) * grad_weighted
            + rest * grad_tail
        )
        pieces.append(beta * solved)
        by_beta = jnp.sum(grad_strict * gram, 1, keepdims=True)
        by_key = gamma * jnp.sum(grad_weighted * key, 1, keepdims=True)
        grad_beta = jnp.sum(solved * value, 1, keepdims=True) + by_key + by_beta
        by_gap = grad_gram * gram + grad_cross * cross
        by_tail = rest * jnp.sum(grad_tail * key, 1, keepdims=True)
        at_end = jnp.sum(by_tail, 0, keepdims=True) + jnp.exp(last) * jnp.sum(
            jnp.sum(state.astype(F32) * after.astype(F32), 1, keepdims=True), 0, keepdims=True
        )
        grad_cum = (
            jnp.sum(by_gap, 1, keepdims=True)
            + gamma * jnp.sum(grad_scaled * query, 1, keepdims=True)
            + beta * by_key
            - by_tail
            + jnp.where(row[:, 0:1] == DH - 1, at_end, 0.0)
        )
        columns = jnp.where(row == 2 + head, jnp.sum(by_gap, 0, keepdims=True), columns)
        sides.append((grad_beta, grad_cum))
    raw = ba_ref[...].astype(F32)
    rate = scales_ref[0]
    bias = scales_ref[1]
    sides = lanes_of([sides[0][0], sides[1][0], sides[0][1], sides[1][1]]) - columns.T
    upper = jnp.where(row <= col, 1.0, 0.0).astype(F32)
    grad_log = dot_exact(upper, sides)
    beta = cols
    gates_ref[...] = bf(
        jnp.where(
            col < 2,
            sides * beta * (1.0 - beta),
            jnp.where(col < 4, grad_log * rate * sigmoid(raw + bias), 0.0),
        )
    )
    key_act = act[:, DH : 2 * DH]
    query_act = act[:, :DH]
    query_size = lax.rsqrt(jnp.sum(query_act * query_act, 1, keepdims=True) + EPS)
    key_size = lax.rsqrt(jnp.sum(key_act * key_act, 1, keepdims=True) + EPS)
    query_dir = query_act * query_size
    grad_query = grad_query * SCALE
    grad_query = query_size * (
        grad_query - query_dir * jnp.sum(grad_query * query_dir, 1, keepdims=True)
    )
    grad_key = key_size * (grad_key - key * jnp.sum(grad_key * key, 1, keepdims=True))
    pad_ref[0:8] = jnp.zeros((8, 4 * DH), F32)
    pad_ref[8 + DH :] = jnp.zeros((8, 4 * DH), F32)
    for place, piece in enumerate([grad_query, grad_key] + pieces):
        span = slice(place * DH, (place + 1) * DH)
        pad_ref[8 : 8 + DH, span] = piece * slope[:, span]
    total = jnp.zeros((8 + DH, 4 * DH), F32)
    for tap in range(CONV):
        start = CONV - 1 - tap
        total = total + taps_ref[tap : tap + 1] * pad_ref[start : start + 8 + DH]
    halo_ref[...] = total[0:8]
    full_ref[...] = total[8:]


def spread_kernel(
    other, full_ref, halo_ref, gates_ref, wq_ref, wk_ref, wv_ref, wb_ref, wa_ref, out_ref
):
    core = core_place()
    core = 1 - core if other else core
    full = full_ref[...]
    end = full[DH - 8 :] + halo_ref[...]
    grads = bf(jnp.concatenate([full[: DH - 8], end], axis=0))
    gates = gates_ref[...]
    parts, _, width = out_ref.shape
    for part in range(parts):
        span = part_span(part, core, width)
        total = dot(grads[:, :DH], wq_ref[span, :], (1, 1))
        total = total + dot(grads[:, DH : 2 * DH], wk_ref[span, :], (1, 1))
        total = total + dot(grads[:, 2 * DH :], wv_ref[span, :], (1, 1))
        total = total + dot(gates[:, 0:2], wb_ref[:, span])
        total = total + dot(gates[:, 2:4], wa_ref[:, span])
        out_ref[part] = total.astype(out_ref.dtype)


def merge_kernel(kept_ref, got_ref, out_ref):
    out_ref[...] = bf(kept_ref[...] + got_ref[...].astype(F32))


def call(kernel, outs, scratch=(), specs=None):
    extra = {} if specs is None else {"in_specs": specs}
    return pl.pallas_call(
        kernel,
        out_shape=[jax.ShapeDtypeStruct(shape, kind) for shape, kind in outs],
        scratch_shapes=list(scratch),
        compiler_params=pltpu.CompilerParams(vmem_limit_bytes=48 * 1024 * 1024),
        **extra,
    )


def stay(array):
    return pltpu.with_memory_space_constraint(array, pltpu.HBM)


def first_project(mine, weights, filters, decay, bias):
    parts, rows, width = mine.shape
    inside = pl.BlockSpec(memory_space=pltpu.VMEM)
    outside = pl.BlockSpec(memory_space=pltpu.HBM)
    model = 2 * parts * width
    wide = [weight.reshape(parts, 2, width, weight.shape[1]) for weight in weights[:3]]
    return call(
        first_project_kernel,
        [
            ((rows, 4 * DH), F32), ((DH, DH), F32), ((8, 4 * DH), F32), ((2, DH, DH), F32),
            ((parts, width, 4 * DH), BF16), ((2, 2, model), BF16),
        ],
        [
            pltpu.VMEM((parts, width, 4 * DH), BF16),
            pltpu.VMEM((CONV, 4 * DH), BF16),
            pltpu.VMEM((2, 1, 2), F32),
            pltpu.SemaphoreType.DMA((13,)),
        ],
        [inside] + [outside] * 10,
    )(mine, *[stay(array) for array in (*wide, *weights[3:], *filters, decay, bias)])


def second_project(other, total, part, rest, narrow):
    return call(
        second_project_kernel,
        [((DH, 4 * DH), BF16), ((DH, DH), BF16), ((16, 4 * DH), BF16)],
    )(other, total, part, rest, narrow)


def slab(proj, tail, taps, cols, gap, grad):
    square = (DH, DH)
    return call(
        slab_kernel,
        [
            ((4, PACK, DH), BF16), ((DH, 4 * DH), F32), ((2,) + square, F32),
            ((2,) + square, BF16), ((2,) + square, F32), ((2,) + square, BF16),
            ((2,) + square, F32), (square, F32), (square, F32),
        ],
        [pltpu.VMEM((8 + DH, 4 * DH), F32)],
    )(proj, tail, taps, cols, gap, grad)


def gradient(states, kept, cols, gap, gates, taps, scales, grad):
    pre, unit, inverse, mixed, weighted, back, gram, cross = kept
    return call(
        gradient_kernel,
        [((DH, 4 * DH), F32), ((DH, DH), BF16), ((8, 4 * DH), F32)],
        [pltpu.VMEM((16 + DH, 4 * DH), F32)],
    )(
        states, pre, unit, cols, gates, inverse, mixed, weighted, back, gap, gram, cross,
        grad, taps, scales,
    )


def spread(full, halo, gates, weights, parts, other):
    width = weights[0].shape[0] // (2 * parts)
    return call(
        functools.partial(spread_kernel, other),
        [((parts, DH, width), BF16 if other else F32)],
    )(full, halo, gates, *weights)[0]


def local(
    inputs, query_weight, key_weight, value_weight, beta_weight, alpha_weight,
    query_filter, key_filter, value_filter, decay_log, step_bias, grad_core,
):
    weights = (query_weight, key_weight, value_weight, beta_weight.T, alpha_weight.T)
    filters = (query_filter, key_filter, value_filter)
    decay = decay_log.reshape(1, 2)
    bias = step_bias.reshape(1, 2)
    count = lax.axis_size("ctx")
    parts = lax.axis_size("tp")
    slabs = range(count)
    group = [[s for s in slabs if s // RADIX == g] for g in range(count // RADIX)]
    rank = [[s for s in slabs if s % 16 == z] for z in range(16)]

    def exchange(value, groups):
        return lax.all_to_all(value, "ctx", 0, 0, axis_index_groups=groups)

    def onward(value, distance):
        steps = [(s, s - distance if s % 2 else s + distance) for s in slabs]
        return lax.ppermute(value, "ctx", [(s, t) for s, t in steps if 0 <= t < count])

    chips = [[2 * chip + core for chip in range(parts // 2)] for core in range(2)]

    def across(value):
        return lax.all_to_all(value, "tp", 0, 0, axis_index_groups=chips)

    def between(value):
        return lax.ppermute(value, "tp", [(t, t ^ 1) for t in range(parts)])

    mine = across(jnp.broadcast_to(inputs[None], (parts // 2,) + inputs.shape))
    other = between(mine)
    total, part, taps, scales, rest, narrow = first_project(mine, weights, filters, decay, bias)
    proj, gates, tail = second_project(other, total, part, rest, narrow)
    tail = lax.ppermute(tail, "ctx", [(s, s + 1) for s in range(count - 1)])
    square = (DH, DH)
    cols, gap = call(gate_kernel, [(square, F32), ((2,) + square, F32)])(gates, scales)
    send, *kept = slab(proj, tail, taps, cols, gap, grad_core)
    got = exchange(send, group)
    total = call(group_kernel, [((PACK, DH), BF16)])(got)[0]
    last = onward(total, RADIX)
    earlier = [last, onward(last, RADIX), onward(total, 3 * RADIX)]
    total, before = call(
        window_kernel, [((RADIX, PACK, DH), BF16), ((PACK, DH), F32)]
    )(total, *earlier)
    states = call(states_kernel, [((RADIX, DH, DH), BF16)])(exchange(total, rank), before, got)[0]
    states = exchange(states, group)
    full, grad_gates, halo = gradient(
        states, kept, cols, gap, gates, taps, scales, grad_core
    )
    halo = lax.ppermute(halo, "ctx", [(s + 1, s) for s in range(count - 1)])
    given = between(spread(full, halo, grad_gates, weights, parts // 2, True))
    kept = spread(full, halo, grad_gates, weights, parts // 2, False)
    shares = call(merge_kernel, [(given.shape, BF16)])(kept, given)[0]
    return jnp.sum(across(shares).astype(F32), axis=0).astype(BF16)


def solution(mesh):
    sharded = P("ctx", "tp")
    kept = P(None, "tp")
    return jax.shard_map(
        local,
        mesh=mesh,
        in_specs=(sharded,) + (kept,) * 8 + (P("tp"), P("tp"), sharded),
        out_specs=sharded,
        check_vma=False,
    )
```

```python
import functools

import jax
import jax.numpy as jnp
from jax import lax
from jax.experimental import pallas as pl
from jax.experimental.pallas import tpu as pltpu
from jax.sharding import PartitionSpec as P

DH = 128
CONV = 4
EPS = 1e-06
SCALE = DH ** (-0.5)
RADIX = 4
PACK = 2 * DH
F32 = jnp.float32
BF16 = jnp.bfloat16


def bf(value):
    return value.astype(BF16)


def dot(left, right, dims=(1, 0)):
    return lax.dot_general(
        bf(left), bf(right), (((dims[0],), (dims[1],)), ((), ())), preferred_element_type=F32
    )


def halves(value):
    high = bf(value)
    return high, bf(value - high.astype(F32))


def dot3(left, right, dims=(1, 0)):
    left_high, left_low = halves(left)
    right_high, right_low = halves(right)
    return dot(left_high, right_high, dims) + (
        dot(left_high, right_low, dims) + dot(left_low, right_high, dims)
    )


def dot_exact(left, right):
    return lax.dot_general(
        left, right, (((1,), (0,)), ((), ())),
        precision=lax.Precision.HIGHEST, preferred_element_type=F32,
    )


def positions(shape=(DH, DH)):
    return lax.broadcasted_iota(jnp.int32, shape, 0), lax.broadcasted_iota(jnp.int32, shape, 1)


def sigmoid(value):
    return 1.0 / (1.0 + jnp.exp(-value))


def softplus(value):
    return jnp.maximum(value, 0.0) + jnp.log1p(jnp.exp(-jnp.abs(value)))


def lanes_of(pieces):
    _, lane = positions()
    result = jnp.zeros((DH, DH), F32)
    for place, piece in enumerate(pieces):
        result = jnp.where(lane == place, piece, result)
    return result


def unit_lower_inverses(stricts):
    row, col = positions()
    identity = jnp.where(row == col, 1.0, 0.0).astype(F32)
    inners = [jnp.where(row // 8 == col // 8, strict, 0.0) for strict in stricts]
    squares = [dot3(inner, inner) for inner in inners]
    results = [dot3(identity - inner, identity + square) for inner, square in zip(inners, squares)]
    fourths = [dot3(square, square) for square in squares]
    results = [dot3(result, identity + fourth) for result, fourth in zip(results, fourths)]
    size = 8
    while size < DH:
        off = (row // (2 * size) == col // (2 * size)) & (row // size != col // size)
        products = [
            dot3(result, jnp.where(off, strict, 0.0)) for result, strict in zip(results, stricts)
        ]
        results = [
            result - dot3(product, result) for result, product in zip(results, products)
        ]
        size *= 2
    return results


def core_place():
    return lax.axis_index("tp") % 2


def part_span(part, core, width):
    return pl.ds(pl.multiple_of((2 * part + core) * width, width), width)


def narrow_sums(x_ref, narrow_ref, core):
    parts, _, width = x_ref.shape
    beta = jnp.zeros((DH, 2), F32)
    alpha = jnp.zeros((DH, 2), F32)
    for part in range(parts):
        span = part_span(part, core, width)
        beta = beta + dot(x_ref[part], narrow_ref[0, :, span], (1, 1))
        alpha = alpha + dot(x_ref[part], narrow_ref[1, :, span], (1, 1))
    return lanes_of([beta[:, 0:1], beta[:, 1:2], alpha[:, 0:1], alpha[:, 1:2]])


def first_project_kernel(
    x_ref, wq_ref, wk_ref, wv_ref, wb_ref, wa_ref, fq_ref, fk_ref, fv_ref, decay_ref, bias_ref,
    total_ref, gates_ref, taps_ref, scales_ref, rest_ref, narrow_ref,
    held_ref, filter_ref, pair_ref, sems,
):
    core = core_place()
    places = (slice(0, DH), slice(DH, 2 * DH), slice(2 * DH, 4 * DH))
    copies = []

    def fetch(source, target):
        copies.append(pltpu.make_async_copy(source, target, sems.at[len(copies)]))
        copies[-1].start()

    for place, weight in zip(places, (wq_ref, wk_ref, wv_ref)):
        fetch(weight.at[:, core], held_ref.at[:, :, place])
    fetch(wb_ref, narrow_ref.at[0])
    fetch(wa_ref, narrow_ref.at[1])
    for place, taps in zip(places, (fq_ref, fk_ref, fv_ref)):
        fetch(taps, filter_ref.at[:, place])
    fetch(decay_ref, pair_ref.at[0])
    fetch(bias_ref, pair_ref.at[1])
    ready = len(copies)
    for place, weight in zip(places, (wq_ref, wk_ref, wv_ref)):
        fetch(weight.at[:, 1 - core], rest_ref.at[:, :, place])
    for copy in copies[:ready]:
        copy.wait()
    total = jnp.zeros((DH, 4 * DH), F32)
    for part in range(x_ref.shape[0]):
        total = total + dot(x_ref[part], held_ref[part])
    total_ref[...] = total
    gates_ref[...] = narrow_sums(x_ref, narrow_ref, core)
    taps_ref[0:CONV] = filter_ref[...].astype(F32)
    taps_ref[CONV:] = jnp.zeros((8 - CONV, 4 * DH), F32)
    decay = pair_ref[0]
    bias = pair_ref[1]
    scales_ref[0] = lanes_of([0.0, 0.0, -jnp.exp(decay[:, 0:1]), -jnp.exp(decay[:, 1:2])])
    scales_ref[1] = lanes_of([0.0, 0.0, bias[:, 0:1], bias[:, 1:2]])
    for copy in copies[ready:]:
        copy.wait()


def second_project_kernel(
    x_ref, total_ref, part_ref, rest_ref, narrow_ref, proj_ref, ba_ref, tail_ref
):
    total = total_ref[...]
    for part in range(x_ref.shape[0]):
        total = total + dot(x_ref[part], rest_ref[part])
    proj_ref[...] = bf(total)
    tail_ref[...] = bf(total[DH - 16 :])
    ba_ref[...] = bf(part_ref[...] + narrow_sums(x_ref, narrow_ref, 1 - core_place()))


def gate_kernel(ba_ref, scales_ref, cols_ref, gap_ref):
    row, col = positions()
    raw = ba_ref[...].astype(F32)
    log_decay = scales_ref[0] * softplus(raw + scales_ref[1])
    lower = jnp.where(row >= col, 1.0, 0.0).astype(F32)
    cols = jnp.where(col < 2, sigmoid(raw), dot_exact(lower, log_decay))
    cols_ref[...] = cols
    rows = cols.T
    for head in range(2):
        between = cols[:, 2 + head : 3 + head] - rows[2 + head : 3 + head, :]
        gap_ref[head] = jnp.where(row >= col, jnp.exp(jnp.where(row >= col, between, 0.0)), 0.0)


def slab_kernel(
    proj_ref, tail_ref, taps_ref, cols_ref, gap_ref, grad_ref,
    send_ref, pre_ref, unit_ref, inverse_ref, mixed_ref, weighted_ref,
    back_ref, gram_ref, cross_ref, pad_ref,
):
    row, col = positions()
    pad_ref[0:8] = tail_ref[8:16].astype(F32)
    pad_ref[8 : 8 + DH] = proj_ref[...].astype(F32)
    pre = jnp.zeros((DH, 4 * DH), F32)
    for tap in range(CONV):
        start = 8 - (CONV - 1) + tap
        pre = pre + taps_ref[tap : tap + 1] * pad_ref[start : start + DH]
    pre_ref[...] = pre
    act = pre * sigmoid(pre)
    query_act, key_act = act[:, :DH], act[:, DH : 2 * DH]
    query = query_act * (lax.rsqrt(jnp.sum(query_act * query_act, 1, keepdims=True) + EPS) * SCALE)
    key = key_act * lax.rsqrt(jnp.sum(key_act * key_act, 1, keepdims=True) + EPS)
    unit_ref[0] = query
    unit_ref[1] = key
    cols = cols_ref[...]
    gram = dot3(key, key, (1, 1))
    cross = dot(query, key, (1, 1))
    gram_ref[...] = gram
    cross_ref[...] = cross
    betas = [cols[:, head : head + 1] for head in range(2)]
    inverses = unit_lower_inverses(
        [
            jnp.where(row > col, beta * gram * gap_ref[head], 0.0)
            for head, beta in enumerate(betas)
        ]
    )
    for head in range(2):
        beta = betas[head]
        inverse = inverses[head]
        cum = cols[:, 2 + head : 3 + head]
        value = act[:, (2 + head) * DH : (3 + head) * DH]
        grad = grad_ref[:, head * DH : (head + 1) * DH]
        gamma = jnp.exp(cum)
        last = cum[DH - 1 : DH, :]
        key_tail = jnp.exp(last - cum) * key
        both = dot3(inverse, jnp.concatenate([beta * value, (beta * gamma) * key], axis=1))
        mixed = both[:, :DH]
        weighted = both[:, DH:]
        back = dot(cross * gap_ref[head], grad, (0, 0))
        inverse_ref[head] = bf(inverse)
        mixed_ref[head] = mixed
        weighted_ref[head] = bf(weighted)
        back_ref[head] = back
        ahead = dot(key_tail, both, (0, 0))
        lost = jnp.where(row == col, 1.0 - jnp.exp(last), 0.0) + ahead[:, DH:]
        send_ref[2 * head, 0:DH] = bf(lost)
        send_ref[2 * head, DH:] = bf(ahead[:, :DH])
        send_ref[2 * head + 1, 0:DH] = bf(lost.T)
        send_ref[2 * head + 1, DH:] = bf(
            dot(gamma * query, grad, (0, 0)) - dot(weighted, back, (0, 0))
        )


def unpack(ref):
    return ref[0:DH], ref[DH:].astype(F32)


def apply_map(later, state):
    matrix, offset = later
    return state - dot(matrix, state) + offset


def compose(later, earlier):
    matrix, offset = later
    before = earlier[0].astype(F32)
    return (
        before + matrix.astype(F32) - dot(matrix, before),
        apply_map(later, earlier[1]),
    )


def pack(total):
    return jnp.concatenate([bf(total[0]), bf(total[1])], axis=0)


def is_backward():
    return lax.axis_index("ctx") % 2 == 1


def in_order(step, backward):
    return jnp.where(backward, RADIX - 1 - step, step)


def group_kernel(got_ref, total_ref):
    backward = is_backward()
    total = unpack(got_ref.at[in_order(0, backward)])
    for step in range(1, RADIX):
        total = compose(unpack(got_ref.at[in_order(step, backward)]), total)
    total_ref[...] = pack(total)


def window_kernel(total_ref, last_ref, middle_ref, first_ref, wider_ref, before_ref):
    before = compose(unpack(last_ref), compose(unpack(middle_ref), unpack(first_ref)))
    before_ref[0:DH] = before[0]
    before_ref[DH:] = before[1]
    wider = pack(compose(unpack(total_ref), before))
    for place in range(RADIX):
        wider_ref[place] = wider


def states_kernel(rows_ref, before_ref, group_ref, out_ref):
    backward = is_backward()
    place = in_order(lax.axis_index("ctx") // (RADIX * RADIX), backward)
    state = jnp.zeros((DH, DH), F32)
    for step in range(RADIX - 1):
        later = apply_map(unpack(rows_ref.at[in_order(step, backward)]), state)
        state = jnp.where(step < place, later, state)
    state = apply_map((before_ref[0:DH], before_ref[DH:]), state)
    for step in range(RADIX):
        spot = in_order(step, backward)
        out_ref[spot] = bf(state)
        if step < RADIX - 1:
            state = apply_map(unpack(group_ref.at[spot]), state)


def gradient_kernel(
    states_ref, pre_ref, unit_ref, cols_ref, ba_ref, inverse_ref, mixed_ref, weighted_ref,
    back_ref, gap_ref, gram_ref, cross_ref, grad_ref, taps_ref, scales_ref,
    full_ref, gates_ref, halo_ref, pad_ref,
):
    row, col = positions()
    cols = cols_ref[...]
    gram = gram_ref[...]
    cross = cross_ref[...]
    query = unit_ref[0]
    key = unit_ref[1]
    pre = pre_ref[...]
    gate = sigmoid(pre)
    act = pre * gate
    slope = gate * (1.0 + pre * (1.0 - gate))
    grad_query = jnp.zeros((DH, DH), F32)
    grad_key = jnp.zeros((DH, DH), F32)
    pieces = []
    columns = jnp.zeros((DH, DH), F32)
    sides = []
    for head in range(2):
        state = states_ref[2 * head]
        after = states_ref[2 * head + 1]
        beta = cols[:, head : head + 1]
        cum = cols[:, 2 + head : 3 + head]
        gamma = jnp.exp(cum)
        last = cum[DH - 1 : DH, :]
        rest = jnp.exp(last - cum)
        value = act[:, (2 + head) * DH : (3 + head) * DH]
        grad = grad_ref[:, head * DH : (head + 1) * DH]
        gap = gap_ref[head]
        fresh = mixed_ref[head] - dot(weighted_ref[head], state)
        grad_fresh = back_ref[head] + dot(rest * key, after)
        solved = dot(inverse_ref[head], grad_fresh, (0, 0))
        grad_strict = jnp.where(row > col, -dot(solved, fresh, (1, 1)), 0.0) * gap
        grad_cross = dot(grad, fresh, (1, 1)) * gap
        grad_weighted = -dot(solved, state, (1, 1))
        grad_scaled = dot(grad, state, (1, 1))
        grad_tail = dot(fresh, after, (1, 1))
        grad_query = grad_query + gamma * grad_scaled + dot(grad_cross, key)
        grad_gram = beta * grad_strict
        grad_key = grad_key + (
            dot(grad_cross, query, (0, 0))
            + dot(grad_gram, key)
            + dot(grad_gram, key, (0, 0))
            + (beta * gamma) * grad_weighted
            + rest * grad_tail
        )
        pieces.append(beta * solved)
        by_beta = jnp.sum(grad_strict * gram, 1, keepdims=True)
        by_key = gamma * jnp.sum(grad_weighted * key, 1, keepdims=True)
        grad_beta = jnp.sum(solved * value, 1, keepdims=True) + by_key + by_beta
        by_gap = grad_gram * gram + grad_cross * cross
        by_tail = rest * jnp.sum(grad_tail * key, 1, keepdims=True)
        at_end = jnp.sum(by_tail, 0, keepdims=True) + jnp.exp(last) * jnp.sum(
            jnp.sum(state.astype(F32) * after.astype(F32), 1, keepdims=True), 0, keepdims=True
        )
        grad_cum = (
            jnp.sum(by_gap, 1, keepdims=True)
            + gamma * jnp.sum(grad_scaled * query, 1, keepdims=True)
            + beta * by_key
            - by_tail
            + jnp.where(row[:, 0:1] == DH - 1, at_end, 0.0)
        )
        columns = jnp.where(row == 2 + head, jnp.sum(by_gap, 0, keepdims=True), columns)
        sides.append((grad_beta, grad_cum))
    raw = ba_ref[...].astype(F32)
    rate = scales_ref[0]
    bias = scales_ref[1]
    sides = lanes_of([sides[0][0], sides[1][0], sides[0][1], sides[1][1]]) - columns.T
    upper = jnp.where(row <= col, 1.0, 0.0).astype(F32)
    grad_log = dot_exact(upper, sides)
    beta = cols
    gates_ref[...] = bf(
        jnp.where(
            col < 2,
            sides * beta * (1.0 - beta),
            jnp.where(col < 4, grad_log * rate * sigmoid(raw + bias), 0.0),
        )
    )
    key_act = act[:, DH : 2 * DH]
    query_act = act[:, :DH]
    query_size = lax.rsqrt(jnp.sum(query_act * query_act, 1, keepdims=True) + EPS)
    key_size = lax.rsqrt(jnp.sum(key_act * key_act, 1, keepdims=True) + EPS)
    query_dir = query_act * query_size
    grad_query = grad_query * SCALE
    grad_query = query_size * (
        grad_query - query_dir * jnp.sum(grad_query * query_dir, 1, keepdims=True)
    )
    grad_key = key_size * (grad_key - key * jnp.sum(grad_key * key, 1, keepdims=True))
    pad_ref[0:8] = jnp.zeros((8, 4 * DH), F32)
    pad_ref[8 + DH :] = jnp.zeros((8, 4 * DH), F32)
    for place, piece in enumerate([grad_query, grad_key] + pieces):
        span = slice(place * DH, (place + 1) * DH)
        pad_ref[8 : 8 + DH, span] = piece * slope[:, span]
    total = jnp.zeros((8 + DH, 4 * DH), F32)
    for tap in range(CONV):
        start = CONV - 1 - tap
        total = total + taps_ref[tap : tap + 1] * pad_ref[start : start + 8 + DH]
    halo_ref[...] = total[0:8]
    full_ref[...] = total[8:]


def spread_kernel(
    other, full_ref, halo_ref, gates_ref, wq_ref, wk_ref, wv_ref, wb_ref, wa_ref, out_ref
):
    core = core_place()
    core = 1 - core if other else core
    full = full_ref[...]
    end = full[DH - 8 :] + halo_ref[...]
    grads = bf(jnp.concatenate([full[: DH - 8], end], axis=0))
    gates = gates_ref[...]
    parts, _, width = out_ref.shape
    for part in range(parts):
        span = part_span(part, core, width)
        total = dot(grads[:, :DH], wq_ref[span, :], (1, 1))
        total = total + dot(grads[:, DH : 2 * DH], wk_ref[span, :], (1, 1))
        total = total + dot(grads[:, 2 * DH :], wv_ref[span, :], (1, 1))
        total = total + dot(gates[:, 0:2], wb_ref[:, span])
        total = total + dot(gates[:, 2:4], wa_ref[:, span])
        out_ref[part] = total.astype(out_ref.dtype)


def merge_kernel(kept_ref, got_ref, out_ref):
    out_ref[...] = bf(kept_ref[...] + got_ref[...].astype(F32))


def call(kernel, outs, scratch=(), specs=None):
    extra = {} if specs is None else {"in_specs": specs}
    return pl.pallas_call(
        kernel,
        out_shape=[jax.ShapeDtypeStruct(shape, kind) for shape, kind in outs],
        scratch_shapes=list(scratch),
        compiler_params=pltpu.CompilerParams(vmem_limit_bytes=48 * 1024 * 1024),
        **extra,
    )


def stay(array):
    return pltpu.with_memory_space_constraint(array, pltpu.HBM)


def first_project(mine, weights, filters, decay, bias):
    parts, rows, width = mine.shape
    inside = pl.BlockSpec(memory_space=pltpu.VMEM)
    outside = pl.BlockSpec(memory_space=pltpu.HBM)
    model = 2 * parts * width
    wide = [weight.reshape(parts, 2, width, weight.shape[1]) for weight in weights[:3]]
    return call(
        first_project_kernel,
        [
            ((rows, 4 * DH), F32), ((DH, DH), F32), ((8, 4 * DH), F32), ((2, DH, DH), F32),
            ((parts, width, 4 * DH), BF16), ((2, 2, model), BF16),
        ],
        [
            pltpu.VMEM((parts, width, 4 * DH), BF16),
            pltpu.VMEM((CONV, 4 * DH), BF16),
            pltpu.VMEM((2, 1, 2), F32),
            pltpu.SemaphoreType.DMA((13,)),
        ],
        [inside] + [outside] * 10,
    )(mine, *[stay(array) for array in (*wide, *weights[3:], *filters, decay, bias)])


def second_project(other, total, part, rest, narrow):
    return call(
        second_project_kernel,
        [((DH, 4 * DH), BF16), ((DH, DH), BF16), ((16, 4 * DH), BF16)],
    )(other, total, part, rest, narrow)


def slab(proj, tail, taps, cols, gap, grad):
    square = (DH, DH)
    return call(
        slab_kernel,
        [
            ((4, PACK, DH), BF16), ((DH, 4 * DH), F32), ((2,) + square, F32),
            ((2,) + square, BF16), ((2,) + square, F32), ((2,) + square, BF16),
            ((2,) + square, F32), (square, F32), (square, F32),
        ],
        [pltpu.VMEM((8 + DH, 4 * DH), F32)],
    )(proj, tail, taps, cols, gap, grad)


def gradient(states, kept, cols, gap, gates, taps, scales, grad):
    pre, unit, inverse, mixed, weighted, back, gram, cross = kept
    return call(
        gradient_kernel,
        [((DH, 4 * DH), F32), ((DH, DH), BF16), ((8, 4 * DH), F32)],
        [pltpu.VMEM((16 + DH, 4 * DH), F32)],
    )(
        states, pre, unit, cols, gates, inverse, mixed, weighted, back, gap, gram, cross,
        grad, taps, scales,
    )


def spread(full, halo, gates, weights, parts, other):
    width = weights[0].shape[0] // (2 * parts)
    return call(
        functools.partial(spread_kernel, other),
        [((parts, DH, width), BF16 if other else F32)],
    )(full, halo, gates, *weights)[0]


def local(
    inputs, query_weight, key_weight, value_weight, beta_weight, alpha_weight,
    query_filter, key_filter, value_filter, decay_log, step_bias, grad_core,
):
    weights = (query_weight, key_weight, value_weight, beta_weight.T, alpha_weight.T)
    filters = (query_filter, key_filter, value_filter)
    decay = decay_log.reshape(1, 2)
    bias = step_bias.reshape(1, 2)
    count = lax.axis_size("ctx")
    parts = lax.axis_size("tp")
    slabs = range(count)
    group = [[s for s in slabs if s // RADIX == g] for g in range(count // RADIX)]
    rank = [[s for s in slabs if s % 16 == z] for z in range(16)]

    def exchange(value, groups):
        return lax.all_to_all(value, "ctx", 0, 0, axis_index_groups=groups)

    def onward(value, distance):
        steps = [(s, s - distance if s % 2 else s + distance) for s in slabs]
        return lax.ppermute(value, "ctx", [(s, t) for s, t in steps if 0 <= t < count])

    chips = [[2 * chip + core for chip in range(parts // 2)] for core in range(2)]

    def across(value):
        return lax.all_to_all(value, "tp", 0, 0, axis_index_groups=chips)

    def between(value):
        return lax.ppermute(value, "tp", [(t, t ^ 1) for t in range(parts)])

    mine = across(jnp.broadcast_to(inputs[None], (parts // 2,) + inputs.shape))
    other = between(mine)
    total, part, taps, scales, rest, narrow = first_project(mine, weights, filters, decay, bias)
    proj, gates, tail = second_project(other, total, part, rest, narrow)
    tail = lax.ppermute(tail, "ctx", [(s, s + 1) for s in range(count - 1)])
    square = (DH, DH)
    cols, gap = call(gate_kernel, [(square, F32), ((2,) + square, F32)])(gates, scales)
    send, *kept = slab(proj, tail, taps, cols, gap, grad_core)
    got = exchange(send, group)
    total = call(group_kernel, [((PACK, DH), BF16)])(got)[0]
    last, again = lax.optimization_barrier((onward(total, RADIX), total))
    earlier = [last, onward(last, RADIX), onward(again, 3 * RADIX)]
    total, before = call(
        window_kernel, [((RADIX, PACK, DH), BF16), ((PACK, DH), F32)]
    )(total, *earlier)
    states = call(states_kernel, [((RADIX, DH, DH), BF16)])(exchange(total, rank), before, got)[0]
    states = exchange(states, group)
    full, grad_gates, halo = gradient(
        states, kept, cols, gap, gates, taps, scales, grad_core
    )
    halo = lax.ppermute(halo, "ctx", [(s + 1, s) for s in range(count - 1)])
    given = between(spread(full, halo, grad_gates, weights, parts // 2, True))
    kept = spread(full, halo, grad_gates, weights, parts // 2, False)
    shares = call(merge_kernel, [(given.shape, BF16)])(kept, given)[0]
    return jnp.sum(across(shares).astype(F32), axis=0).astype(BF16)


def solution(mesh):
    sharded = P("ctx", "tp")
    kept = P(None, "tp")
    return jax.shard_map(
        local,
        mesh=mesh,
        in_specs=(sharded,) + (kept,) * 8 + (P("tp"), P("tp"), sharded),
        out_specs=sharded,
        check_vma=False,
    )
```

```python
import functools

import jax
import jax.numpy as jnp
from jax import lax
from jax.experimental import pallas as pl
from jax.experimental.pallas import tpu as pltpu
from jax.sharding import PartitionSpec as P

DH = 128
CONV = 4
EPS = 1e-06
SCALE = DH ** (-0.5)
RADIX = 4
PACK = 2 * DH
F32 = jnp.float32
BF16 = jnp.bfloat16


def bf(value):
    return value.astype(BF16)


def dot(left, right, dims=(1, 0)):
    return lax.dot_general(
        bf(left), bf(right), (((dims[0],), (dims[1],)), ((), ())), preferred_element_type=F32
    )


def halves(value):
    high = bf(value)
    return high, bf(value - high.astype(F32))


def dot3(left, right, dims=(1, 0)):
    left_high, left_low = halves(left)
    right_high, right_low = halves(right)
    return dot(left_high, right_high, dims) + (
        dot(left_high, right_low, dims) + dot(left_low, right_high, dims)
    )


def dot_exact(left, right):
    return lax.dot_general(
        left, right, (((1,), (0,)), ((), ())),
        precision=lax.Precision.HIGHEST, preferred_element_type=F32,
    )


def positions(shape=(DH, DH)):
    return lax.broadcasted_iota(jnp.int32, shape, 0), lax.broadcasted_iota(jnp.int32, shape, 1)


def sigmoid(value):
    return 1.0 / (1.0 + jnp.exp(-value))


def softplus(value):
    return jnp.maximum(value, 0.0) + jnp.log1p(jnp.exp(-jnp.abs(value)))


def lanes_of(pieces):
    _, lane = positions()
    result = jnp.zeros((DH, DH), F32)
    for place, piece in enumerate(pieces):
        result = jnp.where(lane == place, piece, result)
    return result


def unit_lower_inverses(stricts):
    row, col = positions()
    identity = jnp.where(row == col, 1.0, 0.0).astype(F32)
    inners = [jnp.where(row // 8 == col // 8, strict, 0.0) for strict in stricts]
    squares = [dot3(inner, inner) for inner in inners]
    results = [dot3(identity - inner, identity + square) for inner, square in zip(inners, squares)]
    fourths = [dot3(square, square) for square in squares]
    results = [dot3(result, identity + fourth) for result, fourth in zip(results, fourths)]
    size = 8
    while size < DH:
        off = (row // (2 * size) == col // (2 * size)) & (row // size != col // size)
        times = dot3 if size < 32 else dot
        products = [
            times(result, jnp.where(off, strict, 0.0)) for result, strict in zip(results, stricts)
        ]
        results = [
            result - times(product, result) for result, product in zip(results, products)
        ]
        size *= 2
    return results


def core_place():
    return lax.axis_index("tp") % 2


def part_span(part, core, width):
    return pl.ds(pl.multiple_of((2 * part + core) * width, width), width)


def narrow_sums(x_ref, narrow_ref, core):
    parts, _, width = x_ref.shape
    beta = jnp.zeros((DH, 2), F32)
    alpha = jnp.zeros((DH, 2), F32)
    for part in range(parts):
        span = part_span(part, core, width)
        beta = beta + dot(x_ref[part], narrow_ref[0, :, span], (1, 1))
        alpha = alpha + dot(x_ref[part], narrow_ref[1, :, span], (1, 1))
    return lanes_of([beta[:, 0:1], beta[:, 1:2], alpha[:, 0:1], alpha[:, 1:2]])


def first_project_kernel(
    x_ref, wq_ref, wk_ref, wv_ref, wb_ref, wa_ref, fq_ref, fk_ref, fv_ref, decay_ref, bias_ref,
    total_ref, gates_ref, taps_ref, scales_ref, rest_ref, narrow_ref,
    held_ref, filter_ref, pair_ref, sems,
):
    core = core_place()
    places = (slice(0, DH), slice(DH, 2 * DH), slice(2 * DH, 4 * DH))
    copies = []

    def fetch(source, target):
        copies.append(pltpu.make_async_copy(source, target, sems.at[len(copies)]))
        copies[-1].start()

    for place, weight in zip(places, (wq_ref, wk_ref, wv_ref)):
        fetch(weight.at[:, core], held_ref.at[:, :, place])
    fetch(wb_ref, narrow_ref.at[0])
    fetch(wa_ref, narrow_ref.at[1])
    for place, taps in zip(places, (fq_ref, fk_ref, fv_ref)):
        fetch(taps, filter_ref.at[:, place])
    fetch(decay_ref, pair_ref.at[0])
    fetch(bias_ref, pair_ref.at[1])
    ready = len(copies)
    for place, weight in zip(places, (wq_ref, wk_ref, wv_ref)):
        fetch(weight.at[:, 1 - core], rest_ref.at[:, :, place])
    for copy in copies[:ready]:
        copy.wait()
    total = jnp.zeros((DH, 4 * DH), F32)
    for part in range(x_ref.shape[0]):
        total = total + dot(x_ref[part], held_ref[part])
    total_ref[...] = total
    gates_ref[...] = narrow_sums(x_ref, narrow_ref, core)
    taps_ref[0:CONV] = filter_ref[...].astype(F32)
    taps_ref[CONV:] = jnp.zeros((8 - CONV, 4 * DH), F32)
    decay = pair_ref[0]
    bias = pair_ref[1]
    scales_ref[0] = lanes_of([0.0, 0.0, -jnp.exp(decay[:, 0:1]), -jnp.exp(decay[:, 1:2])])
    scales_ref[1] = lanes_of([0.0, 0.0, bias[:, 0:1], bias[:, 1:2]])
    for copy in copies[ready:]:
        copy.wait()


def second_project_kernel(
    x_ref, total_ref, part_ref, rest_ref, narrow_ref, proj_ref, ba_ref, tail_ref
):
    total = total_ref[...]
    for part in range(x_ref.shape[0]):
        total = total + dot(x_ref[part], rest_ref[part])
    proj_ref[...] = bf(total)
    tail_ref[...] = bf(total[DH - 16 :])
    ba_ref[...] = bf(part_ref[...] + narrow_sums(x_ref, narrow_ref, 1 - core_place()))


def gate_kernel(ba_ref, scales_ref, cols_ref, gap_ref):
    row, col = positions()
    raw = ba_ref[...].astype(F32)
    log_decay = scales_ref[0] * softplus(raw + scales_ref[1])
    lower = jnp.where(row >= col, 1.0, 0.0).astype(F32)
    cols = jnp.where(col < 2, sigmoid(raw), dot_exact(lower, log_decay))
    cols_ref[...] = cols
    rows = cols.T
    for head in range(2):
        between = cols[:, 2 + head : 3 + head] - rows[2 + head : 3 + head, :]
        gap_ref[head] = jnp.where(row >= col, jnp.exp(jnp.where(row >= col, between, 0.0)), 0.0)


def slab_kernel(
    proj_ref, tail_ref, taps_ref, cols_ref, gap_ref, grad_ref,
    send_ref, pre_ref, unit_ref, inverse_ref, mixed_ref, weighted_ref,
    back_ref, gram_ref, cross_ref, pad_ref,
):
    row, col = positions()
    pad_ref[0:8] = tail_ref[8:16].astype(F32)
    pad_ref[8 : 8 + DH] = proj_ref[...].astype(F32)
    pre = jnp.zeros((DH, 4 * DH), F32)
    for tap in range(CONV):
        start = 8 - (CONV - 1) + tap
        pre = pre + taps_ref[tap : tap + 1] * pad_ref[start : start + DH]
    pre_ref[...] = pre
    act = pre * sigmoid(pre)
    query_act, key_act = act[:, :DH], act[:, DH : 2 * DH]
    query = query_act * (lax.rsqrt(jnp.sum(query_act * query_act, 1, keepdims=True) + EPS) * SCALE)
    key = key_act * lax.rsqrt(jnp.sum(key_act * key_act, 1, keepdims=True) + EPS)
    unit_ref[0] = query
    unit_ref[1] = key
    cols = cols_ref[...]
    gram = dot3(key, key, (1, 1))
    cross = dot(query, key, (1, 1))
    gram_ref[...] = gram
    cross_ref[...] = cross
    betas = [cols[:, head : head + 1] for head in range(2)]
    inverses = unit_lower_inverses(
        [
            jnp.where(row > col, beta * gram * gap_ref[head], 0.0)
            for head, beta in enumerate(betas)
        ]
    )
    for head in range(2):
        beta = betas[head]
        inverse = inverses[head]
        cum = cols[:, 2 + head : 3 + head]
        value = act[:, (2 + head) * DH : (3 + head) * DH]
        grad = grad_ref[:, head * DH : (head + 1) * DH]
        gamma = jnp.exp(cum)
        last = cum[DH - 1 : DH, :]
        key_tail = jnp.exp(last - cum) * key
        both = dot(inverse, jnp.concatenate([beta * value, (beta * gamma) * key], axis=1))
        mixed = both[:, :DH]
        weighted = both[:, DH:]
        back = dot(cross * gap_ref[head], grad, (0, 0))
        inverse_ref[head] = bf(inverse)
        mixed_ref[head] = mixed
        weighted_ref[head] = bf(weighted)
        back_ref[head] = back
        ahead = dot(key_tail, both, (0, 0))
        lost = jnp.where(row == col, 1.0 - jnp.exp(last), 0.0) + ahead[:, DH:]
        send_ref[2 * head, 0:DH] = bf(lost)
        send_ref[2 * head, DH:] = bf(ahead[:, :DH])
        send_ref[2 * head + 1, 0:DH] = bf(lost.T)
        send_ref[2 * head + 1, DH:] = bf(
            dot(gamma * query, grad, (0, 0)) - dot(weighted, back, (0, 0))
        )


def unpack(ref):
    return ref[0:DH], ref[DH:].astype(F32)


def apply_map(later, state):
    matrix, offset = later
    return state - dot(matrix, state) + offset


def compose(later, earlier):
    matrix, offset = later
    before = earlier[0].astype(F32)
    return (
        before + matrix.astype(F32) - dot(matrix, before),
        apply_map(later, earlier[1]),
    )


def pack(total):
    return jnp.concatenate([bf(total[0]), bf(total[1])], axis=0)


def is_backward():
    return lax.axis_index("ctx") % 2 == 1


def in_order(step, backward):
    return jnp.where(backward, RADIX - 1 - step, step)


def group_kernel(got_ref, total_ref):
    backward = is_backward()
    total = unpack(got_ref.at[in_order(0, backward)])
    for step in range(1, RADIX):
        total = compose(unpack(got_ref.at[in_order(step, backward)]), total)
    total_ref[...] = pack(total)


def window_kernel(total_ref, last_ref, middle_ref, first_ref, wider_ref, before_ref):
    before = compose(unpack(last_ref), compose(unpack(middle_ref), unpack(first_ref)))
    before_ref[0:DH] = before[0]
    before_ref[DH:] = before[1]
    wider = pack(compose(unpack(total_ref), before))
    for place in range(RADIX):
        wider_ref[place] = wider


def states_kernel(rows_ref, before_ref, group_ref, out_ref):
    backward = is_backward()
    place = in_order(lax.axis_index("ctx") // (RADIX * RADIX), backward)
    state = jnp.zeros((DH, DH), F32)
    for step in range(RADIX - 1):
        later = apply_map(unpack(rows_ref.at[in_order(step, backward)]), state)
        state = jnp.where(step < place, later, state)
    state = apply_map((before_ref[0:DH], before_ref[DH:]), state)
    for step in range(RADIX):
        spot = in_order(step, backward)
        out_ref[spot] = bf(state)
        if step < RADIX - 1:
            state = apply_map(unpack(group_ref.at[spot]), state)


def gradient_kernel(
    states_ref, pre_ref, unit_ref, cols_ref, ba_ref, inverse_ref, mixed_ref, weighted_ref,
    back_ref, gap_ref, gram_ref, cross_ref, grad_ref, taps_ref, scales_ref,
    full_ref, gates_ref, halo_ref, pad_ref,
):
    row, col = positions()
    cols = cols_ref[...]
    gram = gram_ref[...]
    cross = cross_ref[...]
    query = unit_ref[0]
    key = unit_ref[1]
    pre = pre_ref[...]
    gate = sigmoid(pre)
    act = pre * gate
    slope = gate * (1.0 + pre * (1.0 - gate))
    grad_query = jnp.zeros((DH, DH), F32)
    grad_key = jnp.zeros((DH, DH), F32)
    pieces = []
    columns = jnp.zeros((DH, DH), F32)
    sides = []
    for head in range(2):
        state = states_ref[2 * head]
        after = states_ref[2 * head + 1]
        beta = cols[:, head : head + 1]
        cum = cols[:, 2 + head : 3 + head]
        gamma = jnp.exp(cum)
        last = cum[DH - 1 : DH, :]
        rest = jnp.exp(last - cum)
        value = act[:, (2 + head) * DH : (3 + head) * DH]
        grad = grad_ref[:, head * DH : (head + 1) * DH]
        gap = gap_ref[head]
        fresh = mixed_ref[head] - dot(weighted_ref[head], state)
        grad_fresh = back_ref[head] + dot(rest * key, after)
        solved = dot(inverse_ref[head], grad_fresh, (0, 0))
        grad_strict = jnp.where(row > col, -dot(solved, fresh, (1, 1)), 0.0) * gap
        grad_cross = dot(grad, fresh, (1, 1)) * gap
        grad_weighted = -dot(solved, state, (1, 1))
        grad_scaled = dot(grad, state, (1, 1))
        grad_tail = dot(fresh, after, (1, 1))
        grad_query = grad_query + gamma * grad_scaled + dot(grad_cross, key)
        grad_gram = beta * grad_strict
        grad_key = grad_key + (
            dot(grad_cross, query, (0, 0))
            + dot(grad_gram, key)
            + dot(grad_gram, key, (0, 0))
            + (beta * gamma) * grad_weighted
            + rest * grad_tail
        )
        pieces.append(beta * solved)
        by_beta = jnp.sum(grad_strict * gram, 1, keepdims=True)
        by_key = gamma * jnp.sum(grad_weighted * key, 1, keepdims=True)
        grad_beta = jnp.sum(solved * value, 1, keepdims=True) + by_key + by_beta
        by_gap = grad_gram * gram + grad_cross * cross
        by_tail = rest * jnp.sum(grad_tail * key, 1, keepdims=True)
        at_end = jnp.sum(by_tail, 0, keepdims=True) + jnp.exp(last) * jnp.sum(
            jnp.sum(state.astype(F32) * after.astype(F32), 1, keepdims=True), 0, keepdims=True
        )
        grad_cum = (
            jnp.sum(by_gap, 1, keepdims=True)
            + gamma * jnp.sum(grad_scaled * query, 1, keepdims=True)
            + beta * by_key
            - by_tail
            + jnp.where(row[:, 0:1] == DH - 1, at_end, 0.0)
        )
        columns = jnp.where(row == 2 + head, jnp.sum(by_gap, 0, keepdims=True), columns)
        sides.append((grad_beta, grad_cum))
    raw = ba_ref[...].astype(F32)
    rate = scales_ref[0]
    bias = scales_ref[1]
    sides = lanes_of([sides[0][0], sides[1][0], sides[0][1], sides[1][1]]) - columns.T
    upper = jnp.where(row <= col, 1.0, 0.0).astype(F32)
    grad_log = dot_exact(upper, sides)
    beta = cols
    gates_ref[...] = bf(
        jnp.where(
            col < 2,
            sides * beta * (1.0 - beta),
            jnp.where(col < 4, grad_log * rate * sigmoid(raw + bias), 0.0),
        )
    )
    key_act = act[:, DH : 2 * DH]
    query_act = act[:, :DH]
    query_size = lax.rsqrt(jnp.sum(query_act * query_act, 1, keepdims=True) + EPS)
    key_size = lax.rsqrt(jnp.sum(key_act * key_act, 1, keepdims=True) + EPS)
    query_dir = query_act * query_size
    grad_query = grad_query * SCALE
    grad_query = query_size * (
        grad_query - query_dir * jnp.sum(grad_query * query_dir, 1, keepdims=True)
    )
    grad_key = key_size * (grad_key - key * jnp.sum(grad_key * key, 1, keepdims=True))
    pad_ref[0:8] = jnp.zeros((8, 4 * DH), F32)
    pad_ref[8 + DH :] = jnp.zeros((8, 4 * DH), F32)
    for place, piece in enumerate([grad_query, grad_key] + pieces):
        span = slice(place * DH, (place + 1) * DH)
        pad_ref[8 : 8 + DH, span] = piece * slope[:, span]
    total = jnp.zeros((8 + DH, 4 * DH), F32)
    for tap in range(CONV):
        start = CONV - 1 - tap
        total = total + taps_ref[tap : tap + 1] * pad_ref[start : start + 8 + DH]
    halo_ref[...] = total[0:8]
    full_ref[...] = total[8:]


def spread_kernel(
    other, full_ref, halo_ref, gates_ref, wq_ref, wk_ref, wv_ref, wb_ref, wa_ref, out_ref
):
    core = core_place()
    core = 1 - core if other else core
    full = full_ref[...]
    end = full[DH - 8 :] + halo_ref[...]
    grads = bf(jnp.concatenate([full[: DH - 8], end], axis=0))
    gates = gates_ref[...]
    parts, _, width = out_ref.shape
    for part in range(parts):
        span = part_span(part, core, width)
        total = dot(grads[:, :DH], wq_ref[span, :], (1, 1))
        total = total + dot(grads[:, DH : 2 * DH], wk_ref[span, :], (1, 1))
        total = total + dot(grads[:, 2 * DH :], wv_ref[span, :], (1, 1))
        total = total + dot(gates[:, 0:2], wb_ref[:, span])
        total = total + dot(gates[:, 2:4], wa_ref[:, span])
        out_ref[part] = total.astype(out_ref.dtype)


def merge_kernel(kept_ref, got_ref, out_ref):
    out_ref[...] = bf(kept_ref[...] + got_ref[...].astype(F32))


def total_kernel(shares_ref, out_ref):
    total = shares_ref[0].astype(F32)
    for part in range(1, shares_ref.shape[0]):
        total = total + shares_ref[part].astype(F32)
    out_ref[...] = bf(total)


def call(kernel, outs, scratch=(), specs=None):
    extra = {} if specs is None else {"in_specs": specs}
    return pl.pallas_call(
        kernel,
        out_shape=[jax.ShapeDtypeStruct(shape, kind) for shape, kind in outs],
        scratch_shapes=list(scratch),
        compiler_params=pltpu.CompilerParams(vmem_limit_bytes=48 * 1024 * 1024),
        **extra,
    )


def stay(array):
    return pltpu.with_memory_space_constraint(array, pltpu.HBM)


def first_project(mine, weights, filters, decay, bias):
    parts, rows, width = mine.shape
    inside = pl.BlockSpec(memory_space=pltpu.VMEM)
    outside = pl.BlockSpec(memory_space=pltpu.HBM)
    model = 2 * parts * width
    wide = [weight.reshape(parts, 2, width, weight.shape[1]) for weight in weights[:3]]
    return call(
        first_project_kernel,
        [
            ((rows, 4 * DH), F32), ((DH, DH), F32), ((8, 4 * DH), F32), ((2, DH, DH), F32),
            ((parts, width, 4 * DH), BF16), ((2, 2, model), BF16),
        ],
        [
            pltpu.VMEM((parts, width, 4 * DH), BF16),
            pltpu.VMEM((CONV, 4 * DH), BF16),
            pltpu.VMEM((2, 1, 2), F32),
            pltpu.SemaphoreType.DMA((13,)),
        ],
        [inside] + [outside] * 10,
    )(mine, *[stay(array) for array in (*wide, *weights[3:], *filters, decay, bias)])


def second_project(other, total, part, rest, narrow):
    return call(
        second_project_kernel,
        [((DH, 4 * DH), BF16), ((DH, DH), BF16), ((16, 4 * DH), BF16)],
    )(other, total, part, rest, narrow)


def slab(proj, tail, taps, cols, gap, grad):
    square = (DH, DH)
    return call(
        slab_kernel,
        [
            ((4, PACK, DH), BF16), ((DH, 4 * DH), F32), ((2,) + square, F32),
            ((2,) + square, BF16), ((2,) + square, F32), ((2,) + square, BF16),
            ((2,) + square, F32), (square, F32), (square, F32),
        ],
        [pltpu.VMEM((8 + DH, 4 * DH), F32)],
    )(proj, tail, taps, cols, gap, grad)


def gradient(states, kept, cols, gap, gates, taps, scales, grad):
    pre, unit, inverse, mixed, weighted, back, gram, cross = kept
    return call(
        gradient_kernel,
        [((DH, 4 * DH), F32), ((DH, DH), BF16), ((8, 4 * DH), F32)],
        [pltpu.VMEM((16 + DH, 4 * DH), F32)],
    )(
        states, pre, unit, cols, gates, inverse, mixed, weighted, back, gap, gram, cross,
        grad, taps, scales,
    )


def spread(full, halo, gates, weights, parts, other):
    width = weights[0].shape[0] // (2 * parts)
    return call(
        functools.partial(spread_kernel, other),
        [((parts, DH, width), BF16 if other else F32)],
    )(full, halo, gates, *weights)[0]


def local(
    inputs, query_weight, key_weight, value_weight, beta_weight, alpha_weight,
    query_filter, key_filter, value_filter, decay_log, step_bias, grad_core,
):
    weights = (query_weight, key_weight, value_weight, beta_weight.T, alpha_weight.T)
    filters = (query_filter, key_filter, value_filter)
    decay = decay_log.reshape(1, 2)
    bias = step_bias.reshape(1, 2)
    count = lax.axis_size("ctx")
    parts = lax.axis_size("tp")
    slabs = range(count)
    group = [[s for s in slabs if s // RADIX == g] for g in range(count // RADIX)]
    rank = [[s for s in slabs if s % 16 == z] for z in range(16)]

    def exchange(value, groups):
        return lax.all_to_all(value, "ctx", 0, 0, axis_index_groups=groups)

    def onward(value, distance):
        steps = [(s, s - distance if s % 2 else s + distance) for s in slabs]
        return lax.ppermute(value, "ctx", [(s, t) for s, t in steps if 0 <= t < count])

    chips = [[2 * chip + core for chip in range(parts // 2)] for core in range(2)]

    def across(value):
        return lax.all_to_all(value, "tp", 0, 0, axis_index_groups=chips)

    def between(value):
        return lax.ppermute(value, "tp", [(t, t ^ 1) for t in range(parts)])

    mine = across(jnp.broadcast_to(inputs[None], (parts // 2,) + inputs.shape))
    other = between(mine)
    total, part, taps, scales, rest, narrow = first_project(mine, weights, filters, decay, bias)
    proj, gates, tail = second_project(other, total, part, rest, narrow)
    tail = lax.ppermute(tail, "ctx", [(s, s + 1) for s in range(count - 1)])
    square = (DH, DH)
    cols, gap = call(gate_kernel, [(square, F32), ((2,) + square, F32)])(gates, scales)
    send, *kept = slab(proj, tail, taps, cols, gap, grad_core)
    got = exchange(send, group)
    total = call(group_kernel, [((PACK, DH), BF16)])(got)[0]
    last = onward(total, RADIX)
    earlier = [last, onward(last, RADIX), onward(total, 3 * RADIX)]
    total, before = call(
        window_kernel, [((RADIX, PACK, DH), BF16), ((PACK, DH), F32)]
    )(total, *earlier)
    states = call(states_kernel, [((RADIX, DH, DH), BF16)])(exchange(total, rank), before, got)[0]
    states = exchange(states, group)
    full, grad_gates, halo = gradient(
        states, kept, cols, gap, gates, taps, scales, grad_core
    )
    halo = lax.ppermute(halo, "ctx", [(s + 1, s) for s in range(count - 1)])
    given = between(spread(full, halo, grad_gates, weights, parts // 2, True))
    kept = spread(full, halo, grad_gates, weights, parts // 2, False)
    shares = call(merge_kernel, [(given.shape, BF16)])(kept, given)[0]
    return call(total_kernel, [(shares.shape[1:], BF16)])(across(shares))[0]


def solution(mesh):
    sharded = P("ctx", "tp")
    kept = P(None, "tp")
    return jax.shard_map(
        local,
        mesh=mesh,
        in_specs=(sharded,) + (kept,) * 8 + (P("tp"), P("tp"), sharded),
        out_specs=sharded,
        check_vma=False,
    )
```

```python
import functools

import jax
import jax.numpy as jnp
from jax import lax
from jax.experimental import pallas as pl
from jax.experimental.pallas import tpu as pltpu
from jax.sharding import PartitionSpec as P

DH = 128
CONV = 4
EPS = 1e-06
SCALE = DH ** (-0.5)
RADIX = 4
PACK = 2 * DH
F32 = jnp.float32
BF16 = jnp.bfloat16


def bf(value):
    return value.astype(BF16)


def dot(left, right, dims=(1, 0)):
    return lax.dot_general(
        bf(left), bf(right), (((dims[0],), (dims[1],)), ((), ())), preferred_element_type=F32
    )


def halves(value):
    high = bf(value)
    return high, bf(value - high.astype(F32))


def dot3(left, right, dims=(1, 0)):
    left_high, left_low = halves(left)
    right_high, right_low = halves(right)
    return dot(left_high, right_high, dims) + (
        dot(left_high, right_low, dims) + dot(left_low, right_high, dims)
    )


def dot_exact(left, right):
    return lax.dot_general(
        left, right, (((1,), (0,)), ((), ())),
        precision=lax.Precision.HIGHEST, preferred_element_type=F32,
    )


def positions(shape=(DH, DH)):
    return lax.broadcasted_iota(jnp.int32, shape, 0), lax.broadcasted_iota(jnp.int32, shape, 1)


def sigmoid(value):
    return 1.0 / (1.0 + jnp.exp(-value))


def softplus(value):
    return jnp.maximum(value, 0.0) + jnp.log1p(jnp.exp(-jnp.abs(value)))


def lanes_of(pieces):
    _, lane = positions()
    result = jnp.zeros((DH, DH), F32)
    for place, piece in enumerate(pieces):
        result = jnp.where(lane == place, piece, result)
    return result


def unit_lower_inverses(stricts):
    row, col = positions()
    identity = jnp.where(row == col, 1.0, 0.0).astype(F32)
    inners = [jnp.where(row // 8 == col // 8, strict, 0.0) for strict in stricts]
    squares = [dot3(inner, inner) for inner in inners]
    results = [dot3(identity - inner, identity + square) for inner, square in zip(inners, squares)]
    fourths = [dot3(square, square) for square in squares]
    results = [dot3(result, identity + fourth) for result, fourth in zip(results, fourths)]
    size = 8
    while size < DH:
        off = (row // (2 * size) == col // (2 * size)) & (row // size != col // size)
        times = dot3 if size < 32 else dot
        products = [
            times(result, jnp.where(off, strict, 0.0)) for result, strict in zip(results, stricts)
        ]
        results = [
            result - times(product, result) for result, product in zip(results, products)
        ]
        size *= 2
    return results


def core_place():
    return lax.axis_index("tp") % 2


def part_span(part, core, width):
    return pl.ds(pl.multiple_of((2 * part + core) * width, width), width)


def narrow_sums(x_ref, narrow_ref, core):
    parts, _, width = x_ref.shape
    beta = jnp.zeros((DH, 2), F32)
    alpha = jnp.zeros((DH, 2), F32)
    for part in range(parts):
        span = part_span(part, core, width)
        beta = beta + dot(x_ref[part], narrow_ref[0, :, span], (1, 1))
        alpha = alpha + dot(x_ref[part], narrow_ref[1, :, span], (1, 1))
    return lanes_of([beta[:, 0:1], beta[:, 1:2], alpha[:, 0:1], alpha[:, 1:2]])


def first_project_kernel(
    x_ref, wq_ref, wk_ref, wv_ref, wb_ref, wa_ref, fq_ref, fk_ref, fv_ref, decay_ref, bias_ref,
    total_ref, gates_ref, taps_ref, scales_ref, rest_ref, narrow_ref,
    held_ref, filter_ref, pair_ref, sems,
):
    core = core_place()
    places = (slice(0, DH), slice(DH, 2 * DH), slice(2 * DH, 4 * DH))
    copies = []

    def fetch(source, target):
        copies.append(pltpu.make_async_copy(source, target, sems.at[len(copies)]))
        copies[-1].start()

    for place, weight in zip(places, (wq_ref, wk_ref, wv_ref)):
        fetch(weight.at[:, core], held_ref.at[:, :, place])
    fetch(wb_ref, narrow_ref.at[0])
    fetch(wa_ref, narrow_ref.at[1])
    for place, taps in zip(places, (fq_ref, fk_ref, fv_ref)):
        fetch(taps, filter_ref.at[:, place])
    fetch(decay_ref, pair_ref.at[0])
    fetch(bias_ref, pair_ref.at[1])
    ready = len(copies)
    for place, weight in zip(places, (wq_ref, wk_ref, wv_ref)):
        fetch(weight.at[:, 1 - core], rest_ref.at[:, :, place])
    for copy in copies[:ready]:
        copy.wait()
    total = jnp.zeros((DH, 4 * DH), F32)
    for part in range(x_ref.shape[0]):
        total = total + dot(x_ref[part], held_ref[part])
    total_ref[...] = total
    gates_ref[...] = narrow_sums(x_ref, narrow_ref, core)
    taps_ref[0:CONV] = filter_ref[...].astype(F32)
    taps_ref[CONV:] = jnp.zeros((8 - CONV, 4 * DH), F32)
    decay = pair_ref[0]
    bias = pair_ref[1]
    scales_ref[0] = lanes_of([0.0, 0.0, -jnp.exp(decay[:, 0:1]), -jnp.exp(decay[:, 1:2])])
    scales_ref[1] = lanes_of([0.0, 0.0, bias[:, 0:1], bias[:, 1:2]])
    for copy in copies[ready:]:
        copy.wait()


def second_project_kernel(
    x_ref, total_ref, part_ref, rest_ref, narrow_ref, proj_ref, ba_ref, tail_ref
):
    total = total_ref[...]
    for part in range(x_ref.shape[0]):
        total = total + dot(x_ref[part], rest_ref[part])
    proj_ref[...] = bf(total)
    tail_ref[...] = bf(total[DH - 16 :])
    ba_ref[...] = bf(part_ref[...] + narrow_sums(x_ref, narrow_ref, 1 - core_place()))


def gate_kernel(ba_ref, scales_ref, cols_ref, gap_ref):
    row, col = positions()
    raw = ba_ref[...].astype(F32)
    log_decay = scales_ref[0] * softplus(raw + scales_ref[1])
    lower = jnp.where(row >= col, 1.0, 0.0).astype(F32)
    cols = jnp.where(col < 2, sigmoid(raw), dot_exact(lower, log_decay))
    cols_ref[...] = cols
    rows = cols.T
    for head in range(2):
        between = cols[:, 2 + head : 3 + head] - rows[2 + head : 3 + head, :]
        gap_ref[head] = jnp.where(row >= col, jnp.exp(jnp.where(row >= col, between, 0.0)), 0.0)


def slab_kernel(
    proj_ref, tail_ref, taps_ref, cols_ref, gap_ref, grad_ref,
    send_ref, pre_ref, unit_ref, inverse_ref, mixed_ref, weighted_ref,
    back_ref, gram_ref, cross_ref, pad_ref,
):
    row, col = positions()
    pad_ref[0:8] = tail_ref[8:16].astype(F32)
    pad_ref[8 : 8 + DH] = proj_ref[...].astype(F32)
    pre = jnp.zeros((DH, 4 * DH), F32)
    for tap in range(CONV):
        start = 8 - (CONV - 1) + tap
        pre = pre + taps_ref[tap : tap + 1] * pad_ref[start : start + DH]
    pre_ref[...] = pre
    act = pre * sigmoid(pre)
    query_act, key_act = act[:, :DH], act[:, DH : 2 * DH]
    query = query_act * (lax.rsqrt(jnp.sum(query_act * query_act, 1, keepdims=True) + EPS) * SCALE)
    key = key_act * lax.rsqrt(jnp.sum(key_act * key_act, 1, keepdims=True) + EPS)
    unit_ref[0] = query
    unit_ref[1] = key
    cols = cols_ref[...]
    gram = dot3(key, key, (1, 1))
    cross = dot(query, key, (1, 1))
    gram_ref[...] = gram
    cross_ref[...] = cross
    betas = [cols[:, head : head + 1] for head in range(2)]
    inverses = unit_lower_inverses(
        [
            jnp.where(row > col, beta * gram * gap_ref[head], 0.0)
            for head, beta in enumerate(betas)
        ]
    )
    for head in range(2):
        beta = betas[head]
        inverse = inverses[head]
        cum = cols[:, 2 + head : 3 + head]
        value = act[:, (2 + head) * DH : (3 + head) * DH]
        grad = grad_ref[:, head * DH : (head + 1) * DH]
        gamma = jnp.exp(cum)
        last = cum[DH - 1 : DH, :]
        key_tail = jnp.exp(last - cum) * key
        both = dot(inverse, jnp.concatenate([beta * value, (beta * gamma) * key], axis=1))
        mixed = both[:, :DH]
        weighted = both[:, DH:]
        back = dot(cross * gap_ref[head], grad, (0, 0))
        inverse_ref[head] = bf(inverse)
        mixed_ref[head] = mixed
        weighted_ref[head] = bf(weighted)
        back_ref[head] = back
        ahead = dot(key_tail, both, (0, 0))
        lost = jnp.where(row == col, 1.0 - jnp.exp(last), 0.0) + ahead[:, DH:]
        place = 2 * head + core_place()
        send_ref[place, 0:DH] = bf(lost)
        send_ref[place, DH:] = bf(ahead[:, :DH])
        place = 2 * head + 1 - core_place()
        send_ref[place, 0:DH] = bf(lost.T)
        send_ref[place, DH:] = bf(
            dot(gamma * query, grad, (0, 0)) - dot(weighted, back, (0, 0))
        )


def unpack(ref):
    return ref[0:DH], ref[DH:].astype(F32)


def apply_map(later, state):
    matrix, offset = later
    return state - dot(matrix, state) + offset


def compose(later, earlier):
    matrix, offset = later
    before = earlier[0].astype(F32)
    return (
        before + matrix.astype(F32) - dot(matrix, before),
        apply_map(later, earlier[1]),
    )


def pack(total):
    return jnp.concatenate([bf(total[0]), bf(total[1])], axis=0)


def is_backward():
    return (lax.axis_index("ctx") + core_place()) % 2 == 1


def in_order(step, backward):
    return jnp.where(backward, RADIX - 1 - step, step)


def group_kernel(got_ref, total_ref):
    backward = is_backward()
    total = unpack(got_ref.at[in_order(0, backward)])
    for step in range(1, RADIX):
        total = compose(unpack(got_ref.at[in_order(step, backward)]), total)
    total_ref[...] = pack(total)


def window_kernel(total_ref, last_ref, middle_ref, first_ref, wider_ref, before_ref):
    before = compose(unpack(last_ref), compose(unpack(middle_ref), unpack(first_ref)))
    before_ref[0:DH] = before[0]
    before_ref[DH:] = before[1]
    wider = pack(compose(unpack(total_ref), before))
    for place in range(RADIX):
        wider_ref[place] = wider


def states_kernel(rows_ref, before_ref, group_ref, out_ref):
    backward = is_backward()
    place = in_order(lax.axis_index("ctx") // (RADIX * RADIX), backward)
    state = jnp.zeros((DH, DH), F32)
    for step in range(RADIX - 1):
        later = apply_map(unpack(rows_ref.at[in_order(step, backward)]), state)
        state = jnp.where(step < place, later, state)
    state = apply_map((before_ref[0:DH], before_ref[DH:]), state)
    for step in range(RADIX):
        spot = in_order(step, backward)
        out_ref[spot] = bf(state)
        if step < RADIX - 1:
            state = apply_map(unpack(group_ref.at[spot]), state)


def gradient_kernel(
    states_ref, pre_ref, unit_ref, cols_ref, ba_ref, inverse_ref, mixed_ref, weighted_ref,
    back_ref, gap_ref, gram_ref, cross_ref, grad_ref, taps_ref, scales_ref,
    full_ref, gates_ref, halo_ref, pad_ref,
):
    row, col = positions()
    cols = cols_ref[...]
    gram = gram_ref[...]
    cross = cross_ref[...]
    query = unit_ref[0]
    key = unit_ref[1]
    pre = pre_ref[...]
    gate = sigmoid(pre)
    act = pre * gate
    slope = gate * (1.0 + pre * (1.0 - gate))
    grad_query = jnp.zeros((DH, DH), F32)
    grad_key = jnp.zeros((DH, DH), F32)
    pieces = []
    columns = jnp.zeros((DH, DH), F32)
    sides = []
    for head in range(2):
        state = states_ref[2 * head + core_place()]
        after = states_ref[2 * head + 1 - core_place()]
        beta = cols[:, head : head + 1]
        cum = cols[:, 2 + head : 3 + head]
        gamma = jnp.exp(cum)
        last = cum[DH - 1 : DH, :]
        rest = jnp.exp(last - cum)
        value = act[:, (2 + head) * DH : (3 + head) * DH]
        grad = grad_ref[:, head * DH : (head + 1) * DH]
        gap = gap_ref[head]
        fresh = mixed_ref[head] - dot(weighted_ref[head], state)
        grad_fresh = back_ref[head] + dot(rest * key, after)
        solved = dot(inverse_ref[head], grad_fresh, (0, 0))
        grad_strict = jnp.where(row > col, -dot(solved, fresh, (1, 1)), 0.0) * gap
        grad_cross = dot(grad, fresh, (1, 1)) * gap
        grad_weighted = -dot(solved, state, (1, 1))
        grad_scaled = dot(grad, state, (1, 1))
        grad_tail = dot(fresh, after, (1, 1))
        grad_query = grad_query + gamma * grad_scaled + dot(grad_cross, key)
        grad_gram = beta * grad_strict
        grad_key = grad_key + (
            dot(grad_cross, query, (0, 0))
            + dot(grad_gram, key)
            + dot(grad_gram, key, (0, 0))
            + (beta * gamma) * grad_weighted
            + rest * grad_tail
        )
        pieces.append(beta * solved)
        by_beta = jnp.sum(grad_strict * gram, 1, keepdims=True)
        by_key = gamma * jnp.sum(grad_weighted * key, 1, keepdims=True)
        grad_beta = jnp.sum(solved * value, 1, keepdims=True) + by_key + by_beta
        by_gap = grad_gram * gram + grad_cross * cross
        by_tail = rest * jnp.sum(grad_tail * key, 1, keepdims=True)
        at_end = jnp.sum(by_tail, 0, keepdims=True) + jnp.exp(last) * jnp.sum(
            jnp.sum(state.astype(F32) * after.astype(F32), 1, keepdims=True), 0, keepdims=True
        )
        grad_cum = (
            jnp.sum(by_gap, 1, keepdims=True)
            + gamma * jnp.sum(grad_scaled * query, 1, keepdims=True)
            + beta * by_key
            - by_tail
            + jnp.where(row[:, 0:1] == DH - 1, at_end, 0.0)
        )
        columns = jnp.where(row == 2 + head, jnp.sum(by_gap, 0, keepdims=True), columns)
        sides.append((grad_beta, grad_cum))
    raw = ba_ref[...].astype(F32)
    rate = scales_ref[0]
    bias = scales_ref[1]
    sides = lanes_of([sides[0][0], sides[1][0], sides[0][1], sides[1][1]]) - columns.T
    upper = jnp.where(row <= col, 1.0, 0.0).astype(F32)
    grad_log = dot_exact(upper, sides)
    beta = cols
    gates_ref[...] = bf(
        jnp.where(
            col < 2,
            sides * beta * (1.0 - beta),
            jnp.where(col < 4, grad_log * rate * sigmoid(raw + bias), 0.0),
        )
    )
    key_act = act[:, DH : 2 * DH]
    query_act = act[:, :DH]
    query_size = lax.rsqrt(jnp.sum(query_act * query_act, 1, keepdims=True) + EPS)
    key_size = lax.rsqrt(jnp.sum(key_act * key_act, 1, keepdims=True) + EPS)
    query_dir = query_act * query_size
    grad_query = grad_query * SCALE
    grad_query = query_size * (
        grad_query - query_dir * jnp.sum(grad_query * query_dir, 1, keepdims=True)
    )
    grad_key = key_size * (grad_key - key * jnp.sum(grad_key * key, 1, keepdims=True))
    pad_ref[0:8] = jnp.zeros((8, 4 * DH), F32)
    pad_ref[8 + DH :] = jnp.zeros((8, 4 * DH), F32)
    for place, piece in enumerate([grad_query, grad_key] + pieces):
        span = slice(place * DH, (place + 1) * DH)
        pad_ref[8 : 8 + DH, span] = piece * slope[:, span]
    total = jnp.zeros((8 + DH, 4 * DH), F32)
    for tap in range(CONV):
        start = CONV - 1 - tap
        total = total + taps_ref[tap : tap + 1] * pad_ref[start : start + 8 + DH]
    halo_ref[...] = total[0:8]
    full_ref[...] = total[8:]


def spread_kernel(
    other, full_ref, halo_ref, gates_ref, wq_ref, wk_ref, wv_ref, wb_ref, wa_ref, out_ref
):
    core = core_place()
    core = 1 - core if other else core
    full = full_ref[...]
    end = full[DH - 8 :] + halo_ref[...]
    grads = bf(jnp.concatenate([full[: DH - 8], end], axis=0))
    gates = gates_ref[...]
    parts, _, width = out_ref.shape
    for part in range(parts):
        span = part_span(part, core, width)
        total = dot(grads[:, :DH], wq_ref[span, :], (1, 1))
        total = total + dot(grads[:, DH : 2 * DH], wk_ref[span, :], (1, 1))
        total = total + dot(grads[:, 2 * DH :], wv_ref[span, :], (1, 1))
        total = total + dot(gates[:, 0:2], wb_ref[:, span])
        total = total + dot(gates[:, 2:4], wa_ref[:, span])
        out_ref[part] = total.astype(out_ref.dtype)


def merge_kernel(kept_ref, got_ref, out_ref):
    out_ref[...] = bf(kept_ref[...] + got_ref[...].astype(F32))


def total_kernel(shares_ref, out_ref):
    total = shares_ref[0].astype(F32)
    for part in range(1, shares_ref.shape[0]):
        total = total + shares_ref[part].astype(F32)
    out_ref[...] = bf(total)


def call(kernel, outs, scratch=(), specs=None):
    extra = {} if specs is None else {"in_specs": specs}
    return pl.pallas_call(
        kernel,
        out_shape=[jax.ShapeDtypeStruct(shape, kind) for shape, kind in outs],
        scratch_shapes=list(scratch),
        compiler_params=pltpu.CompilerParams(vmem_limit_bytes=48 * 1024 * 1024),
        **extra,
    )


def stay(array):
    return pltpu.with_memory_space_constraint(array, pltpu.HBM)


def first_project(mine, weights, filters, decay, bias):
    parts, rows, width = mine.shape
    inside = pl.BlockSpec(memory_space=pltpu.VMEM)
    outside = pl.BlockSpec(memory_space=pltpu.HBM)
    model = 2 * parts * width
    wide = [weight.reshape(parts, 2, width, weight.shape[1]) for weight in weights[:3]]
    return call(
        first_project_kernel,
        [
            ((rows, 4 * DH), F32), ((DH, DH), F32), ((8, 4 * DH), F32), ((2, DH, DH), F32),
            ((parts, width, 4 * DH), BF16), ((2, 2, model), BF16),
        ],
        [
            pltpu.VMEM((parts, width, 4 * DH), BF16),
            pltpu.VMEM((CONV, 4 * DH), BF16),
            pltpu.VMEM((2, 1, 2), F32),
            pltpu.SemaphoreType.DMA((13,)),
        ],
        [inside] + [outside] * 10,
    )(mine, *[stay(array) for array in (*wide, *weights[3:], *filters, decay, bias)])


def second_project(other, total, part, rest, narrow):
    return call(
        second_project_kernel,
        [((DH, 4 * DH), BF16), ((DH, DH), BF16), ((16, 4 * DH), BF16)],
    )(other, total, part, rest, narrow)


def slab(proj, tail, taps, cols, gap, grad):
    square = (DH, DH)
    return call(
        slab_kernel,
        [
            ((4, PACK, DH), BF16), ((DH, 4 * DH), F32), ((2,) + square, F32),
            ((2,) + square, BF16), ((2,) + square, F32), ((2,) + square, BF16),
            ((2,) + square, F32), (square, F32), (square, F32),
        ],
        [pltpu.VMEM((8 + DH, 4 * DH), F32)],
    )(proj, tail, taps, cols, gap, grad)


def gradient(states, kept, cols, gap, gates, taps, scales, grad):
    pre, unit, inverse, mixed, weighted, back, gram, cross = kept
    return call(
        gradient_kernel,
        [((DH, 4 * DH), F32), ((DH, DH), BF16), ((8, 4 * DH), F32)],
        [pltpu.VMEM((16 + DH, 4 * DH), F32)],
    )(
        states, pre, unit, cols, gates, inverse, mixed, weighted, back, gap, gram, cross,
        grad, taps, scales,
    )


def spread(full, halo, gates, weights, parts, other):
    width = weights[0].shape[0] // (2 * parts)
    return call(
        functools.partial(spread_kernel, other),
        [((parts, DH, width), BF16 if other else F32)],
    )(full, halo, gates, *weights)[0]


def local(
    inputs, query_weight, key_weight, value_weight, beta_weight, alpha_weight,
    query_filter, key_filter, value_filter, decay_log, step_bias, grad_core,
):
    weights = (query_weight, key_weight, value_weight, beta_weight.T, alpha_weight.T)
    filters = (query_filter, key_filter, value_filter)
    decay = decay_log.reshape(1, 2)
    bias = step_bias.reshape(1, 2)
    count = lax.axis_size("ctx")
    parts = lax.axis_size("tp")
    slabs = range(count)
    group = [[s for s in slabs if s // RADIX == g] for g in range(count // RADIX)]
    rank = [[s for s in slabs if s % 16 == z] for z in range(16)]

    def exchange(value, groups):
        return lax.all_to_all(value, "ctx", 0, 0, axis_index_groups=groups)

    def onward(value, distance):
        steps = [
            (s, s - distance if (s + t) % 2 else s + distance, t)
            for s in slabs for t in range(parts)
        ]
        pairs = [(s * parts + t, d * parts + t) for s, d, t in steps if 0 <= d < count]
        return lax.ppermute(value, ("ctx", "tp"), pairs)

    chips = [[2 * chip + core for chip in range(parts // 2)] for core in range(2)]

    def across(value):
        return lax.all_to_all(value, "tp", 0, 0, axis_index_groups=chips)

    def between(value):
        return lax.ppermute(value, "tp", [(t, t ^ 1) for t in range(parts)])

    mine = across(jnp.broadcast_to(inputs[None], (parts // 2,) + inputs.shape))
    other = between(mine)
    total, part, taps, scales, rest, narrow = first_project(mine, weights, filters, decay, bias)
    proj, gates, tail = second_project(other, total, part, rest, narrow)
    tail = lax.ppermute(tail, "ctx", [(s, s + 1) for s in range(count - 1)])
    square = (DH, DH)
    cols, gap = call(gate_kernel, [(square, F32), ((2,) + square, F32)])(gates, scales)
    send, *kept = slab(proj, tail, taps, cols, gap, grad_core)
    got = exchange(send, group)
    total = call(group_kernel, [((PACK, DH), BF16)])(got)[0]
    last = onward(total, RADIX)
    earlier = [last, onward(last, RADIX), onward(total, 3 * RADIX)]
    total, before = call(
        window_kernel, [((RADIX, PACK, DH), BF16), ((PACK, DH), F32)]
    )(total, *earlier)
    states = call(states_kernel, [((RADIX, DH, DH), BF16)])(exchange(total, rank), before, got)[0]
    states = exchange(states, group)
    full, grad_gates, halo = gradient(
        states, kept, cols, gap, gates, taps, scales, grad_core
    )
    halo = lax.ppermute(halo, "ctx", [(s + 1, s) for s in range(count - 1)])
    given = between(spread(full, halo, grad_gates, weights, parts // 2, True))
    kept = spread(full, halo, grad_gates, weights, parts // 2, False)
    shares = call(merge_kernel, [(given.shape, BF16)])(kept, given)[0]
    return call(total_kernel, [(shares.shape[1:], BF16)])(across(shares))[0]


def solution(mesh):
    sharded = P("ctx", "tp")
    kept = P(None, "tp")
    return jax.shard_map(
        local,
        mesh=mesh,
        in_specs=(sharded,) + (kept,) * 8 + (P("tp"), P("tp"), sharded),
        out_specs=sharded,
        check_vma=False,
    )
```

```python
import functools

import jax
import jax.numpy as jnp
from jax import lax
from jax.experimental import pallas as pl
from jax.experimental.pallas import tpu as pltpu
from jax.sharding import PartitionSpec as P

DH = 128
CONV = 4
EPS = 1e-06
SCALE = DH ** (-0.5)
RADIX = 4
PACK = 2 * DH
F32 = jnp.float32
BF16 = jnp.bfloat16


def bf(value):
    return value.astype(BF16)


def dot(left, right, dims=(1, 0)):
    return lax.dot_general(
        bf(left), bf(right), (((dims[0],), (dims[1],)), ((), ())), preferred_element_type=F32
    )


def halves(value):
    high = bf(value)
    return high, bf(value - high.astype(F32))


def dot3(left, right, dims=(1, 0)):
    left_high, left_low = halves(left)
    right_high, right_low = halves(right)
    return dot(left_high, right_high, dims) + (
        dot(left_high, right_low, dims) + dot(left_low, right_high, dims)
    )


def dot_exact(left, right):
    return lax.dot_general(
        left, right, (((1,), (0,)), ((), ())),
        precision=lax.Precision.HIGHEST, preferred_element_type=F32,
    )


def positions(shape=(DH, DH)):
    return lax.broadcasted_iota(jnp.int32, shape, 0), lax.broadcasted_iota(jnp.int32, shape, 1)


def sigmoid(value):
    return 1.0 / (1.0 + jnp.exp(-value))


def softplus(value):
    return jnp.maximum(value, 0.0) + jnp.log1p(jnp.exp(-jnp.abs(value)))


def lanes_of(pieces):
    _, lane = positions()
    result = jnp.zeros((DH, DH), F32)
    for place, piece in enumerate(pieces):
        result = jnp.where(lane == place, piece, result)
    return result


def unit_lower_inverses(stricts):
    row, col = positions()
    identity = jnp.where(row == col, 1.0, 0.0).astype(F32)
    inners = [jnp.where(row // 8 == col // 8, strict, 0.0) for strict in stricts]
    squares = [dot3(inner, inner) for inner in inners]
    results = [dot3(identity - inner, identity + square) for inner, square in zip(inners, squares)]
    fourths = [dot3(square, square) for square in squares]
    results = [dot3(result, identity + fourth) for result, fourth in zip(results, fourths)]
    size = 8
    while size < DH:
        off = (row // (2 * size) == col // (2 * size)) & (row // size != col // size)
        times = dot3 if size < 32 else dot
        products = [
            times(result, jnp.where(off, strict, 0.0)) for result, strict in zip(results, stricts)
        ]
        results = [
            result - times(product, result) for result, product in zip(results, products)
        ]
        size *= 2
    return results


def core_place():
    return lax.axis_index("tp") % 2


def part_span(part, core, width):
    return pl.ds(pl.multiple_of((2 * part + core) * width, width), width)


def narrow_sums(x_ref, narrow_ref, core):
    parts, _, width = x_ref.shape
    beta = jnp.zeros((DH, 2), F32)
    alpha = jnp.zeros((DH, 2), F32)
    for part in range(parts):
        span = part_span(part, core, width)
        beta = beta + dot(x_ref[part], narrow_ref[0, :, span], (1, 1))
        alpha = alpha + dot(x_ref[part], narrow_ref[1, :, span], (1, 1))
    return lanes_of([beta[:, 0:1], beta[:, 1:2], alpha[:, 0:1], alpha[:, 1:2]])


def first_project_kernel(
    x_ref, wq_ref, wk_ref, wv_ref, wb_ref, wa_ref, fq_ref, fk_ref, fv_ref, decay_ref, bias_ref,
    total_ref, gates_ref, taps_ref, scales_ref, rest_ref, narrow_ref,
    held_ref, filter_ref, pair_ref, sems,
):
    core = core_place()
    places = (slice(0, DH), slice(DH, 2 * DH), slice(2 * DH, 4 * DH))
    copies = []

    def fetch(source, target):
        copies.append(pltpu.make_async_copy(source, target, sems.at[len(copies)]))
        copies[-1].start()

    for place, weight in zip(places, (wq_ref, wk_ref, wv_ref)):
        fetch(weight.at[:, core], held_ref.at[:, :, place])
    fetch(wb_ref, narrow_ref.at[0])
    fetch(wa_ref, narrow_ref.at[1])
    for place, taps in zip(places, (fq_ref, fk_ref, fv_ref)):
        fetch(taps, filter_ref.at[:, place])
    fetch(decay_ref, pair_ref.at[0])
    fetch(bias_ref, pair_ref.at[1])
    ready = len(copies)
    for place, weight in zip(places, (wq_ref, wk_ref, wv_ref)):
        fetch(weight.at[:, 1 - core], rest_ref.at[:, :, place])
    for copy in copies[:ready]:
        copy.wait()
    total = jnp.zeros((DH, 4 * DH), F32)
    for part in range(x_ref.shape[0]):
        total = total + dot(x_ref[part], held_ref[part])
    total_ref[...] = total
    gates_ref[...] = narrow_sums(x_ref, narrow_ref, core)
    taps_ref[0:CONV] = filter_ref[...].astype(F32)
    taps_ref[CONV:] = jnp.zeros((8 - CONV, 4 * DH), F32)
    decay = pair_ref[0]
    bias = pair_ref[1]
    scales_ref[0] = lanes_of([0.0, 0.0, -jnp.exp(decay[:, 0:1]), -jnp.exp(decay[:, 1:2])])
    scales_ref[1] = lanes_of([0.0, 0.0, bias[:, 0:1], bias[:, 1:2]])
    for copy in copies[ready:]:
        copy.wait()


def second_project_kernel(
    x_ref, total_ref, part_ref, rest_ref, narrow_ref, proj_ref, ba_ref, tail_ref
):
    total = total_ref[...]
    for part in range(x_ref.shape[0]):
        total = total + dot(x_ref[part], rest_ref[part])
    proj_ref[...] = bf(total)
    tail_ref[...] = bf(total[DH - 16 :])
    ba_ref[...] = bf(part_ref[...] + narrow_sums(x_ref, narrow_ref, 1 - core_place()))


def gate_kernel(ba_ref, scales_ref, cols_ref, gap_ref):
    row, col = positions()
    raw = ba_ref[...].astype(F32)
    log_decay = scales_ref[0] * softplus(raw + scales_ref[1])
    lower = jnp.where(row >= col, 1.0, 0.0).astype(F32)
    cols = jnp.where(col < 2, sigmoid(raw), dot_exact(lower, log_decay))
    cols_ref[...] = cols
    rows = cols.T
    for head in range(2):
        between = cols[:, 2 + head : 3 + head] - rows[2 + head : 3 + head, :]
        gap_ref[head] = jnp.where(row >= col, jnp.exp(jnp.where(row >= col, between, 0.0)), 0.0)


def slab_kernel(
    proj_ref, tail_ref, taps_ref, cols_ref, gap_ref, grad_ref,
    send_ref, pre_ref, unit_ref, inverse_ref, mixed_ref, weighted_ref,
    back_ref, gram_ref, cross_ref, pad_ref,
):
    row, col = positions()
    pad_ref[0:8] = tail_ref[8:16].astype(F32)
    pad_ref[8 : 8 + DH] = proj_ref[...].astype(F32)
    pre = jnp.zeros((DH, 4 * DH), F32)
    for tap in range(CONV):
        start = 8 - (CONV - 1) + tap
        pre = pre + taps_ref[tap : tap + 1] * pad_ref[start : start + DH]
    pre_ref[...] = pre
    act = pre * sigmoid(pre)
    query_act, key_act = act[:, :DH], act[:, DH : 2 * DH]
    query = query_act * (lax.rsqrt(jnp.sum(query_act * query_act, 1, keepdims=True) + EPS) * SCALE)
    key = key_act * lax.rsqrt(jnp.sum(key_act * key_act, 1, keepdims=True) + EPS)
    unit_ref[0] = query
    unit_ref[1] = key
    cols = cols_ref[...]
    gram = dot3(key, key, (1, 1))
    cross = dot(query, key, (1, 1))
    gram_ref[...] = gram
    cross_ref[...] = cross
    betas = [cols[:, head : head + 1] for head in range(2)]
    inverses = unit_lower_inverses(
        [
            jnp.where(row > col, beta * gram * gap_ref[head], 0.0)
            for head, beta in enumerate(betas)
        ]
    )
    for head in range(2):
        beta = betas[head]
        inverse = inverses[head]
        cum = cols[:, 2 + head : 3 + head]
        value = act[:, (2 + head) * DH : (3 + head) * DH]
        grad = grad_ref[:, head * DH : (head + 1) * DH]
        gamma = jnp.exp(cum)
        last = cum[DH - 1 : DH, :]
        key_tail = jnp.exp(last - cum) * key
        both = dot(inverse, jnp.concatenate([beta * value, (beta * gamma) * key], axis=1))
        mixed = both[:, :DH]
        weighted = both[:, DH:]
        back = dot(cross * gap_ref[head], grad, (0, 0))
        inverse_ref[head] = bf(inverse)
        mixed_ref[head] = mixed
        weighted_ref[head] = bf(weighted)
        back_ref[head] = back
        ahead = dot(key_tail, both, (0, 0))
        lost = jnp.where(row == col, 1.0 - jnp.exp(last), 0.0) + ahead[:, DH:]
        send_ref[2 * head, 0:DH] = bf(lost)
        send_ref[2 * head, DH:] = bf(ahead[:, :DH])
        send_ref[2 * head + 1, 0:DH] = bf(lost.T)
        send_ref[2 * head + 1, DH:] = bf(
            dot(gamma * query, grad, (0, 0)) - dot(weighted, back, (0, 0))
        )


def unpack(ref):
    return ref[0:DH], ref[DH:].astype(F32)


def apply_map(later, state):
    matrix, offset = later
    return state - dot(matrix, state) + offset


def compose(later, earlier):
    matrix, offset = later
    before = earlier[0].astype(F32)
    return (
        before + matrix.astype(F32) - dot(matrix, before),
        apply_map(later, earlier[1]),
    )


def pack(total):
    return jnp.concatenate([bf(total[0]), bf(total[1])], axis=0)


def is_backward():
    return lax.axis_index("ctx") % 2 == 1


def in_order(step, backward):
    return jnp.where(backward, RADIX - 1 - step, step)


def group_kernel(got_ref, total_ref):
    backward = is_backward()
    total = unpack(got_ref.at[in_order(0, backward)])
    for step in range(1, RADIX):
        total = compose(unpack(got_ref.at[in_order(step, backward)]), total)
    total_ref[...] = pack(total)


def window_kernel(total_ref, last_ref, middle_ref, first_ref, wider_ref, before_ref):
    before = compose(unpack(last_ref), compose(unpack(middle_ref), unpack(first_ref)))
    before_ref[0:DH] = before[0]
    before_ref[DH:] = before[1]
    wider_ref[...] = pack(compose(unpack(total_ref), before))


def rows_kernel(wider_ref, before_ref, got_ref, offset_ref, past_ref):
    got = unpack(got_ref)
    offset_ref[...] = bf(apply_map(unpack(wider_ref), got[1]))
    past = compose((before_ref[0:DH], before_ref[DH:]), got)
    past_ref[0:DH] = past[0]
    past_ref[DH:] = past[1]


def states_kernel(got_ref, past_ref, group_ref, out_ref):
    backward = is_backward()
    state = apply_map((past_ref[0:DH], past_ref[DH:]), got_ref[...].astype(F32))
    for step in range(RADIX):
        spot = in_order(step, backward)
        out_ref[spot] = bf(state)
        if step < RADIX - 1:
            state = apply_map(unpack(group_ref.at[spot]), state)


def gradient_kernel(
    states_ref, pre_ref, unit_ref, cols_ref, ba_ref, inverse_ref, mixed_ref, weighted_ref,
    back_ref, gap_ref, gram_ref, cross_ref, grad_ref, taps_ref, scales_ref,
    full_ref, gates_ref, halo_ref, pad_ref,
):
    row, col = positions()
    cols = cols_ref[...]
    gram = gram_ref[...]
    cross = cross_ref[...]
    query = unit_ref[0]
    key = unit_ref[1]
    pre = pre_ref[...]
    gate = sigmoid(pre)
    act = pre * gate
    slope = gate * (1.0 + pre * (1.0 - gate))
    grad_query = jnp.zeros((DH, DH), F32)
    grad_key = jnp.zeros((DH, DH), F32)
    pieces = []
    columns = jnp.zeros((DH, DH), F32)
    sides = []
    for head in range(2):
        state = states_ref[2 * head]
        after = states_ref[2 * head + 1]
        beta = cols[:, head : head + 1]
        cum = cols[:, 2 + head : 3 + head]
        gamma = jnp.exp(cum)
        last = cum[DH - 1 : DH, :]
        rest = jnp.exp(last - cum)
        value = act[:, (2 + head) * DH : (3 + head) * DH]
        grad = grad_ref[:, head * DH : (head + 1) * DH]
        gap = gap_ref[head]
        fresh = mixed_ref[head] - dot(weighted_ref[head], state)
        grad_fresh = back_ref[head] + dot(rest * key, after)
        solved = dot(inverse_ref[head], grad_fresh, (0, 0))
        grad_strict = jnp.where(row > col, -dot(solved, fresh, (1, 1)), 0.0) * gap
        grad_cross = dot(grad, fresh, (1, 1)) * gap
        grad_weighted = -dot(solved, state, (1, 1))
        grad_scaled = dot(grad, state, (1, 1))
        grad_tail = dot(fresh, after, (1, 1))
        grad_query = grad_query + gamma * grad_scaled + dot(grad_cross, key)
        grad_gram = beta * grad_strict
        grad_key = grad_key + (
            dot(grad_cross, query, (0, 0))
            + dot(grad_gram, key)
            + dot(grad_gram, key, (0, 0))
            + (beta * gamma) * grad_weighted
            + rest * grad_tail
        )
        pieces.append(beta * solved)
        by_beta = jnp.sum(grad_strict * gram, 1, keepdims=True)
        by_key = gamma * jnp.sum(grad_weighted * key, 1, keepdims=True)
        grad_beta = jnp.sum(solved * value, 1, keepdims=True) + by_key + by_beta
        by_gap = grad_gram * gram + grad_cross * cross
        by_tail = rest * jnp.sum(grad_tail * key, 1, keepdims=True)
        at_end = jnp.sum(by_tail, 0, keepdims=True) + jnp.exp(last) * jnp.sum(
            jnp.sum(state.astype(F32) * after.astype(F32), 1, keepdims=True), 0, keepdims=True
        )
        grad_cum = (
            jnp.sum(by_gap, 1, keepdims=True)
            + gamma * jnp.sum(grad_scaled * query, 1, keepdims=True)
            + beta * by_key
            - by_tail
            + jnp.where(row[:, 0:1] == DH - 1, at_end, 0.0)
        )
        columns = jnp.where(row == 2 + head, jnp.sum(by_gap, 0, keepdims=True), columns)
        sides.append((grad_beta, grad_cum))
    raw = ba_ref[...].astype(F32)
    rate = scales_ref[0]
    bias = scales_ref[1]
    sides = lanes_of([sides[0][0], sides[1][0], sides[0][1], sides[1][1]]) - columns.T
    upper = jnp.where(row <= col, 1.0, 0.0).astype(F32)
    grad_log = dot_exact(upper, sides)
    beta = cols
    gates_ref[...] = bf(
        jnp.where(
            col < 2,
            sides * beta * (1.0 - beta),
            jnp.where(col < 4, grad_log * rate * sigmoid(raw + bias), 0.0),
        )
    )
    key_act = act[:, DH : 2 * DH]
    query_act = act[:, :DH]
    query_size = lax.rsqrt(jnp.sum(query_act * query_act, 1, keepdims=True) + EPS)
    key_size = lax.rsqrt(jnp.sum(key_act * key_act, 1, keepdims=True) + EPS)
    query_dir = query_act * query_size
    grad_query = grad_query * SCALE
    grad_query = query_size * (
        grad_query - query_dir * jnp.sum(grad_query * query_dir, 1, keepdims=True)
    )
    grad_key = key_size * (grad_key - key * jnp.sum(grad_key * key, 1, keepdims=True))
    pad_ref[0:8] = jnp.zeros((8, 4 * DH), F32)
    pad_ref[8 + DH :] = jnp.zeros((8, 4 * DH), F32)
    for place, piece in enumerate([grad_query, grad_key] + pieces):
        span = slice(place * DH, (place + 1) * DH)
        pad_ref[8 : 8 + DH, span] = piece * slope[:, span]
    total = jnp.zeros((8 + DH, 4 * DH), F32)
    for tap in range(CONV):
        start = CONV - 1 - tap
        total = total + taps_ref[tap : tap + 1] * pad_ref[start : start + 8 + DH]
    halo_ref[...] = total[0:8]
    full_ref[...] = total[8:]


def spread_kernel(
    other, full_ref, halo_ref, gates_ref, wq_ref, wk_ref, wv_ref, wb_ref, wa_ref, out_ref
):
    core = core_place()
    core = 1 - core if other else core
    full = full_ref[...]
    end = full[DH - 8 :] + halo_ref[...]
    grads = bf(jnp.concatenate([full[: DH - 8], end], axis=0))
    gates = gates_ref[...]
    parts, _, width = out_ref.shape
    for part in range(parts):
        span = part_span(part, core, width)
        total = dot(grads[:, :DH], wq_ref[span, :], (1, 1))
        total = total + dot(grads[:, DH : 2 * DH], wk_ref[span, :], (1, 1))
        total = total + dot(grads[:, 2 * DH :], wv_ref[span, :], (1, 1))
        total = total + dot(gates[:, 0:2], wb_ref[:, span])
        total = total + dot(gates[:, 2:4], wa_ref[:, span])
        out_ref[part] = total.astype(out_ref.dtype)


def merge_kernel(kept_ref, got_ref, out_ref):
    out_ref[...] = bf(kept_ref[...] + got_ref[...].astype(F32))


def total_kernel(shares_ref, out_ref):
    total = shares_ref[0].astype(F32)
    for part in range(1, shares_ref.shape[0]):
        total = total + shares_ref[part].astype(F32)
    out_ref[...] = bf(total)


def call(kernel, outs, scratch=(), specs=None):
    extra = {} if specs is None else {"in_specs": specs}
    return pl.pallas_call(
        kernel,
        out_shape=[jax.ShapeDtypeStruct(shape, kind) for shape, kind in outs],
        scratch_shapes=list(scratch),
        compiler_params=pltpu.CompilerParams(vmem_limit_bytes=48 * 1024 * 1024),
        **extra,
    )


def stay(array):
    return pltpu.with_memory_space_constraint(array, pltpu.HBM)


def first_project(mine, weights, filters, decay, bias):
    parts, rows, width = mine.shape
    inside = pl.BlockSpec(memory_space=pltpu.VMEM)
    outside = pl.BlockSpec(memory_space=pltpu.HBM)
    model = 2 * parts * width
    wide = [weight.reshape(parts, 2, width, weight.shape[1]) for weight in weights[:3]]
    return call(
        first_project_kernel,
        [
            ((rows, 4 * DH), F32), ((DH, DH), F32), ((8, 4 * DH), F32), ((2, DH, DH), F32),
            ((parts, width, 4 * DH), BF16), ((2, 2, model), BF16),
        ],
        [
            pltpu.VMEM((parts, width, 4 * DH), BF16),
            pltpu.VMEM((CONV, 4 * DH), BF16),
            pltpu.VMEM((2, 1, 2), F32),
            pltpu.SemaphoreType.DMA((13,)),
        ],
        [inside] + [outside] * 10,
    )(mine, *[stay(array) for array in (*wide, *weights[3:], *filters, decay, bias)])


def second_project(other, total, part, rest, narrow):
    return call(
        second_project_kernel,
        [((DH, 4 * DH), BF16), ((DH, DH), BF16), ((16, 4 * DH), BF16)],
    )(other, total, part, rest, narrow)


def slab(proj, tail, taps, cols, gap, grad):
    square = (DH, DH)
    return call(
        slab_kernel,
        [
            ((4, PACK, DH), BF16), ((DH, 4 * DH), F32), ((2,) + square, F32),
            ((2,) + square, BF16), ((2,) + square, F32), ((2,) + square, BF16),
            ((2,) + square, F32), (square, F32), (square, F32),
        ],
        [pltpu.VMEM((8 + DH, 4 * DH), F32)],
    )(proj, tail, taps, cols, gap, grad)


def gradient(states, kept, cols, gap, gates, taps, scales, grad):
    pre, unit, inverse, mixed, weighted, back, gram, cross = kept
    return call(
        gradient_kernel,
        [((DH, 4 * DH), F32), ((DH, DH), BF16), ((8, 4 * DH), F32)],
        [pltpu.VMEM((16 + DH, 4 * DH), F32)],
    )(
        states, pre, unit, cols, gates, inverse, mixed, weighted, back, gap, gram, cross,
        grad, taps, scales,
    )


def spread(full, halo, gates, weights, parts, other):
    width = weights[0].shape[0] // (2 * parts)
    return call(
        functools.partial(spread_kernel, other),
        [((parts, DH, width), BF16 if other else F32)],
    )(full, halo, gates, *weights)[0]


def local(
    inputs, query_weight, key_weight, value_weight, beta_weight, alpha_weight,
    query_filter, key_filter, value_filter, decay_log, step_bias, grad_core,
):
    weights = (query_weight, key_weight, value_weight, beta_weight.T, alpha_weight.T)
    filters = (query_filter, key_filter, value_filter)
    decay = decay_log.reshape(1, 2)
    bias = step_bias.reshape(1, 2)
    count = lax.axis_size("ctx")
    parts = lax.axis_size("tp")
    slabs = range(count)
    group = [[s for s in slabs if s // RADIX == g] for g in range(count // RADIX)]

    def exchange(value, groups):
        return lax.all_to_all(value, "ctx", 0, 0, axis_index_groups=groups)

    def onward(value, distance):
        steps = [(s, s - distance if s % 2 else s + distance) for s in slabs]
        return lax.ppermute(value, "ctx", [(s, t) for s, t in steps if 0 <= t < count])

    chips = [[2 * chip + core for chip in range(parts // 2)] for core in range(2)]

    def across(value):
        return lax.all_to_all(value, "tp", 0, 0, axis_index_groups=chips)

    def between(value):
        return lax.ppermute(value, "tp", [(t, t ^ 1) for t in range(parts)])

    mine = across(jnp.broadcast_to(inputs[None], (parts // 2,) + inputs.shape))
    other = between(mine)
    total, part, taps, scales, rest, narrow = first_project(mine, weights, filters, decay, bias)
    proj, gates, tail = second_project(other, total, part, rest, narrow)
    tail = lax.ppermute(tail, "ctx", [(s, s + 1) for s in range(count - 1)])
    square = (DH, DH)
    cols, gap = call(gate_kernel, [(square, F32), ((2,) + square, F32)])(gates, scales)
    send, *kept = slab(proj, tail, taps, cols, gap, grad_core)
    got = exchange(send, group)
    total = call(group_kernel, [((PACK, DH), BF16)])(got)[0]
    last = onward(total, RADIX)
    earlier = [last, onward(last, RADIX), onward(total, 3 * RADIX)]
    packed = (PACK, DH)
    wider, before = call(window_kernel, [(packed, BF16), (packed, F32)])(total, *earlier)
    across_rows = RADIX * RADIX
    offset, past = call(rows_kernel, [((DH, DH), BF16), (packed, F32)])(
        wider, before, onward(wider, across_rows)
    )
    states = call(states_kernel, [((RADIX, DH, DH), BF16)])(
        onward(offset, 2 * across_rows), past, got
    )[0]
    states = exchange(states, group)
    full, grad_gates, halo = gradient(
        states, kept, cols, gap, gates, taps, scales, grad_core
    )
    halo = lax.ppermute(halo, "ctx", [(s + 1, s) for s in range(count - 1)])
    given = between(spread(full, halo, grad_gates, weights, parts // 2, True))
    kept = spread(full, halo, grad_gates, weights, parts // 2, False)
    shares = call(merge_kernel, [(given.shape, BF16)])(kept, given)[0]
    return call(total_kernel, [(shares.shape[1:], BF16)])(across(shares))[0]


def solution(mesh):
    sharded = P("ctx", "tp")
    kept = P(None, "tp")
    return jax.shard_map(
        local,
        mesh=mesh,
        in_specs=(sharded,) + (kept,) * 8 + (P("tp"), P("tp"), sharded),
        out_specs=sharded,
        check_vma=False,
    )
```
